32 devices in a mesh: gx: 8 (over z, x), yz: 4 (over y, core).
Axes of the slice: x: 2, y: 2, z: 4, core: 2. Of those that a mesh axis runs over, the one named last changes fastest.
Arguments:
- pops_start: float32 [64, 19, 16, 512], P(('gx', 'yz'))
- tile_pos: int32 [64], replicated, may hold values from -1 to 7, as said below
- wall_mask: int32 [64, 16, 512], P(('gx', 'yz')), may hold values 0 or 1
- wall_frac: float32 [64, 16, 512], P(('gx', 'yz')), may hold values from 0.2 to 0.9
- patch_id: int32 [64, 16, 512], P(('gx', 'yz')), may hold values from 0 to 2047
- probe: float32 [64, 16, 512], P(('gx', 'yz')), may hold values from -4 to 4
Outputs:
- pops_final: float32 [64, 19, 16, 512], P(('gx', 'yz'))
- adjoint_start: float32 [64, 19, 16, 512], P(('gx', 'yz'))
- patch_sens: float32 [2048], P(('gx', 'yz'))
The draws below stay inside these ranges and needn't reach their ends.
Inputs may be any that keep to these rules, and one draw needn't show every extreme that they name: Slots with tile_pos -1 are empty. Each device's live slots come first; every device holds 1 to 2 tiles and some device holds 2. Within one gx index no position appears twice.
All inputs are finite; a program needn't handle non-finite values. No bound on the sum of `wall_mask` on one device may be relied on, other than what follows from the above.
Results may differ from the reference program's by a relative error of at most 0.0003.
Values sent between devices are 32-bit elements; how exact they have to be, the bound alone decides.
No kernel may reach another device: no remote copies, remote signals or barrier semaphores. Data moves between devices by JAX's collectives and lax.ppermute only.
A program may use at most 256 MiB of HBM per device.

```python
import jax
import jax.numpy as jnp
import numpy as np
from jax import lax

TL = 16
TA = 16
TB = 32
SLOTS = 2
STEPS = 2
TILES = 64
PATCHES = 2048
N_GX = 8
N_YZ = 4


WEIGHTS = [1.0 / 3.0] + [1.0 / 18.0] * 6 + [1.0 / 36.0] * 12


def draw_pops_start(key, part):
    shape = (TILES, 19, TL, TA * TB)
    first, second = jax.random.split(key)
    noise = jax.random.uniform(first, shape, jnp.float32, -1.0, 1.0)
    weight = jnp.asarray(WEIGHTS, jnp.float32)[None, :, None, None]
    return (weight * (1.0 + 0.3 * noise)).astype(jnp.float32)


def draw_tile_pos(key, part):
    first, second, third = jax.random.split(key, 3)
    counts = jax.random.randint(first, (N_GX * N_YZ,), 1, SLOTS + 1)
    fullest = jax.random.randint(second, (), 0, N_GX * N_YZ)
    counts = jnp.where(jnp.arange(N_GX * N_YZ) == fullest, SLOTS, counts).reshape(N_GX, N_YZ)
    starts = jnp.cumsum(counts, axis=1) - counts
    orders = jax.vmap(lambda sub: jax.random.permutation(sub, N_YZ * SLOTS))(jax.random.split(third, N_GX))
    slot = jnp.arange(SLOTS)
    index = jnp.clip(starts[:, :, None] + slot[None, None, :], 0, N_YZ * SLOTS - 1).reshape(N_GX, -1)
    picked = jnp.take_along_axis(orders, index, axis=1).reshape(N_GX, N_YZ, SLOTS)
    alive = slot[None, None, :] < counts[:, :, None]
    return jnp.where(alive, picked, -1).reshape(-1).astype(jnp.int32)


def touch_ends(drawn, stream_key, smallest, largest):
    longest = drawn.shape.index(max(drawn.shape))
    spots = []
    for shift in (0, 1):
        where = [jax.random.randint(jax.random.fold_in(stream_key, axis), (), 0, length) for axis, length in enumerate(drawn.shape)]
        where[longest] = (where[longest] + shift) % drawn.shape[longest]
        spots.append(tuple(where))
    return drawn.at[spots[0]].set(smallest).at[spots[1]].set(largest)


def shard_levels(stream_key, shape, cuts, least, top_value):
    def one(position, blocks):
        steps = jax.random.uniform(jax.random.fold_in(jax.random.fold_in(stream_key, 6), position), (blocks,), jnp.float32, least / len(cuts), top_value / len(cuts))
        return jnp.repeat(jnp.exp(steps), shape[position] // blocks).reshape((-1,) + (1,) * (len(shape) - position - 1))

    factor_of = one(*cuts[0])
    for cut in cuts[1:]:
        factor_of = factor_of * one(*cut)
    return factor_of


def gaussian(rng, dims, spread, reach, cuts=(), kind=jnp.bfloat16):
    values = spread * jax.random.normal(rng, dims, jnp.float32)
    if cuts:
        values = values * shard_levels(rng, dims, cuts, -0.22, 0.18)
    return jnp.clip(values, -reach, reach).astype(kind)


def setup_inputs(seed: int = 0) -> dict:
    streams_of = jax.random.split(jax.random.key(seed), 7)
    pops_start = draw_pops_start(jax.random.fold_in(streams_of[6], 71), 0)
    tile_pos = draw_tile_pos(jax.random.fold_in(streams_of[6], 71), 0)
    wall_mask = touch_ends((jax.random.randint(streams_of[2], (TILES, TL, TA * TB), 0, 4) < 1).astype(jnp.int32), jax.random.fold_in(streams_of[2], 1), 0, 1)
    wall_frac = jnp.clip(0.2 + 0.7 * jax.random.uniform(streams_of[3], (TILES, TL, TA * TB), jnp.float32) ** shard_levels(streams_of[3], (TILES, TL, TA * TB), ((0, 32),), -0.2, 0.2), 0.2, 0.9)
    patch_id = touch_ends(jax.random.randint(streams_of[4], (TILES, TL, TA * TB), 0, PATCHES), jax.random.fold_in(streams_of[4], 1), 0, PATCHES - 1).astype(jnp.int32)
    probe = gaussian(streams_of[5], (TILES, TL, TA * TB), 1.0, 4.0, ((0, 32),), jnp.float32)
    return {"pops_start": pops_start, "tile_pos": tile_pos, "wall_mask": wall_mask, "wall_frac": wall_frac, "patch_id": patch_id, "probe": probe}


VELOCITY = np.array([[0, 0, 0], [1, 0, 0], [-1, 0, 0], [0, 1, 0], [0, -1, 0], [0, 0, 1], [0, 0, -1], [1, 1, 0], [-1, -1, 0], [1, -1, 0], [-1, 1, 0], [1, 0, 1], [-1, 0, -1], [1, 0, -1], [-1, 0, 1], [0, 1, 1], [0, -1, -1], [0, 1, -1], [0, -1, 1]])
WEIGHTS = [1.0 / 3.0] + [1.0 / 18.0] * 6 + [1.0 / 36.0] * 12
REVERSE = [0, 2, 1, 4, 3, 6, 5, 8, 7, 10, 9, 12, 11, 14, 13, 16, 15, 18, 17]
OMEGA = 1.25

def collide(field, solid):
    shape = (19,) + (1,) * (field.ndim - 1)
    vel_l = jnp.asarray(VELOCITY[:, 0], jnp.float32).reshape(shape)
    vel_a = jnp.asarray(VELOCITY[:, 1], jnp.float32).reshape(shape)
    vel_b = jnp.asarray(VELOCITY[:, 2], jnp.float32).reshape(shape)
    weight = jnp.asarray(WEIGHTS, jnp.float32).reshape(shape)
    density = lax.optimization_barrier(jnp.sum(field, axis=0))
    speed_l = lax.optimization_barrier(jnp.sum(field * vel_l, axis=0)) / density
    speed_a = lax.optimization_barrier(jnp.sum(field * vel_a, axis=0)) / density
    speed_b = lax.optimization_barrier(jnp.sum(field * vel_b, axis=0)) / density
    square = speed_l * speed_l + speed_a * speed_a + speed_b * speed_b
    along = vel_l * speed_l + vel_a * speed_a + vel_b * speed_b
    equil = weight * density * (1.0 + 3.0 * along + 4.5 * along * along - 1.5 * square)
    relaxed = field - OMEGA * (field - equil)
    reverse = jnp.concatenate([field[i:i + 1] for i in REVERSE], axis=0)
    return (1.0 - solid) * relaxed + solid * reverse

def reference(pops_start, tile_pos, wall_mask, wall_frac, patch_id, probe):
    group = N_YZ * SLOTS
    grouped = tile_pos.reshape(N_GX, group)
    match = grouped[:, None, :] == jnp.arange(group, dtype=jnp.int32)[None, :, None]
    source = lax.optimization_barrier(jnp.sum(jnp.where(match, jnp.arange(group, dtype=jnp.int32)[None, None, :], 0), axis=2))
    present = jnp.any(match, axis=2)
    flat_index = (jnp.arange(N_GX, dtype=jnp.int32)[:, None] * group + source).reshape(-1).astype(jnp.int32)

    def embed(tiles, fill):
        chans = tiles.shape[1]
        picked = jnp.take(tiles, flat_index, axis=0).reshape(N_GX, group, chans, TL, TA * TB)
        picked = jnp.where(present[:, :, None, None, None], picked, fill)
        picked = picked.reshape(N_GX, N_YZ, SLOTS, chans, TL, TA, TB)
        return picked.transpose(3, 0, 4, 1, 5, 2, 6).reshape(chans, N_GX * TL, N_YZ * TA, SLOTS * TB)

    def extract(dense):
        chans = dense.shape[0]
        cube = dense.reshape(chans, N_GX, TL, N_YZ, TA, SLOTS, TB).transpose(1, 3, 5, 0, 2, 4, 6)
        cube = cube.reshape(N_GX, group, chans, TL, TA * TB)
        slot_pos = jnp.clip(grouped, 0, group - 1).astype(jnp.int32)
        picked = jax.vmap(lambda layer_cube, layer_pos: jnp.take(layer_cube, layer_pos, axis=0))(cube, slot_pos)
        picked = jnp.where((grouped >= 0)[:, :, None, None, None], picked, 0.0)
        return picked.reshape(N_GX * group, chans, TL, TA * TB)
    weight_col = jnp.asarray(WEIGHTS, jnp.float32)
    zero_fill = jnp.zeros((1, 1, 1), jnp.float32)
    live = embed(jnp.ones((TILES, 1, TL, TA * TB), jnp.float32), zero_fill)[0] > 0.5
    mask_float = wall_mask.astype(jnp.float32)
    solid = embed((mask_float * wall_frac)[:, None], zero_fill)[0]
    seed_field = embed(probe[:, None], zero_fill)[0]
    start = embed(pops_start, weight_col[:, None, None])
    size_l, size_a, size_b = (N_GX * TL, N_YZ * TA, SLOTS * TB)

    def step(field, solid_part):
        post = collide(field, solid_part)
        parts = []
        for i in range(19):
            padded = jnp.pad(post[i], 1, constant_values=WEIGHTS[i])
            cl, ca, cb = (int(VELOCITY[i, 0]), int(VELOCITY[i, 1]), int(VELOCITY[i, 2]))
            parts.append(padded[1 - cl:1 - cl + size_l, 1 - ca:1 - ca + size_a, 1 - cb:1 - cb + size_b])
        read = jnp.stack(parts, axis=0)
        return jnp.where(live[None], read, weight_col[:, None, None, None])
    states = [start]
    for k in range(STEPS):
        states.append(step(states[-1], solid))
    vel_l = jnp.asarray(VELOCITY[:, 0], jnp.float32)
    adjoint = seed_field[None] * vel_l[:, None, None, None]
    sens = jnp.zeros_like(solid)
    for k in reversed(range(STEPS)):
        _, backward = jax.vjp(step, states[k], solid)
        adjoint, dsolid = backward(adjoint)
        sens = sens + dsolid
    pops_final = extract(states[-1])
    adjoint_start = extract(adjoint)
    sens_tiles = extract(sens[None])[:, 0]
    patch_sens = jax.ops.segment_sum((mask_float * sens_tiles).reshape(-1), patch_id.reshape(-1), num_segments=PATCHES)
    return (pops_final, adjoint_start, patch_sens)
```

```python
import functools

import jax
import jax.numpy as jnp
import numpy as np
from jax import lax
from jax.experimental import pallas as pl
from jax.experimental.pallas import tpu as pltpu
from jax.sharding import PartitionSpec as P

TL = 16
TA = 16
TB = 32
CELLS = TA * TB
LANES = 128
COLS = CELLS // LANES
OMEGA = 1.25

VELOCITY = np.array(
    [
        [0, 0, 0],
        [1, 0, 0],
        [-1, 0, 0],
        [0, 1, 0],
        [0, -1, 0],
        [0, 0, 1],
        [0, 0, -1],
        [1, 1, 0],
        [-1, -1, 0],
        [1, -1, 0],
        [-1, 1, 0],
        [1, 0, 1],
        [-1, 0, -1],
        [1, 0, -1],
        [-1, 0, 1],
        [0, 1, 1],
        [0, -1, -1],
        [0, 1, -1],
        [0, -1, 1],
    ]
)
Q = 19
WEIGHTS = [1.0 / 3.0] + [1.0 / 18.0] * 6 + [1.0 / 36.0] * 12
PAIRS = [(2 * k + 1, 2 * k + 2) for k in range(9)]
AXIAL = [i for i in range(Q) if VELOCITY[i, 0] != 0]


def vel(i):
    return tuple(int(v) for v in VELOCITY[i])


def members_of(dim, value):
    return [i for i in range(Q) if vel(i)[dim] == value]


def face_list(stage, dim, side):
    if stage == 1:
        return [("post", i) for i in members_of(dim, side)] + [("probe", 0)]
    return [("post", i) for i in members_of(dim, side)] + [
        ("adj", i) for i in members_of(dim, -side)
    ]


class Pack:
    def __init__(self, stage):
        self.n = len(face_list(stage, 0, 1))
        self.lists = {
            (d, s): face_list(stage, d, s) for d in range(3) for s in (-1, 1)
        }
        self.fold = 2 if 2 * self.n <= TB // 2 else 1
        self.a_cols = -(-2 * self.n * TB // LANES)
        self.b_cols = COLS // self.fold
        self.a_row = 0
        self.b_row = TL * self.a_cols
        self.ab_rows = self.b_row + TL * self.b_cols
        self.l_rows = self.n * COLS
        self.up_row = self.ab_rows
        self.dn_row = self.up_row + self.l_rows
        self.rows = self.dn_row + self.l_rows

    def slot(self, dim, side, key):
        j = self.lists[(dim, side)].index(key)
        return j if dim == 0 or side < 0 else j + self.n


PACK1 = Pack(1)
PACK2 = Pack(2)


def lane_roll(x, shift):
    shift = shift % x.shape[-1]
    return x if shift == 0 else pltpu.roll(x, shift, axis=x.ndim - 1)


def row_roll(x, shift):
    shift = shift % x.shape[0]
    return x if shift == 0 else pltpu.roll(x, shift, axis=0)


def lane_iota(shape):
    return lax.broadcasted_iota(jnp.int32, shape, len(shape) - 1)


def row_iota(shape):
    return lax.broadcasted_iota(jnp.int32, shape, 0)


def combine(c, parts):
    total = None
    for v, p in zip(c, parts):
        if v == 0:
            continue
        if total is None:
            total = p if v > 0 else -p
        else:
            total = total + p if v > 0 else total - p
    return total


def flow(f):
    rho = f[0]
    momentum = [None, None, None]
    for i, j in PAIRS:
        rho = rho + (f[i] + f[j])
        diff = f[i] - f[j]
        for d, v in enumerate(vel(i)):
            if v == 0:
                continue
            if momentum[d] is None:
                momentum[d] = diff if v > 0 else -diff
            else:
                momentum[d] = momentum[d] + diff if v > 0 else momentum[d] - diff
    inv = 1.0 / rho
    u = [m * inv for m in momentum]
    square = u[0] * u[0] + u[1] * u[1] + u[2] * u[2]
    return rho, u, 1.0 - 1.5 * square


def collide(f, solid, rho, u, base):
    fluid = 1.0 - solid
    keep = (1.0 - OMEGA) * fluid
    scale = OMEGA * fluid * rho
    out = [None] * Q
    out[0] = (keep + solid) * f[0] + WEIGHTS[0] * scale * base
    for i, j in PAIRS:
        along = combine(vel(i), u)
        ws = WEIGHTS[i] * scale
        even = ws * (base + 4.5 * along * along)
        odd = ws * (3.0 * along)
        out[i] = keep * f[i] + solid * f[j] + (even + odd)
        out[j] = keep * f[j] + solid * f[i] + (even - odd)
    return out


def pullback(f, solid, rho, u, base, g):
    fluid = 1.0 - solid
    keep = (1.0 - OMEGA) * fluid
    gain = OMEGA * fluid
    lin = [None, None, None]
    total = None
    dens = None
    cross = None

    def plus(a, b):
        return b if a is None else a + b

    if g[0] is not None:
        e = WEIGHTS[0] * g[0]
        total = e
        dens = e * base
        cross = OMEGA * (g[0] * f[0])
    for i, j in PAIRS:
        if g[i] is None:
            continue
        along = combine(vel(i), u)
        w = WEIGHTS[i]
        even = w * (g[i] + g[j])
        odd = w * (g[i] - g[j])
        total = plus(total, even)
        dens = plus(dens, even * (base + 4.5 * along * along) + 3.0 * along * odd)
        push = 3.0 * odd + 9.0 * along * even
        for d, v in enumerate(vel(i)):
            if v:
                lin[d] = plus(lin[d], push if v > 0 else -push)
        cross = plus(
            cross,
            g[i] * (f[j] - (1.0 - OMEGA) * f[i]) + g[j] * (f[i] - (1.0 - OMEGA) * f[j]),
        )
    lin = [
        (-3.0 * u[d] * total if lin[d] is None else lin[d] - 3.0 * u[d] * total)
        for d in range(3)
    ]
    dsolid = cross - OMEGA * rho * dens
    shared = gain * (dens - (lin[0] * u[0] + lin[1] * u[1] + lin[2] * u[2]))
    lin = [gain * v for v in lin]
    out = [None] * Q
    out[0] = shared if g[0] is None else (keep + solid) * g[0] + shared
    for i, j in PAIRS:
        slope = combine(vel(i), lin)
        if g[i] is None:
            out[i] = shared + slope
            out[j] = shared - slope
        else:
            out[i] = keep * g[i] + solid * g[j] + (shared + slope)
            out[j] = keep * g[j] + solid * g[i] + (shared - slope)
    return out, dsolid


def load_chunk(ref, t, i, r, c):
    return ref[t, i, pl.ds(8 * r, 8), pl.ds(c, LANES)]


def for_chunks(count, run):
    def step(k, carry):
        t = k // (2 * COLS)
        r = (k // COLS) % 2
        c = pl.multiple_of((k % COLS) * LANES, LANES)
        run(t, pl.multiple_of(r * 8, 8), c)
        return carry

    lax.fori_loop(0, count * 2 * COLS, step, 0)


def chunk(ref, t, i, r, c):
    return ref[t, i, pl.ds(r, 8), pl.ds(c, LANES)]


def plane_chunk(ref, t, r, c):
    return ref[t, pl.ds(r, 8), pl.ds(c, LANES)]


def write_faces(pack, t, get, ab_ref, up_ref, dn_ref):
    lane = lane_iota((TL, LANES))
    for col in range(pack.a_cols):
        acc = jnp.zeros((TL, LANES), jnp.float32)
        for side in (-1, 1):
            for key in pack.lists[(1, side)]:
                j = pack.slot(1, side, key)
                if j // 4 != col:
                    continue
                to = TB * (j % 4)
                if side < 0:
                    part = lane_roll(get(key, slice(None), slice(0, LANES)), to)
                else:
                    part = lane_roll(
                        get(key, slice(None), slice(CELLS - LANES, CELLS)),
                        to - (LANES - TB),
                    )
                acc = jnp.where(lane // TB == j % 4, part, acc)
        ab_ref[t, pack.a_row + TL * col : pack.a_row + TL * (col + 1), :] = acc
    for col in range(pack.b_cols):
        acc = jnp.zeros((TL, LANES), jnp.float32)
        for half in range(pack.fold):
            src = col + half * pack.b_cols
            for side in (-1, 1):
                for key in pack.lists[(2, side)]:
                    j = pack.slot(2, side, key) + half * (TB // 2)
                    part = get(key, slice(None), slice(LANES * src, LANES * (src + 1)))
                    part = lane_roll(part, j if side < 0 else j - (TB - 1))
                    acc = jnp.where(lane % TB == j, part, acc)
        ab_ref[t, pack.b_row + TL * col : pack.b_row + TL * (col + 1), :] = acc
    for side, ref in ((1, up_ref), (-1, dn_ref)):
        row = TL - 1 if side > 0 else 0
        for key in pack.lists[(0, side)]:
            j = pack.slot(0, side, key)
            for col in range(COLS):
                ref[t, j * COLS + col : j * COLS + col + 1, :] = get(
                    key, slice(row, row + 1), slice(LANES * col, LANES * (col + 1))
                )


def build_inverse(pos_ref, inv_ref, n_layers, group):
    layer = lax.axis_index("gx")
    for off in (-1, 0, 1):
        for w in range(group + 1):
            inv_ref[off + 1, w] = -1
        target = layer + off
        valid = (target >= 0) & (target < n_layers)
        first = jnp.clip(target, 0, n_layers - 1) * group
        for s in range(group):
            p = pos_ref[first + s]
            inv_ref[off + 1, jnp.where(valid & (p >= 0), p, group)] = s


class Neighbours:
    def __init__(self, pack, t, faces_ref, pos_ref, inv_ref, n_cross, count):
        self.pack = pack
        self.ref = faces_ref
        group = n_cross * count
        own = pos_ref[lax.axis_index("gx") * group + lax.axis_index("yz") * count + t]
        p = jnp.maximum(own, 0)
        a, b = p // count, p % count
        self.alive = own >= 0
        self.where = {}
        for d in [vel(i) for i in range(1, Q)]:
            ta, tb = a + d[1], b + d[2]
            ok = (ta >= 0) & (ta < n_cross) & (tb >= 0) & (tb < count)
            s = inv_ref[d[0] + 1, jnp.where(ok, ta * count + tb, group)]
            found = ok & (s >= 0)
            self.where[d] = (jnp.where(found, s, 0), found)
        self.planes = {}

    def a_face(self, d, side, key, fill):
        k, found = self.where[d]
        j = self.pack.slot(1, side, key)
        row = self.pack.a_row + TL * (j // 4)
        face = self.ref[k, row : row + TL, :]
        face = lane_roll(face, (LANES - TB if side > 0 else 0) - TB * (j % 4))
        return jnp.where(found, face, fill)

    def b_plane(self, d):
        if d not in self.planes:
            k, found = self.where[d]
            row = self.pack.b_row
            half = jnp.concatenate(
                [
                    self.ref[k, row + TL * c : row + TL * (c + 1), :]
                    for c in range(self.pack.b_cols)
                ],
                axis=1,
            )
            if self.pack.fold == 2:
                half = jnp.concatenate([half, lane_roll(half, -(TB // 2))], axis=1)
            self.planes[d] = half
        return self.planes[d], self.where[d][1]

    def l_row(self, d, side, key, fill):
        k, found = self.where[d]
        first = self.pack.up_row if side > 0 else self.pack.dn_row
        first = first + self.pack.slot(0, side, key) * COLS
        row = jnp.concatenate(
            [self.ref[k, first + c : first + c + 1, :] for c in range(COLS)], axis=1
        )
        return jnp.where(found, row, fill)

    def stream(self, own, c, key, fill):
        cl, ca, cb = c
        shape = (TL, CELLS)
        lane = lane_iota(shape)
        edge_b = lane % TB == (TB - 1 if cb > 0 else 0)
        edge_a = lane // TB == (TA - 1 if ca > 0 else 0)
        x = own
        if ca:
            face = self.a_face((0, -ca, 0), ca, key, fill)
            part = slice(CELLS - LANES, CELLS) if ca > 0 else slice(0, LANES)
            inner = lane_iota((TL, LANES))
            hit = inner >= LANES - TB if ca > 0 else inner < TB
            face = jnp.where(hit, face, x[:, part])
            x = jnp.concatenate(
                [x[:, : CELLS - LANES], face] if ca > 0 else [face, x[:, LANES:]], axis=1
            )
        if cb:
            j = self.pack.slot(2, cb, key)
            shift = -1 - j if cb > 0 else TB - j
            plane, found = self.b_plane((0, 0, -cb))
            face = jnp.where(found, lane_roll(plane, shift), fill)
            if ca:
                plane, found = self.b_plane((0, -ca, -cb))
                corner = jnp.where(found, lane_roll(plane, shift), fill)
                at = (TA - 1 if ca > 0 else 0) + (-1 if cb > 0 else 1)
                face = jnp.where(lane // TB == at % TA, corner, face)
            x = jnp.where(edge_b, face, x)
        if cl:
            row = self.l_row((-cl, 0, 0), cl, key, fill)
            lane_r = lane_iota((1, CELLS))
            if ca:
                corner = self.l_row((-cl, -ca, 0), cl, key, fill)
                row = jnp.where(lane_r // TB == (TA - 1 if ca > 0 else 0), corner, row)
            if cb:
                corner = self.l_row((-cl, 0, -cb), cl, key, fill)
                corner = lane_roll(corner, -TB if cb > 0 else TB)
                row = jnp.where(lane_r % TB == (TB - 1 if cb > 0 else 0), corner, row)
            at = TL - 1 if cl > 0 else 0
            x = jnp.where(row_iota(shape) == at, jnp.broadcast_to(row, shape), x)
        return row_roll(lane_roll(x, TB * ca + cb), cl)


def first_kernel(pops, mask, frac, probe, post, ab, up, dn):
    count = pops.shape[0]

    def run(t, r, c):
        f = [chunk(pops, t, i, r, c) for i in range(Q)]
        solid = plane_chunk(mask, t, r, c).astype(jnp.float32) * plane_chunk(frac, t, r, c)
        out = collide(f, solid, *flow(f))
        for i in range(Q):
            post[t, i, pl.ds(r, 8), pl.ds(c, LANES)] = out[i]

    for_chunks(count, run)

    def faces(t, carry):
        def get(key, rows, lanes):
            if key[0] == "probe":
                return probe[t, rows, lanes]
            return post[t, key[1], rows, lanes]

        write_faces(PACK1, t, get, ab, up, dn)
        return carry

    lax.fori_loop(0, count, faces, 0)


def second_kernel(
    dims, pos, post0, mask, frac, probe, around, post1, adj1, dsolid, ab, up, dn, state, pulled, inv
):
    n_layers, n_cross = dims
    count = post0.shape[0]
    build_inverse(pos, inv, n_layers, n_cross * count)

    def move(t, carry):
        near = Neighbours(PACK1, t, around, pos, inv, n_cross, count)
        for i in range(Q):
            state[t, i] = near.stream(post0[t, i], vel(i), ("post", i), WEIGHTS[i])
        for n, i in enumerate(AXIAL):
            back = tuple(-v for v in vel(i))
            moved = near.stream(probe[t], back, ("probe", 0), 0.0)
            pulled[t, n] = moved if vel(i)[0] > 0 else -moved
        return carry

    lax.fori_loop(0, count, move, 0)

    def run(t, r, c):
        f = [chunk(state, t, i, r, c) for i in range(Q)]
        solid = plane_chunk(mask, t, r, c).astype(jnp.float32) * plane_chunk(frac, t, r, c)
        rho, u, base = flow(f)
        out = collide(f, solid, rho, u, base)
        for i in range(Q):
            post1[t, i, pl.ds(r, 8), pl.ds(c, LANES)] = out[i]
        g = [None] * Q
        for n, i in enumerate(AXIAL):
            g[i] = chunk(pulled, t, n, r, c)
        back, ds = pullback(f, solid, rho, u, base, g)
        for i in range(Q):
            adj1[t, i, pl.ds(r, 8), pl.ds(c, LANES)] = back[i]
        dsolid[t, pl.ds(r, 8), pl.ds(c, LANES)] = ds

    for_chunks(count, run)

    def faces(t, carry):
        def get(key, rows, lanes):
            return (post1 if key[0] == "post" else adj1)[t, key[1], rows, lanes]

        write_faces(PACK2, t, get, ab, up, dn)
        return carry

    lax.fori_loop(0, count, faces, 0)


def third_kernel(
    dims, pos, post1, adj1, pops, mask, frac, patch, dsolid, around, final, start, sums, pulled, weighted, inv
):
    n_layers, n_cross = dims
    count = pops.shape[0]
    group = n_cross * count
    build_inverse(pos, inv, n_layers, group)

    def move(t, carry):
        near = Neighbours(PACK2, t, around, pos, inv, n_cross, count)
        for i in range(Q):
            moved = near.stream(post1[t, i], vel(i), ("post", i), WEIGHTS[i])
            final[t, i] = jnp.where(near.alive, moved, 0.0)
            back = tuple(-v for v in vel(i))
            pulled[t, i] = near.stream(adj1[t, i], back, ("adj", i), 0.0)
        return carry

    lax.fori_loop(0, count, move, 0)
    base_slot = lax.axis_index("gx") * group + lax.axis_index("yz") * count

    def run(t, r, c):
        alive = pos[base_slot + t] >= 0
        f = [chunk(pops, t, i, r, c) for i in range(Q)]
        g = [chunk(pulled, t, i, r, c) for i in range(Q)]
        wall = plane_chunk(mask, t, r, c).astype(jnp.float32)
        solid = wall * plane_chunk(frac, t, r, c)
        rho, u, base = flow(f)
        back, ds = pullback(f, solid, rho, u, base, g)
        for i in range(Q):
            start[t, i, pl.ds(r, 8), pl.ds(c, LANES)] = jnp.where(alive, back[i], 0.0)
        total = wall * (ds + plane_chunk(dsolid, t, r, c))
        weighted[t, pl.ds(r, 8), pl.ds(c, LANES)] = jnp.where(alive, total, 0.0)

    for_chunks(count, run)

    n_high = sums.shape[0]
    high_iota = lax.broadcasted_iota(jnp.int32, (n_high, CELLS), 0)
    low_iota = lax.broadcasted_iota(jnp.int32, (LANES, CELLS), 0)

    def add(k, acc):
        t = k // TL
        r = k % TL
        ids = patch[t, pl.ds(r, 1), :]
        w = weighted[t, pl.ds(r, 1), :]
        w1 = w.astype(jnp.bfloat16).astype(jnp.float32)
        w2 = (w - w1).astype(jnp.bfloat16).astype(jnp.float32)
        w3 = w - w1 - w2
        high = high_iota == ids // LANES
        left = jnp.concatenate(
            [jnp.where(high, part, 0.0).astype(jnp.bfloat16) for part in (w1, w2, w3)],
            axis=0,
        )
        right = jnp.where(low_iota == ids % LANES, 1.0, 0.0).astype(jnp.bfloat16)
        return acc + lax.dot_general(
            left, right, (((1,), (1,)), ((), ())), preferred_element_type=jnp.float32
        )

    acc = lax.fori_loop(
        0, count * TL, add, jnp.zeros((3 * n_high, LANES), jnp.float32)
    )
    sums[...] = acc[:n_high] + acc[n_high : 2 * n_high] + acc[2 * n_high :]


def call(kernel, outs, scratch, args, in_smem=()):
    vmem = pl.BlockSpec(memory_space=pltpu.VMEM)
    smem = pl.BlockSpec(memory_space=pltpu.SMEM)
    return pl.pallas_call(
        kernel,
        out_shape=[jax.ShapeDtypeStruct(s, jnp.float32) for s in outs],
        in_specs=[smem if n in in_smem else vmem for n in range(len(args))],
        out_specs=[vmem] * len(outs),
        scratch_shapes=scratch,
        compiler_params=pltpu.CompilerParams(vmem_limit_bytes=40 << 20),
    )(*args)


def exchange(pack, ab, up, dn):
    n = lax.axis_size("gx")
    forward = [(i, (i + 1) % n) for i in range(n)]
    backward = [(j, i) for i, j in forward]
    below = lax.ppermute(up, "gx", forward)
    above = lax.ppermute(dn, "gx", backward)
    block = jnp.concatenate([ab, below, above], axis=1)
    return lax.all_gather(block, "yz", axis=0, tiled=True)


def body(pops_start, tile_pos, wall_mask, wall_frac, patch_id, probe):
    count = pops_start.shape[0]
    n_layers = lax.axis_size("gx")
    n_cross = lax.axis_size("yz")
    parts = n_layers * n_cross
    dims = (n_layers, n_cross)
    field = pops_start.shape
    plane = wall_frac.shape
    patch_dev = 64
    n_high = patch_dev * parts // LANES
    inverse = pltpu.SMEM((3, n_cross * count + 1), jnp.int32)

    def packs(pack):
        return [
            (count, pack.ab_rows, LANES),
            (count, pack.l_rows, LANES),
            (count, pack.l_rows, LANES),
        ]

    post0, ab, up, dn = call(
        first_kernel,
        [field] + packs(PACK1),
        [],
        (pops_start, wall_mask, wall_frac, probe),
    )
    around = exchange(PACK1, ab, up, dn)
    post1, adj1, dsolid, ab, up, dn = call(
        functools.partial(second_kernel, dims),
        [field, field, plane] + packs(PACK2),
        [
            pltpu.VMEM(field, jnp.float32),
            pltpu.VMEM((count, len(AXIAL)) + plane[1:], jnp.float32),
            inverse,
        ],
        (tile_pos, post0, wall_mask, wall_frac, probe, around),
        in_smem=(0,),
    )
    around = exchange(PACK2, ab, up, dn)
    pops_final, adjoint_start, sums = call(
        functools.partial(third_kernel, dims),
        [field, field, (n_high, LANES)],
        [
            pltpu.VMEM(field, jnp.float32),
            pltpu.VMEM(plane, jnp.float32),
            inverse,
        ],
        (tile_pos, post1, adj1, pops_start, wall_mask, wall_frac, patch_id, dsolid, around),
        in_smem=(0,),
    )
    shares = lax.all_to_all(
        sums.reshape(parts, patch_dev), ("gx", "yz"), 0, 0, tiled=True
    )
    return (pops_final, adjoint_start, jnp.sum(shares, axis=0))


def solution(mesh):
    in_specs = (
        P(("gx", "yz"), None, None, None),
        P(),
        P(("gx", "yz"), None, None),
        P(("gx", "yz"), None, None),
        P(("gx", "yz"), None, None),
        P(("gx", "yz"), None, None),
    )
    out_specs = (
        P(("gx", "yz"), None, None, None),
        P(("gx", "yz"), None, None, None),
        P(("gx", "yz")),
    )
    return jax.shard_map(body, mesh=mesh, in_specs=in_specs, out_specs=out_specs, check_vma=False)
```

```python
import functools

import jax
import jax.numpy as jnp
import numpy as np
from jax import lax
from jax.experimental import pallas as pl
from jax.experimental.pallas import tpu as pltpu
from jax.sharding import PartitionSpec as P

TL = 16
TA = 16
TB = 32
CELLS = TA * TB
LANES = 128
COLS = CELLS // LANES
OMEGA = 1.25

VELOCITY = np.array(
    [
        [0, 0, 0],
        [1, 0, 0],
        [-1, 0, 0],
        [0, 1, 0],
        [0, -1, 0],
        [0, 0, 1],
        [0, 0, -1],
        [1, 1, 0],
        [-1, -1, 0],
        [1, -1, 0],
        [-1, 1, 0],
        [1, 0, 1],
        [-1, 0, -1],
        [1, 0, -1],
        [-1, 0, 1],
        [0, 1, 1],
        [0, -1, -1],
        [0, 1, -1],
        [0, -1, 1],
    ]
)
Q = 19
WEIGHTS = [1.0 / 3.0] + [1.0 / 18.0] * 6 + [1.0 / 36.0] * 12
PAIRS = [(2 * k + 1, 2 * k + 2) for k in range(9)]
AXIAL = [i for i in range(Q) if VELOCITY[i, 0] != 0]


def vel(i):
    return tuple(int(v) for v in VELOCITY[i])


def members_of(dim, value):
    return [i for i in range(Q) if vel(i)[dim] == value]


def face_list(stage, dim, side):
    if stage == 1:
        return [("post", i) for i in members_of(dim, side)] + [("probe", 0)]
    return [("post", i) for i in members_of(dim, side)] + [
        ("adj", i) for i in members_of(dim, -side)
    ]


class Pack:
    def __init__(self, stage):
        self.n = len(face_list(stage, 0, 1))
        self.lists = {
            (d, s): face_list(stage, d, s) for d in range(3) for s in (-1, 1)
        }
        self.fold = 2 if 2 * self.n <= TB // 2 else 1
        self.a_cols = -(-2 * self.n * TB // LANES)
        self.b_cols = COLS // self.fold
        self.a_row = 0
        self.b_row = TL * self.a_cols
        self.ab_rows = self.b_row + TL * self.b_cols
        self.l_rows = self.n * COLS
        self.up_row = self.ab_rows
        self.dn_row = self.up_row + self.l_rows
        self.rows = self.dn_row + self.l_rows

    def slot(self, dim, side, key):
        j = self.lists[(dim, side)].index(key)
        return j if dim == 0 or side < 0 else j + self.n


PACK1 = Pack(1)
PACK2 = Pack(2)


def lane_roll(x, shift):
    shift = shift % x.shape[-1]
    return x if shift == 0 else pltpu.roll(x, shift, axis=x.ndim - 1)


def row_roll(x, shift):
    shift = shift % x.shape[0]
    return x if shift == 0 else pltpu.roll(x, shift, axis=0)


def lane_iota(shape):
    return lax.broadcasted_iota(jnp.int32, shape, len(shape) - 1)


def row_iota(shape):
    return lax.broadcasted_iota(jnp.int32, shape, 0)


def combine(c, parts):
    total = None
    for v, p in zip(c, parts):
        if v == 0:
            continue
        if total is None:
            total = p if v > 0 else -p
        else:
            total = total + p if v > 0 else total - p
    return total


def flow(f):
    rho = f[0]
    momentum = [None, None, None]
    for i, j in PAIRS:
        rho = rho + (f[i] + f[j])
        diff = f[i] - f[j]
        for d, v in enumerate(vel(i)):
            if v == 0:
                continue
            if momentum[d] is None:
                momentum[d] = diff if v > 0 else -diff
            else:
                momentum[d] = momentum[d] + diff if v > 0 else momentum[d] - diff
    inv = 1.0 / rho
    u = [m * inv for m in momentum]
    square = u[0] * u[0] + u[1] * u[1] + u[2] * u[2]
    return rho, u, 1.0 - 1.5 * square


def collide(f, solid, rho, u, base):
    fluid = 1.0 - solid
    keep = (1.0 - OMEGA) * fluid
    scale = OMEGA * fluid * rho
    out = [None] * Q
    out[0] = (keep + solid) * f[0] + WEIGHTS[0] * scale * base
    for i, j in PAIRS:
        along = combine(vel(i), u)
        ws = WEIGHTS[i] * scale
        even = ws * (base + 4.5 * along * along)
        odd = ws * (3.0 * along)
        out[i] = keep * f[i] + solid * f[j] + (even + odd)
        out[j] = keep * f[j] + solid * f[i] + (even - odd)
    return out


def pullback(f, solid, rho, u, base, g):
    fluid = 1.0 - solid
    keep = (1.0 - OMEGA) * fluid
    gain = OMEGA * fluid
    lin = [None, None, None]
    total = None
    dens = None
    cross = None

    def plus(a, b):
        return b if a is None else a + b

    if g[0] is not None:
        e = WEIGHTS[0] * g[0]
        total = e
        dens = e * base
        cross = OMEGA * (g[0] * f[0])
    for i, j in PAIRS:
        if g[i] is None:
            continue
        along = combine(vel(i), u)
        w = WEIGHTS[i]
        even = w * (g[i] + g[j])
        odd = w * (g[i] - g[j])
        total = plus(total, even)
        dens = plus(dens, even * (base + 4.5 * along * along) + 3.0 * along * odd)
        push = 3.0 * odd + 9.0 * along * even
        for d, v in enumerate(vel(i)):
            if v:
                lin[d] = plus(lin[d], push if v > 0 else -push)
        cross = plus(
            cross,
            g[i] * (f[j] - (1.0 - OMEGA) * f[i]) + g[j] * (f[i] - (1.0 - OMEGA) * f[j]),
        )
    lin = [
        (-3.0 * u[d] * total if lin[d] is None else lin[d] - 3.0 * u[d] * total)
        for d in range(3)
    ]
    dsolid = cross - OMEGA * rho * dens
    shared = gain * (dens - (lin[0] * u[0] + lin[1] * u[1] + lin[2] * u[2]))
    lin = [gain * v for v in lin]
    out = [None] * Q
    out[0] = shared if g[0] is None else (keep + solid) * g[0] + shared
    for i, j in PAIRS:
        slope = combine(vel(i), lin)
        if g[i] is None:
            out[i] = shared + slope
            out[j] = shared - slope
        else:
            out[i] = keep * g[i] + solid * g[j] + (shared + slope)
            out[j] = keep * g[j] + solid * g[i] + (shared - slope)
    return out, dsolid


def load_chunk(ref, t, i, r, c):
    return ref[t, i, pl.ds(8 * r, 8), pl.ds(c, LANES)]


def for_chunks(count, run):
    def step(k, carry):
        t = k // (2 * COLS)
        r = (k // COLS) % 2
        c = pl.multiple_of((k % COLS) * LANES, LANES)
        run(t, pl.multiple_of(r * 8, 8), c)
        return carry

    lax.fori_loop(0, count * 2 * COLS, step, 0)


def chunk(ref, t, i, r, c):
    return ref[t, i, pl.ds(r, 8), pl.ds(c, LANES)]


def plane_chunk(ref, t, r, c):
    return ref[t, pl.ds(r, 8), pl.ds(c, LANES)]


def write_faces(pack, t, get, ab_ref, up_ref, dn_ref):
    lane = lane_iota((TL, LANES))
    for col in range(pack.a_cols):
        acc = jnp.zeros((TL, LANES), jnp.float32)
        for side in (-1, 1):
            for key in pack.lists[(1, side)]:
                j = pack.slot(1, side, key)
                if j // 4 != col:
                    continue
                to = TB * (j % 4)
                if side < 0:
                    part = lane_roll(get(key, slice(None), slice(0, LANES)), to)
                else:
                    part = lane_roll(
                        get(key, slice(None), slice(CELLS - LANES, CELLS)),
                        to - (LANES - TB),
                    )
                acc = jnp.where((lane >> 5) == j % 4, part, acc)
        ab_ref[t, pack.a_row + TL * col : pack.a_row + TL * (col + 1), :] = acc
    for col in range(pack.b_cols):
        acc = jnp.zeros((TL, LANES), jnp.float32)
        for half in range(pack.fold):
            src = col + half * pack.b_cols
            for side in (-1, 1):
                for key in pack.lists[(2, side)]:
                    j = pack.slot(2, side, key) + half * (TB // 2)
                    part = get(key, slice(None), slice(LANES * src, LANES * (src + 1)))
                    part = lane_roll(part, j if side < 0 else j - (TB - 1))
                    acc = jnp.where((lane & (TB - 1)) == j, part, acc)
        ab_ref[t, pack.b_row + TL * col : pack.b_row + TL * (col + 1), :] = acc
    for side, ref in ((1, up_ref), (-1, dn_ref)):
        row = TL - 1 if side > 0 else 0
        for key in pack.lists[(0, side)]:
            j = pack.slot(0, side, key)
            for col in range(COLS):
                ref[t, j * COLS + col : j * COLS + col + 1, :] = get(
                    key, slice(row, row + 1), slice(LANES * col, LANES * (col + 1))
                )


def build_inverse(pos_ref, inv_ref, n_layers, group):
    layer = lax.axis_index("gx")
    for off in (-1, 0, 1):
        for w in range(group + 1):
            inv_ref[off + 1, w] = -1
        target = layer + off
        valid = (target >= 0) & (target < n_layers)
        first = jnp.clip(target, 0, n_layers - 1) * group
        for s in range(group):
            p = pos_ref[first + s]
            inv_ref[off + 1, jnp.where(valid & (p >= 0), p, group)] = s


class Neighbours:
    def __init__(self, pack, t, faces_ref, pos_ref, inv_ref, n_cross, count):
        self.pack = pack
        self.ref = faces_ref
        group = n_cross * count
        own = pos_ref[lax.axis_index("gx") * group + lax.axis_index("yz") * count + t]
        p = jnp.maximum(own, 0)
        a, b = p // count, p % count
        self.alive = own >= 0
        self.where = {}
        for d in [vel(i) for i in range(1, Q)]:
            ta, tb = a + d[1], b + d[2]
            ok = (ta >= 0) & (ta < n_cross) & (tb >= 0) & (tb < count)
            s = inv_ref[d[0] + 1, jnp.where(ok, ta * count + tb, group)]
            found = ok & (s >= 0)
            self.where[d] = (jnp.where(found, s, 0), found)
        self.planes = {}

    def a_face(self, d, side, key, fill):
        k, found = self.where[d]
        j = self.pack.slot(1, side, key)
        row = self.pack.a_row + TL * (j // 4)
        face = self.ref[k, row : row + TL, :]
        face = lane_roll(face, (LANES - TB if side > 0 else 0) - TB * (j % 4))
        return jnp.where(found, face, fill)

    def b_plane(self, d):
        if d not in self.planes:
            k, found = self.where[d]
            row = self.pack.b_row
            half = jnp.concatenate(
                [
                    self.ref[k, row + TL * c : row + TL * (c + 1), :]
                    for c in range(self.pack.b_cols)
                ],
                axis=1,
            )
            if self.pack.fold == 2:
                half = jnp.concatenate([half, lane_roll(half, -(TB // 2))], axis=1)
            self.planes[d] = half
        return self.planes[d], self.where[d][1]

    def l_row(self, d, side, key, fill):
        k, found = self.where[d]
        first = self.pack.up_row if side > 0 else self.pack.dn_row
        first = first + self.pack.slot(0, side, key) * COLS
        row = jnp.concatenate(
            [self.ref[k, first + c : first + c + 1, :] for c in range(COLS)], axis=1
        )
        return jnp.where(found, row, fill)

    def stream(self, own, c, key, fill):
        cl, ca, cb = c
        shape = (TL, CELLS)
        lane = lane_iota(shape)
        edge_b = (lane & (TB - 1)) == (TB - 1 if cb > 0 else 0)
        edge_a = (lane >> 5) == (TA - 1 if ca > 0 else 0)
        x = own
        if ca:
            face = self.a_face((0, -ca, 0), ca, key, fill)
            part = slice(CELLS - LANES, CELLS) if ca > 0 else slice(0, LANES)
            inner = lane_iota((TL, LANES))
            hit = inner >= LANES - TB if ca > 0 else inner < TB
            face = jnp.where(hit, face, x[:, part])
            x = jnp.concatenate(
                [x[:, : CELLS - LANES], face] if ca > 0 else [face, x[:, LANES:]], axis=1
            )
        if cb:
            j = self.pack.slot(2, cb, key)
            shift = -1 - j if cb > 0 else TB - j
            plane, found = self.b_plane((0, 0, -cb))
            face = jnp.where(found, lane_roll(plane, shift), fill)
            if ca:
                plane, found = self.b_plane((0, -ca, -cb))
                corner = jnp.where(found, lane_roll(plane, shift), fill)
                at = (TA - 1 if ca > 0 else 0) + (-1 if cb > 0 else 1)
                face = jnp.where((lane >> 5) == at % TA, corner, face)
            x = jnp.where(edge_b, face, x)
        if cl:
            row = self.l_row((-cl, 0, 0), cl, key, fill)
            lane_r = lane_iota((1, CELLS))
            if ca:
                corner = self.l_row((-cl, -ca, 0), cl, key, fill)
                row = jnp.where((lane_r >> 5) == (TA - 1 if ca > 0 else 0), corner, row)
            if cb:
                corner = self.l_row((-cl, 0, -cb), cl, key, fill)
                corner = lane_roll(corner, -TB if cb > 0 else TB)
                row = jnp.where((lane_r & (TB - 1)) == (TB - 1 if cb > 0 else 0), corner, row)
            at = TL - 1 if cl > 0 else 0
            x = jnp.where(row_iota(shape) == at, jnp.broadcast_to(row, shape), x)
        return row_roll(lane_roll(x, TB * ca + cb), cl)


def first_kernel(pops_in, mask_in, frac_in, probe_in, post, solid, probe, ab, up, dn, pops, mask, frac, sems):
    count = pops.shape[0]
    small = [
        pltpu.make_async_copy(src, dst, sems.at[n])
        for n, (src, dst) in enumerate(((mask_in, mask), (frac_in, frac), (probe_in, probe)))
    ]
    halves = [(t, r) for t in range(count) for r in range(2)]
    large = [
        pltpu.make_async_copy(
            pops_in.at[t, :, pl.ds(8 * r, 8), :],
            pops.at[t, :, pl.ds(8 * r, 8), :],
            sems.at[len(small) + n],
        )
        for n, (t, r) in enumerate(halves)
    ]
    for copy in small[:2] + large + small[2:]:
        copy.start()
    for copy in small[:2]:
        copy.wait()
    solid[...] = mask[...].astype(jnp.float32) * frac[...]

    for n, (t, r) in enumerate(halves):
        large[n].wait()

        def run(k, carry, t=t, r=8 * r):
            c = pl.multiple_of(k * LANES, LANES)
            f = [chunk(pops, t, i, r, c) for i in range(Q)]
            out = collide(f, plane_chunk(solid, t, r, c), *flow(f))
            for i in range(Q):
                post[t, i, pl.ds(r, 8), pl.ds(c, LANES)] = out[i]
            return carry

        lax.fori_loop(0, COLS, run, 0)
    small[2].wait()

    def faces(t, carry):
        def get(key, rows, lanes):
            if key[0] == "probe":
                return probe[t, rows, lanes]
            return post[t, key[1], rows, lanes]

        write_faces(PACK1, t, get, ab, up, dn)
        return carry

    lax.fori_loop(0, count, faces, 0)


def second_kernel(
    dims, pos, post0, solid_in, probe, around, post1, adj1, dsolid, ab, up, dn, state, pulled, inv
):
    n_layers, n_cross = dims
    count = post0.shape[0]
    build_inverse(pos, inv, n_layers, n_cross * count)

    def move(t, carry):
        near = Neighbours(PACK1, t, around, pos, inv, n_cross, count)
        for i in range(Q):
            state[t, i] = near.stream(post0[t, i], vel(i), ("post", i), WEIGHTS[i])
        for n, i in enumerate(AXIAL):
            back = tuple(-v for v in vel(i))
            moved = near.stream(probe[t], back, ("probe", 0), 0.0)
            pulled[t, n] = moved if vel(i)[0] > 0 else -moved
        return carry

    lax.fori_loop(0, count, move, 0)

    def run(t, r, c):
        f = [chunk(state, t, i, r, c) for i in range(Q)]
        solid = plane_chunk(solid_in, t, r, c)
        rho, u, base = flow(f)
        out = collide(f, solid, rho, u, base)
        for i in range(Q):
            post1[t, i, pl.ds(r, 8), pl.ds(c, LANES)] = out[i]
        g = [None] * Q
        for n, i in enumerate(AXIAL):
            g[i] = chunk(pulled, t, n, r, c)
        back, ds = pullback(f, solid, rho, u, base, g)
        for i in range(Q):
            adj1[t, i, pl.ds(r, 8), pl.ds(c, LANES)] = back[i]
        dsolid[t, pl.ds(r, 8), pl.ds(c, LANES)] = ds

    for_chunks(count, run)

    def faces(t, carry):
        def get(key, rows, lanes):
            return (post1 if key[0] == "post" else adj1)[t, key[1], rows, lanes]

        write_faces(PACK2, t, get, ab, up, dn)
        return carry

    lax.fori_loop(0, count, faces, 0)


def third_kernel(
    dims, pos, post1, adj1, pops, mask, solid_in, patch, dsolid, around, final_out, start_out, sums, final, start, pulled, weighted, inv, sems
):
    n_layers, n_cross = dims
    count = pops.shape[0]
    group = n_cross * count
    build_inverse(pos, inv, n_layers, group)

    def move(t, carry):
        near = Neighbours(PACK2, t, around, pos, inv, n_cross, count)
        for i in range(Q):
            moved = near.stream(post1[t, i], vel(i), ("post", i), WEIGHTS[i])
            final[t, i] = jnp.where(near.alive, moved, 0.0)
            back = tuple(-v for v in vel(i))
            pulled[t, i] = near.stream(adj1[t, i], back, ("adj", i), 0.0)
        return carry

    lax.fori_loop(0, count, move, 0)
    out_final = pltpu.make_async_copy(final, final_out, sems.at[0])
    out_final.start()
    base_slot = lax.axis_index("gx") * group + lax.axis_index("yz") * count

    def run(t, r, c):
        alive = pos[base_slot + t] >= 0
        f = [chunk(pops, t, i, r, c) for i in range(Q)]
        g = [chunk(pulled, t, i, r, c) for i in range(Q)]
        wall = plane_chunk(mask, t, r, c).astype(jnp.float32)
        solid = plane_chunk(solid_in, t, r, c)
        rho, u, base = flow(f)
        back, ds = pullback(f, solid, rho, u, base, g)
        for i in range(Q):
            start[t, i, pl.ds(r, 8), pl.ds(c, LANES)] = jnp.where(alive, back[i], 0.0)
        total = wall * (ds + plane_chunk(dsolid, t, r, c))
        weighted[t, pl.ds(r, 8), pl.ds(c, LANES)] = jnp.where(alive, total, 0.0)

    for_chunks(count, run)
    out_start = pltpu.make_async_copy(start, start_out, sems.at[1])
    out_start.start()

    n_high = sums.shape[0]
    high_iota = lax.broadcasted_iota(jnp.int32, (n_high, CELLS), 0)
    low_iota = lax.broadcasted_iota(jnp.int32, (LANES, CELLS), 0)

    def add(k, acc):
        t = k // 2
        r = pl.multiple_of((k % 2) * 8, 8)
        ids8 = patch[t, pl.ds(r, 8), :]
        w8 = weighted[t, pl.ds(r, 8), :]
        for n in range(8):
            ids = ids8[n : n + 1]
            w = w8[n : n + 1]
            w1 = w.astype(jnp.bfloat16).astype(jnp.float32)
            w2 = (w - w1).astype(jnp.bfloat16).astype(jnp.float32)
            w3 = w - w1 - w2
            high = high_iota == (ids >> 7)
            left = jnp.concatenate(
                [jnp.where(high, part, 0.0).astype(jnp.bfloat16) for part in (w1, w2, w3)],
                axis=0,
            )
            right = jnp.where(low_iota == (ids & (LANES - 1)), 1.0, 0.0).astype(jnp.bfloat16)
            acc = acc + lax.dot_general(
                left, right, (((1,), (1,)), ((), ())), preferred_element_type=jnp.float32
            )
        return acc

    acc = lax.fori_loop(
        0, count * 2, add, jnp.zeros((3 * n_high, LANES), jnp.float32)
    )
    out_final.wait()
    out_start.wait()
    sums[...] = acc[:n_high] + acc[n_high : 2 * n_high] + acc[2 * n_high :]


def call(kernel, outs, scratch, args, in_smem=(), in_hbm=(), out_hbm=()):
    vmem = pl.BlockSpec(memory_space=pltpu.VMEM)
    hbm = pl.BlockSpec(memory_space=pltpu.HBM)
    smem = pl.BlockSpec(memory_space=pltpu.SMEM)
    return pl.pallas_call(
        kernel,
        out_shape=[jax.ShapeDtypeStruct(s, jnp.float32) for s in outs],
        in_specs=[
            smem if n in in_smem else hbm if n in in_hbm else vmem for n in range(len(args))
        ],
        out_specs=[hbm if n in out_hbm else vmem for n in range(len(outs))],
        scratch_shapes=scratch,
        compiler_params=pltpu.CompilerParams(vmem_limit_bytes=40 << 20),
    )(*args)


def exchange(pack, ab, up, dn):
    n = lax.axis_size("gx")
    forward = [(i, (i + 1) % n) for i in range(n)]
    backward = [(j, i) for i, j in forward]
    below = lax.ppermute(up, "gx", forward)
    above = lax.ppermute(dn, "gx", backward)
    block = jnp.concatenate([ab, below, above], axis=1)
    return lax.all_gather(block, "yz", axis=0, tiled=True)


def body(pops_start, tile_pos, wall_mask, wall_frac, patch_id, probe):
    count = pops_start.shape[0]
    n_layers = lax.axis_size("gx")
    n_cross = lax.axis_size("yz")
    parts = n_layers * n_cross
    dims = (n_layers, n_cross)
    field = pops_start.shape
    plane = wall_frac.shape
    patch_dev = 64
    n_high = patch_dev * parts // LANES
    inverse = pltpu.SMEM((3, n_cross * count + 1), jnp.int32)

    def packs(pack):
        return [
            (count, pack.ab_rows, LANES),
            (count, pack.l_rows, LANES),
            (count, pack.l_rows, LANES),
        ]

    post0, solid, probe_kept, ab, up, dn = call(
        first_kernel,
        [field, plane, plane] + packs(PACK1),
        [
            pltpu.VMEM(field, jnp.float32),
            pltpu.VMEM(plane, jnp.int32),
            pltpu.VMEM(plane, jnp.float32),
            pltpu.SemaphoreType.DMA((3 + 2 * count,)),
        ],
        tuple(
            pltpu.with_memory_space_constraint(x, pltpu.HBM)
            for x in (pops_start, wall_mask, wall_frac, probe)
        ),
        in_hbm=range(4),
    )
    around = exchange(PACK1, ab, up, dn)
    post1, adj1, dsolid, ab, up, dn = call(
        functools.partial(second_kernel, dims),
        [field, field, plane] + packs(PACK2),
        [
            pltpu.VMEM(field, jnp.float32),
            pltpu.VMEM((count, len(AXIAL)) + plane[1:], jnp.float32),
            inverse,
        ],
        (tile_pos, post0, solid, probe_kept, around),
        in_smem=(0,),
    )
    around = exchange(PACK2, ab, up, dn)
    pops_final, adjoint_start, sums = call(
        functools.partial(third_kernel, dims),
        [field, field, (n_high, LANES)],
        [
            pltpu.VMEM(field, jnp.float32),
            pltpu.VMEM(field, jnp.float32),
            pltpu.VMEM(field, jnp.float32),
            pltpu.VMEM(plane, jnp.float32),
            inverse,
            pltpu.SemaphoreType.DMA((2,)),
        ],
        (tile_pos, post1, adj1, pops_start, wall_mask, solid, patch_id, dsolid, around),
        in_smem=(0,),
        out_hbm=(0, 1),
    )
    shares = lax.all_to_all(
        sums.reshape(parts, patch_dev), ("gx", "yz"), 0, 0, tiled=True
    )
    return (pops_final, adjoint_start, jnp.sum(shares, axis=0))


def solution(mesh):
    in_specs = (
        P(("gx", "yz"), None, None, None),
        P(),
        P(("gx", "yz"), None, None),
        P(("gx", "yz"), None, None),
        P(("gx", "yz"), None, None),
        P(("gx", "yz"), None, None),
    )
    out_specs = (
        P(("gx", "yz"), None, None, None),
        P(("gx", "yz"), None, None, None),
        P(("gx", "yz")),
    )
    return jax.shard_map(body, mesh=mesh, in_specs=in_specs, out_specs=out_specs, check_vma=False)
```

```python
import functools

import jax
import jax.numpy as jnp
import numpy as np
from jax import lax
from jax.experimental import pallas as pl
from jax.experimental.pallas import tpu as pltpu
from jax.sharding import PartitionSpec as P

TL = 16
TA = 16
TB = 32
CELLS = TA * TB
LANES = 128
COLS = CELLS // LANES
OMEGA = 1.25

VELOCITY = np.array(
    [
        [0, 0, 0],
        [1, 0, 0],
        [-1, 0, 0],
        [0, 1, 0],
        [0, -1, 0],
        [0, 0, 1],
        [0, 0, -1],
        [1, 1, 0],
        [-1, -1, 0],
        [1, -1, 0],
        [-1, 1, 0],
        [1, 0, 1],
        [-1, 0, -1],
        [1, 0, -1],
        [-1, 0, 1],
        [0, 1, 1],
        [0, -1, -1],
        [0, 1, -1],
        [0, -1, 1],
    ]
)
Q = 19
WEIGHTS = [1.0 / 3.0] + [1.0 / 18.0] * 6 + [1.0 / 36.0] * 12
PAIRS = [(2 * k + 1, 2 * k + 2) for k in range(9)]
AXIAL = [i for i in range(Q) if VELOCITY[i, 0] != 0]


def vel(i):
    return tuple(int(v) for v in VELOCITY[i])


def members_of(dim, value):
    return [i for i in range(Q) if vel(i)[dim] == value]


def face_list(stage, dim, side):
    if stage == 1:
        return [("post", i) for i in members_of(dim, side)] + [("probe", 0)]
    return [("post", i) for i in members_of(dim, side)] + [
        ("adj", i) for i in members_of(dim, -side)
    ]


class Pack:
    def __init__(self, stage):
        self.n = len(face_list(stage, 0, 1))
        self.lists = {
            (d, s): face_list(stage, d, s) for d in range(3) for s in (-1, 1)
        }
        self.fold = 2 if 2 * self.n <= TB // 2 else 1
        self.a_cols = -(-2 * self.n * TB // LANES)
        self.b_cols = COLS // self.fold
        self.a_row = 0
        self.b_row = TL * self.a_cols
        self.ab_rows = self.b_row + TL * self.b_cols
        self.l_rows = self.n * COLS
        self.up_row = self.ab_rows
        self.dn_row = self.up_row + self.l_rows
        self.rows = self.dn_row + self.l_rows

    def slot(self, dim, side, key):
        j = self.lists[(dim, side)].index(key)
        return j if dim == 0 or side < 0 else j + self.n


PACK1 = Pack(1)
PACK2 = Pack(2)


def lane_roll(x, shift):
    shift = shift % x.shape[-1]
    return x if shift == 0 else pltpu.roll(x, shift, axis=x.ndim - 1)


def row_roll(x, shift):
    shift = shift % x.shape[0]
    return x if shift == 0 else pltpu.roll(x, shift, axis=0)


def lane_iota(shape):
    return lax.broadcasted_iota(jnp.int32, shape, len(shape) - 1)


def row_iota(shape):
    return lax.broadcasted_iota(jnp.int32, shape, 0)


def combine(c, parts):
    total = None
    for v, p in zip(c, parts):
        if v == 0:
            continue
        if total is None:
            total = p if v > 0 else -p
        else:
            total = total + p if v > 0 else total - p
    return total


def flow(f):
    rho = f[0]
    momentum = [None, None, None]
    for i, j in PAIRS:
        rho = rho + (f[i] + f[j])
        diff = f[i] - f[j]
        for d, v in enumerate(vel(i)):
            if v == 0:
                continue
            if momentum[d] is None:
                momentum[d] = diff if v > 0 else -diff
            else:
                momentum[d] = momentum[d] + diff if v > 0 else momentum[d] - diff
    inv = 1.0 / rho
    u = [m * inv for m in momentum]
    square = u[0] * u[0] + u[1] * u[1] + u[2] * u[2]
    return rho, u, 1.0 - 1.5 * square


def collide(f, solid, rho, u, base):
    fluid = 1.0 - solid
    keep = (1.0 - OMEGA) * fluid
    scale = OMEGA * fluid * rho
    out = [None] * Q
    out[0] = (keep + solid) * f[0] + WEIGHTS[0] * scale * base
    for i, j in PAIRS:
        along = combine(vel(i), u)
        ws = WEIGHTS[i] * scale
        even = ws * (base + 4.5 * along * along)
        odd = ws * (3.0 * along)
        out[i] = keep * f[i] + solid * f[j] + (even + odd)
        out[j] = keep * f[j] + solid * f[i] + (even - odd)
    return out


def pullback(f, solid, rho, u, base, g):
    fluid = 1.0 - solid
    keep = (1.0 - OMEGA) * fluid
    gain = OMEGA * fluid
    lin = [None, None, None]
    total = None
    dens = None
    cross = None

    def plus(a, b):
        return b if a is None else a + b

    if g[0] is not None:
        e = WEIGHTS[0] * g[0]
        total = e
        dens = e * base
        cross = OMEGA * (g[0] * f[0])
    for i, j in PAIRS:
        if g[i] is None:
            continue
        along = combine(vel(i), u)
        w = WEIGHTS[i]
        even = w * (g[i] + g[j])
        odd = w * (g[i] - g[j])
        total = plus(total, even)
        dens = plus(dens, even * (base + 4.5 * along * along) + 3.0 * along * odd)
        push = 3.0 * odd + 9.0 * along * even
        for d, v in enumerate(vel(i)):
            if v:
                lin[d] = plus(lin[d], push if v > 0 else -push)
        cross = plus(
            cross,
            g[i] * (f[j] - (1.0 - OMEGA) * f[i]) + g[j] * (f[i] - (1.0 - OMEGA) * f[j]),
        )
    lin = [
        (-3.0 * u[d] * total if lin[d] is None else lin[d] - 3.0 * u[d] * total)
        for d in range(3)
    ]
    dsolid = cross - OMEGA * rho * dens
    shared = gain * (dens - (lin[0] * u[0] + lin[1] * u[1] + lin[2] * u[2]))
    lin = [gain * v for v in lin]
    out = [None] * Q
    out[0] = shared if g[0] is None else (keep + solid) * g[0] + shared
    for i, j in PAIRS:
        slope = combine(vel(i), lin)
        if g[i] is None:
            out[i] = shared + slope
            out[j] = shared - slope
        else:
            out[i] = keep * g[i] + solid * g[j] + (shared + slope)
            out[j] = keep * g[j] + solid * g[i] + (shared - slope)
    return out, dsolid


def load_chunk(ref, t, i, r, c):
    return ref[t, i, pl.ds(8 * r, 8), pl.ds(c, LANES)]


def for_chunks(count, run):
    def step(k, carry):
        t = k // (2 * COLS)
        r = (k // COLS) % 2
        c = pl.multiple_of((k % COLS) * LANES, LANES)
        run(t, pl.multiple_of(r * 8, 8), c)
        return carry

    lax.fori_loop(0, count * 2 * COLS, step, 0)


def chunk(ref, t, i, r, c):
    return ref[t, i, pl.ds(r, 8), pl.ds(c, LANES)]


def plane_chunk(ref, t, r, c):
    return ref[t, pl.ds(r, 8), pl.ds(c, LANES)]


def write_faces(pack, t, get, ab_ref, up_ref, dn_ref):
    lane = lane_iota((TL, LANES))
    for col in range(pack.a_cols):
        acc = jnp.zeros((TL, LANES), jnp.float32)
        for side in (-1, 1):
            for key in pack.lists[(1, side)]:
                j = pack.slot(1, side, key)
                if j // 4 != col:
                    continue
                to = TB * (j % 4)
                if side < 0:
                    part = lane_roll(get(key, slice(None), slice(0, LANES)), to)
                else:
                    part = lane_roll(
                        get(key, slice(None), slice(CELLS - LANES, CELLS)),
                        to - (LANES - TB),
                    )
                acc = jnp.where((lane >> 5) == j % 4, part, acc)
        ab_ref[t, pack.a_row + TL * col : pack.a_row + TL * (col + 1), :] = acc
    for col in range(pack.b_cols):
        acc = jnp.zeros((TL, LANES), jnp.float32)
        for half in range(pack.fold):
            src = col + half * pack.b_cols
            for side in (-1, 1):
                for key in pack.lists[(2, side)]:
                    j = pack.slot(2, side, key) + half * (TB // 2)
                    part = get(key, slice(None), slice(LANES * src, LANES * (src + 1)))
                    part = lane_roll(part, j if side < 0 else j - (TB - 1))
                    acc = jnp.where((lane & (TB - 1)) == j, part, acc)
        ab_ref[t, pack.b_row + TL * col : pack.b_row + TL * (col + 1), :] = acc
    for side, ref in ((1, up_ref), (-1, dn_ref)):
        row = TL - 1 if side > 0 else 0
        for key in pack.lists[(0, side)]:
            j = pack.slot(0, side, key)
            for col in range(COLS):
                ref[t, j * COLS + col : j * COLS + col + 1, :] = get(
                    key, slice(row, row + 1), slice(LANES * col, LANES * (col + 1))
                )


def build_inverse(pos_ref, inv_ref, n_layers, group):
    layer = lax.axis_index("gx")
    for off in (-1, 0, 1):
        for w in range(group + 1):
            inv_ref[off + 1, w] = -1
        target = layer + off
        valid = (target >= 0) & (target < n_layers)
        first = jnp.clip(target, 0, n_layers - 1) * group
        for s in range(group):
            p = pos_ref[first + s]
            inv_ref[off + 1, jnp.where(valid & (p >= 0), p, group)] = s


class Neighbours:
    def __init__(self, pack, t, faces_ref, pos_ref, inv_ref, n_cross, count):
        self.pack = pack
        self.ref = faces_ref
        group = n_cross * count
        own = pos_ref[lax.axis_index("gx") * group + lax.axis_index("yz") * count + t]
        p = jnp.maximum(own, 0)
        a, b = p // count, p % count
        self.alive = own >= 0
        self.where = {}
        for d in [vel(i) for i in range(1, Q)]:
            ta, tb = a + d[1], b + d[2]
            ok = (ta >= 0) & (ta < n_cross) & (tb >= 0) & (tb < count)
            s = inv_ref[d[0] + 1, jnp.where(ok, ta * count + tb, group)]
            found = ok & (s >= 0)
            self.where[d] = (jnp.where(found, s, 0), found)
        self.planes = {}

    def a_face(self, d, side, key, fill):
        k, found = self.where[d]
        j = self.pack.slot(1, side, key)
        row = self.pack.a_row + TL * (j // 4)
        face = self.ref[k, row : row + TL, :]
        face = lane_roll(face, (LANES - TB if side > 0 else 0) - TB * (j % 4))
        return jnp.where(found, face, fill)

    def b_plane(self, d):
        if d not in self.planes:
            k, found = self.where[d]
            row = self.pack.b_row
            half = jnp.concatenate(
                [
                    self.ref[k, row + TL * c : row + TL * (c + 1), :]
                    for c in range(self.pack.b_cols)
                ],
                axis=1,
            )
            if self.pack.fold == 2:
                half = jnp.concatenate([half, lane_roll(half, -(TB // 2))], axis=1)
            self.planes[d] = half
        return self.planes[d], self.where[d][1]

    def l_row(self, d, side, key, fill):
        k, found = self.where[d]
        first = self.pack.up_row if side > 0 else self.pack.dn_row
        first = first + self.pack.slot(0, side, key) * COLS
        row = jnp.concatenate(
            [self.ref[k, first + c : first + c + 1, :] for c in range(COLS)], axis=1
        )
        return jnp.where(found, row, fill)

    def stream(self, own, c, key, fill):
        cl, ca, cb = c
        shape = (TL, CELLS)
        lane = lane_iota(shape)
        edge_b = (lane & (TB - 1)) == (TB - 1 if cb > 0 else 0)
        edge_a = (lane >> 5) == (TA - 1 if ca > 0 else 0)
        x = own
        if ca:
            face = self.a_face((0, -ca, 0), ca, key, fill)
            part = slice(CELLS - LANES, CELLS) if ca > 0 else slice(0, LANES)
            inner = lane_iota((TL, LANES))
            hit = inner >= LANES - TB if ca > 0 else inner < TB
            face = jnp.where(hit, face, x[:, part])
            x = jnp.concatenate(
                [x[:, : CELLS - LANES], face] if ca > 0 else [face, x[:, LANES:]], axis=1
            )
        if cb:
            j = self.pack.slot(2, cb, key)
            shift = -1 - j if cb > 0 else TB - j
            plane, found = self.b_plane((0, 0, -cb))
            face = jnp.where(found, lane_roll(plane, shift), fill)
            if ca:
                plane, found = self.b_plane((0, -ca, -cb))
                corner = jnp.where(found, lane_roll(plane, shift), fill)
                at = (TA - 1 if ca > 0 else 0) + (-1 if cb > 0 else 1)
                face = jnp.where((lane >> 5) == at % TA, corner, face)
            x = jnp.where(edge_b, face, x)
        if cl:
            row = self.l_row((-cl, 0, 0), cl, key, fill)
            lane_r = lane_iota((1, CELLS))
            if ca:
                corner = self.l_row((-cl, -ca, 0), cl, key, fill)
                row = jnp.where((lane_r >> 5) == (TA - 1 if ca > 0 else 0), corner, row)
            if cb:
                corner = self.l_row((-cl, 0, -cb), cl, key, fill)
                corner = lane_roll(corner, -TB if cb > 0 else TB)
                row = jnp.where((lane_r & (TB - 1)) == (TB - 1 if cb > 0 else 0), corner, row)
            at = TL - 1 if cl > 0 else 0
            x = jnp.where(row_iota(shape) == at, jnp.broadcast_to(row, shape), x)
        return row_roll(lane_roll(x, TB * ca + cb), cl)


def first_kernel(pops_in, mask_in, frac_in, probe_in, post, solid, probe, ab, up, dn, pops, mask, frac, sems):
    count = pops.shape[0]
    small = [
        pltpu.make_async_copy(src, dst, sems.at[n])
        for n, (src, dst) in enumerate(((mask_in, mask), (frac_in, frac), (probe_in, probe)))
    ]
    halves = [(t, r) for t in range(count) for r in range(2)]
    large = [
        pltpu.make_async_copy(
            pops_in.at[t, :, pl.ds(8 * r, 8), :],
            pops.at[t, :, pl.ds(8 * r, 8), :],
            sems.at[len(small) + n],
        )
        for n, (t, r) in enumerate(halves)
    ]
    for copy in small[:2] + large + small[2:]:
        copy.start()
    for copy in small[:2]:
        copy.wait()
    solid[...] = mask[...].astype(jnp.float32) * frac[...]

    for n, (t, r) in enumerate(halves):
        large[n].wait()

        def run(k, carry, t=t, r=8 * r):
            c = pl.multiple_of(k * LANES, LANES)
            f = [chunk(pops, t, i, r, c) for i in range(Q)]
            out = collide(f, plane_chunk(solid, t, r, c), *flow(f))
            for i in range(Q):
                post[t, i, pl.ds(r, 8), pl.ds(c, LANES)] = out[i]
            return carry

        lax.fori_loop(0, COLS, run, 0)
    small[2].wait()

    def faces(t, carry):
        def get(key, rows, lanes):
            if key[0] == "probe":
                return probe[t, rows, lanes]
            return post[t, key[1], rows, lanes]

        write_faces(PACK1, t, get, ab, up, dn)
        return carry

    lax.fori_loop(0, count, faces, 0)


def second_kernel(
    dims, pos, post0, solid_in, probe, around, post1, adj1, dsolid, ab, up, dn, state, pulled, inv
):
    n_layers, n_cross = dims
    count = post0.shape[0]
    build_inverse(pos, inv, n_layers, n_cross * count)

    def move(t, carry):
        near = Neighbours(PACK1, t, around, pos, inv, n_cross, count)
        for i in range(Q):
            state[t, i] = near.stream(post0[t, i], vel(i), ("post", i), WEIGHTS[i])
        for n, i in enumerate(AXIAL):
            back = tuple(-v for v in vel(i))
            moved = near.stream(probe[t], back, ("probe", 0), 0.0)
            pulled[t, n] = moved if vel(i)[0] > 0 else -moved
        return carry

    lax.fori_loop(0, count, move, 0)

    def run(t, r, c):
        f = [chunk(state, t, i, r, c) for i in range(Q)]
        solid = plane_chunk(solid_in, t, r, c)
        rho, u, base = flow(f)
        out = collide(f, solid, rho, u, base)
        for i in range(Q):
            post1[t, i, pl.ds(r, 8), pl.ds(c, LANES)] = out[i]
        g = [None] * Q
        for n, i in enumerate(AXIAL):
            g[i] = chunk(pulled, t, n, r, c)
        back, ds = pullback(f, solid, rho, u, base, g)
        for i in range(Q):
            adj1[t, i, pl.ds(r, 8), pl.ds(c, LANES)] = back[i]
        dsolid[t, pl.ds(r, 8), pl.ds(c, LANES)] = ds

    for_chunks(count, run)

    def faces(t, carry):
        def get(key, rows, lanes):
            return (post1 if key[0] == "post" else adj1)[t, key[1], rows, lanes]

        write_faces(PACK2, t, get, ab, up, dn)
        return carry

    lax.fori_loop(0, count, faces, 0)


def third_kernel(
    dims, pos, post1, adj1, pops, mask, solid_in, patch, dsolid, around, final_out, start_out, sums, final, start, pulled, weighted, inv, sems
):
    n_layers, n_cross = dims
    count = pops.shape[0]
    group = n_cross * count
    build_inverse(pos, inv, n_layers, group)

    def move(t, carry):
        near = Neighbours(PACK2, t, around, pos, inv, n_cross, count)
        for i in range(Q):
            moved = near.stream(post1[t, i], vel(i), ("post", i), WEIGHTS[i])
            final[t, i] = jnp.where(near.alive, moved, 0.0)
            back = tuple(-v for v in vel(i))
            pulled[t, i] = near.stream(adj1[t, i], back, ("adj", i), 0.0)
        return carry

    lax.fori_loop(0, count, move, 0)
    out_final = pltpu.make_async_copy(final, final_out, sems.at[0])
    out_final.start()
    base_slot = lax.axis_index("gx") * group + lax.axis_index("yz") * count

    def run(t, r, c):
        alive = pos[base_slot + t] >= 0
        f = [chunk(pops, t, i, r, c) for i in range(Q)]
        g = [chunk(pulled, t, i, r, c) for i in range(Q)]
        wall = plane_chunk(mask, t, r, c).astype(jnp.float32)
        solid = plane_chunk(solid_in, t, r, c)
        rho, u, base = flow(f)
        back, ds = pullback(f, solid, rho, u, base, g)
        for i in range(Q):
            start[t, i, pl.ds(r, 8), pl.ds(c, LANES)] = jnp.where(alive, back[i], 0.0)
        total = wall * (ds + plane_chunk(dsolid, t, r, c))
        weighted[t, pl.ds(r, 8), pl.ds(c, LANES)] = jnp.where(alive, total, 0.0)

    for_chunks(count, run)
    out_start = pltpu.make_async_copy(start, start_out, sems.at[1])
    out_start.start()

    n_high = sums.shape[0]
    high_iota = lax.broadcasted_iota(jnp.int32, (n_high, CELLS), 0)
    low_iota = lax.broadcasted_iota(jnp.int32, (LANES, CELLS), 0)

    def add(k, acc):
        t = k // 2
        r = pl.multiple_of((k % 2) * 8, 8)
        ids8 = patch[t, pl.ds(r, 8), :]
        w8 = weighted[t, pl.ds(r, 8), :]
        for n in range(8):
            ids = ids8[n : n + 1]
            w = w8[n : n + 1]
            w1 = w.astype(jnp.bfloat16).astype(jnp.float32)
            w2 = (w - w1).astype(jnp.bfloat16).astype(jnp.float32)
            w3 = w - w1 - w2
            high = high_iota == (ids >> 7)
            left = jnp.concatenate(
                [jnp.where(high, part, 0.0).astype(jnp.bfloat16) for part in (w1, w2, w3)],
                axis=0,
            )
            right = jnp.where(low_iota == (ids & (LANES - 1)), 1.0, 0.0).astype(jnp.bfloat16)
            acc = acc + lax.dot_general(
                left, right, (((1,), (1,)), ((), ())), preferred_element_type=jnp.float32
            )
        return acc

    acc = lax.fori_loop(
        0, count * 2, add, jnp.zeros((3 * n_high, LANES), jnp.float32)
    )
    out_final.wait()
    out_start.wait()
    sums[...] = acc[:n_high] + acc[n_high : 2 * n_high] + acc[2 * n_high :]


def call(kernel, outs, scratch, args, in_smem=(), in_hbm=(), out_hbm=()):
    vmem = pl.BlockSpec(memory_space=pltpu.VMEM)
    hbm = pl.BlockSpec(memory_space=pltpu.HBM)
    smem = pl.BlockSpec(memory_space=pltpu.SMEM)
    return pl.pallas_call(
        kernel,
        out_shape=[jax.ShapeDtypeStruct(s, jnp.float32) for s in outs],
        in_specs=[
            smem if n in in_smem else hbm if n in in_hbm else vmem for n in range(len(args))
        ],
        out_specs=[hbm if n in out_hbm else vmem for n in range(len(outs))],
        scratch_shapes=scratch,
        compiler_params=pltpu.CompilerParams(vmem_limit_bytes=40 << 20),
    )(*args)


def exchange(pack, ab, up, dn):
    n = lax.axis_size("gx")
    m = lax.axis_size("yz")
    hop = []
    for q in range(m):
        for g in range(n):
            to = g + 1 if q % 2 == 0 else g - 1
            hop.append((g * m + q, to * m + q if 0 <= to < n else g * m + (q ^ 1)))
    is_even = lax.axis_index("yz") % 2 == 0
    one = lax.ppermute(jnp.where(is_even, up, dn), ("gx", "yz"), hop)
    two = lax.ppermute(jnp.where(is_even, dn, up), ("gx", "yz"), [(j, i) for i, j in hop])
    below = jnp.where(is_even, one, two)
    above = jnp.where(is_even, two, one)
    block = jnp.concatenate([ab, below, above], axis=1)
    return lax.all_gather(block, "yz", axis=0, tiled=True)


def body(pops_start, tile_pos, wall_mask, wall_frac, patch_id, probe):
    count = pops_start.shape[0]
    n_layers = lax.axis_size("gx")
    n_cross = lax.axis_size("yz")
    parts = n_layers * n_cross
    dims = (n_layers, n_cross)
    field = pops_start.shape
    plane = wall_frac.shape
    patch_dev = 64
    n_high = patch_dev * parts // LANES
    inverse = pltpu.SMEM((3, n_cross * count + 1), jnp.int32)

    def packs(pack):
        return [
            (count, pack.ab_rows, LANES),
            (count, pack.l_rows, LANES),
            (count, pack.l_rows, LANES),
        ]

    post0, solid, probe_kept, ab, up, dn = call(
        first_kernel,
        [field, plane, plane] + packs(PACK1),
        [
            pltpu.VMEM(field, jnp.float32),
            pltpu.VMEM(plane, jnp.int32),
            pltpu.VMEM(plane, jnp.float32),
            pltpu.SemaphoreType.DMA((3 + 2 * count,)),
        ],
        tuple(
            pltpu.with_memory_space_constraint(x, pltpu.HBM)
            for x in (pops_start, wall_mask, wall_frac, probe)
        ),
        in_hbm=range(4),
    )
    around = exchange(PACK1, ab, up, dn)
    post1, adj1, dsolid, ab, up, dn = call(
        functools.partial(second_kernel, dims),
        [field, field, plane] + packs(PACK2),
        [
            pltpu.VMEM(field, jnp.float32),
            pltpu.VMEM((count, len(AXIAL)) + plane[1:], jnp.float32),
            inverse,
        ],
        (tile_pos, post0, solid, probe_kept, around),
        in_smem=(0,),
    )
    around = exchange(PACK2, ab, up, dn)
    pops_final, adjoint_start, sums = call(
        functools.partial(third_kernel, dims),
        [field, field, (n_high, LANES)],
        [
            pltpu.VMEM(field, jnp.float32),
            pltpu.VMEM(field, jnp.float32),
            pltpu.VMEM(field, jnp.float32),
            pltpu.VMEM(plane, jnp.float32),
            inverse,
            pltpu.SemaphoreType.DMA((2,)),
        ],
        (tile_pos, post1, adj1, pops_start, wall_mask, solid, patch_id, dsolid, around),
        in_smem=(0,),
        out_hbm=(0, 1),
    )
    shares = lax.all_to_all(
        sums.reshape(parts, patch_dev), ("gx", "yz"), 0, 0, tiled=True
    )
    return (pops_final, adjoint_start, jnp.sum(shares, axis=0))


def solution(mesh):
    in_specs = (
        P(("gx", "yz"), None, None, None),
        P(),
        P(("gx", "yz"), None, None),
        P(("gx", "yz"), None, None),
        P(("gx", "yz"), None, None),
        P(("gx", "yz"), None, None),
    )
    out_specs = (
        P(("gx", "yz"), None, None, None),
        P(("gx", "yz"), None, None, None),
        P(("gx", "yz")),
    )
    return jax.shard_map(body, mesh=mesh, in_specs=in_specs, out_specs=out_specs, check_vma=False)
```

```python
import functools

import jax
import jax.numpy as jnp
import numpy as np
from jax import lax
from jax.experimental import pallas as pl
from jax.experimental.pallas import tpu as pltpu
from jax.sharding import PartitionSpec as P

TL = 16
TA = 16
TB = 32
CELLS = TA * TB
LANES = 128
COLS = CELLS // LANES
OMEGA = 1.25

VELOCITY = np.array(
    [
        [0, 0, 0],
        [1, 0, 0],
        [-1, 0, 0],
        [0, 1, 0],
        [0, -1, 0],
        [0, 0, 1],
        [0, 0, -1],
        [1, 1, 0],
        [-1, -1, 0],
        [1, -1, 0],
        [-1, 1, 0],
        [1, 0, 1],
        [-1, 0, -1],
        [1, 0, -1],
        [-1, 0, 1],
        [0, 1, 1],
        [0, -1, -1],
        [0, 1, -1],
        [0, -1, 1],
    ]
)
Q = 19
WEIGHTS = [1.0 / 3.0] + [1.0 / 18.0] * 6 + [1.0 / 36.0] * 12
PAIRS = [(2 * k + 1, 2 * k + 2) for k in range(9)]
AXIAL = [i for i in range(Q) if VELOCITY[i, 0] != 0]


def vel(i):
    return tuple(int(v) for v in VELOCITY[i])


def members_of(dim, value):
    return [i for i in range(Q) if vel(i)[dim] == value]


def face_list(stage, dim, side):
    if stage == 1:
        return [("post", i) for i in members_of(dim, side)] + [("probe", 0)]
    return [("post", i) for i in members_of(dim, side)] + [
        ("adj", i) for i in members_of(dim, -side)
    ]


class Pack:
    def __init__(self, stage):
        self.n = len(face_list(stage, 0, 1))
        self.lists = {
            (d, s): face_list(stage, d, s) for d in range(3) for s in (-1, 1)
        }
        self.fold = 2 if 2 * self.n <= TB // 2 else 1
        self.a_cols = -(-2 * self.n * TB // LANES)
        self.b_cols = COLS // self.fold
        self.a_row = 0
        self.b_row = TL * self.a_cols
        self.ab_rows = self.b_row + TL * self.b_cols
        self.l_rows = self.n * COLS
        self.up_row = self.ab_rows
        self.dn_row = self.up_row + self.l_rows
        self.rows = self.dn_row + self.l_rows

    def slot(self, dim, side, key):
        j = self.lists[(dim, side)].index(key)
        return j if dim == 0 or side < 0 else j + self.n


PACK1 = Pack(1)
PACK2 = Pack(2)


def lane_roll(x, shift):
    shift = shift % x.shape[-1]
    return x if shift == 0 else pltpu.roll(x, shift, axis=x.ndim - 1)


def row_roll(x, shift):
    shift = shift % x.shape[0]
    return x if shift == 0 else pltpu.roll(x, shift, axis=0)


def lane_iota(shape):
    return lax.broadcasted_iota(jnp.int32, shape, len(shape) - 1)


def row_iota(shape):
    return lax.broadcasted_iota(jnp.int32, shape, 0)


def combine(c, parts):
    total = None
    for v, p in zip(c, parts):
        if v == 0:
            continue
        if total is None:
            total = p if v > 0 else -p
        else:
            total = total + p if v > 0 else total - p
    return total


def flow(f):
    rho = f[0]
    momentum = [None, None, None]
    for i, j in PAIRS:
        rho = rho + (f[i] + f[j])
        diff = f[i] - f[j]
        for d, v in enumerate(vel(i)):
            if v == 0:
                continue
            if momentum[d] is None:
                momentum[d] = diff if v > 0 else -diff
            else:
                momentum[d] = momentum[d] + diff if v > 0 else momentum[d] - diff
    inv = 1.0 / rho
    u = [m * inv for m in momentum]
    square = u[0] * u[0] + u[1] * u[1] + u[2] * u[2]
    return rho, u, 1.0 - 1.5 * square


def collide(f, solid, rho, u, base):
    fluid = 1.0 - solid
    keep = (1.0 - OMEGA) * fluid
    scale = OMEGA * fluid * rho
    out = [None] * Q
    out[0] = (keep + solid) * f[0] + WEIGHTS[0] * scale * base
    for i, j in PAIRS:
        along = combine(vel(i), u)
        ws = WEIGHTS[i] * scale
        even = ws * (base + 4.5 * along * along)
        odd = ws * (3.0 * along)
        out[i] = keep * f[i] + solid * f[j] + (even + odd)
        out[j] = keep * f[j] + solid * f[i] + (even - odd)
    return out


def pullback(f, solid, rho, u, base, g):
    fluid = 1.0 - solid
    keep = (1.0 - OMEGA) * fluid
    gain = OMEGA * fluid
    lin = [None, None, None]
    total = None
    dens = None
    cross = None

    def plus(a, b):
        return b if a is None else a + b

    if g[0] is not None:
        e = WEIGHTS[0] * g[0]
        total = e
        dens = e * base
        cross = OMEGA * (g[0] * f[0])
    for i, j in PAIRS:
        if g[i] is None:
            continue
        along = combine(vel(i), u)
        w = WEIGHTS[i]
        even = w * (g[i] + g[j])
        odd = w * (g[i] - g[j])
        total = plus(total, even)
        dens = plus(dens, even * (base + 4.5 * along * along) + 3.0 * along * odd)
        push = 3.0 * odd + 9.0 * along * even
        for d, v in enumerate(vel(i)):
            if v:
                lin[d] = plus(lin[d], push if v > 0 else -push)
        cross = plus(
            cross,
            g[i] * (f[j] - (1.0 - OMEGA) * f[i]) + g[j] * (f[i] - (1.0 - OMEGA) * f[j]),
        )
    lin = [
        (-3.0 * u[d] * total if lin[d] is None else lin[d] - 3.0 * u[d] * total)
        for d in range(3)
    ]
    dsolid = cross - OMEGA * rho * dens
    shared = gain * (dens - (lin[0] * u[0] + lin[1] * u[1] + lin[2] * u[2]))
    lin = [gain * v for v in lin]
    out = [None] * Q
    out[0] = shared if g[0] is None else (keep + solid) * g[0] + shared
    for i, j in PAIRS:
        slope = combine(vel(i), lin)
        if g[i] is None:
            out[i] = shared + slope
            out[j] = shared - slope
        else:
            out[i] = keep * g[i] + solid * g[j] + (shared + slope)
            out[j] = keep * g[j] + solid * g[i] + (shared - slope)
    return out, dsolid


def face_jobs(pack, t, get, ab_ref, up_ref, dn_ref):
    lane = lane_iota((TL, LANES))

    def a_col(col):
        acc = jnp.zeros((TL, LANES), jnp.float32)
        for side in (-1, 1):
            for key in pack.lists[(1, side)]:
                j = pack.slot(1, side, key)
                if j // 4 != col:
                    continue
                to = TB * (j % 4)
                if side < 0:
                    part = lane_roll(get(key, slice(None), slice(0, LANES)), to)
                else:
                    part = lane_roll(
                        get(key, slice(None), slice(CELLS - LANES, CELLS)),
                        to - (LANES - TB),
                    )
                acc = jnp.where((lane >> 5) == j % 4, part, acc)
        ab_ref[t, pack.a_row + TL * col : pack.a_row + TL * (col + 1), :] = acc

    def b_col(col):
        acc = jnp.zeros((TL, LANES), jnp.float32)
        for half in range(pack.fold):
            src = col + half * pack.b_cols
            for side in (-1, 1):
                for key in pack.lists[(2, side)]:
                    j = pack.slot(2, side, key) + half * (TB // 2)
                    part = get(key, slice(None), slice(LANES * src, LANES * (src + 1)))
                    part = lane_roll(part, j if side < 0 else j - (TB - 1))
                    acc = jnp.where((lane & (TB - 1)) == j, part, acc)
        ab_ref[t, pack.b_row + TL * col : pack.b_row + TL * (col + 1), :] = acc

    def l_rows(side, ref, key):
        row = TL - 1 if side > 0 else 0
        j = pack.slot(0, side, key)
        for col in range(COLS):
            ref[t, j * COLS + col : j * COLS + col + 1, :] = get(
                key, slice(row, row + 1), slice(LANES * col, LANES * (col + 1))
            )

    return (
        [functools.partial(a_col, c) for c in range(pack.a_cols)]
        + [functools.partial(b_col, c) for c in range(pack.b_cols)]
        + [
            functools.partial(l_rows, side, ref, key)
            for side, ref in ((1, up_ref), (-1, dn_ref))
            for key in pack.lists[(0, side)]
        ]
    )


def weave(lists):
    jobs = [
        ((n + 0.5) / len(items), k, job)
        for k, items in enumerate(lists)
        for n, job in enumerate(items)
    ]
    for _, _, job in sorted(jobs, key=lambda job: job[:2]):
        job()


def staged(count, stages, after=None):
    for step in range(count + len(stages) - 1):
        live = [(k, step - k) for k in range(len(stages)) if 0 <= step - k < count]
        weave([stages[k](t) for k, t in live])
        if after is not None:
            for k, t in live:
                after(k, t)


def build_inverse(pos_ref, inv_ref, n_layers, group):
    layer = lax.axis_index("gx")
    for off in (-1, 0, 1):
        for w in range(group + 1):
            inv_ref[off + 1, w] = -1
        target = layer + off
        valid = (target >= 0) & (target < n_layers)
        first = jnp.clip(target, 0, n_layers - 1) * group
        for s in range(group):
            p = pos_ref[first + s]
            inv_ref[off + 1, jnp.where(valid & (p >= 0), p, group)] = s


class Neighbours:
    def __init__(self, pack, t, faces_ref, pos_ref, inv_ref, n_cross, count):
        self.pack = pack
        self.ref = faces_ref
        group = n_cross * count
        own = pos_ref[lax.axis_index("gx") * group + lax.axis_index("yz") * count + t]
        p = jnp.maximum(own, 0)
        a, b = p // count, p % count
        self.alive = own >= 0
        self.where = {}
        for d in [vel(i) for i in range(1, Q)]:
            ta, tb = a + d[1], b + d[2]
            ok = (ta >= 0) & (ta < n_cross) & (tb >= 0) & (tb < count)
            s = inv_ref[d[0] + 1, jnp.where(ok, ta * count + tb, group)]
            found = ok & (s >= 0)
            s = jnp.where(found, s, 0)
            owner, slot = s // count, s % count
            half = ((owner ^ lax.axis_index("yz")) >> 1) & 1
            block = ((owner & 1) * 2 + half) * count + slot
            self.where[d] = (block, found)
        self.planes = {}

    def a_face(self, d, side, key, fill):
        k, found = self.where[d]
        j = self.pack.slot(1, side, key)
        row = self.pack.a_row + TL * (j // 4)
        face = self.ref[k, row : row + TL, :]
        face = lane_roll(face, (LANES - TB if side > 0 else 0) - TB * (j % 4))
        return jnp.where(found, face, fill)

    def b_plane(self, d):
        if d not in self.planes:
            k, found = self.where[d]
            row = self.pack.b_row
            half = jnp.concatenate(
                [
                    self.ref[k, row + TL * c : row + TL * (c + 1), :]
                    for c in range(self.pack.b_cols)
                ],
                axis=1,
            )
            if self.pack.fold == 2:
                half = jnp.concatenate([half, lane_roll(half, -(TB // 2))], axis=1)
            self.planes[d] = half
        return self.planes[d], self.where[d][1]

    def l_row(self, d, side, key, fill):
        k, found = self.where[d]
        first = self.pack.up_row if side > 0 else self.pack.dn_row
        first = first + self.pack.slot(0, side, key) * COLS
        row = jnp.concatenate(
            [self.ref[k, first + c : first + c + 1, :] for c in range(COLS)], axis=1
        )
        return jnp.where(found, row, fill)

    def stream(self, own, c, key, fill):
        cl, ca, cb = c
        shape = (TL, CELLS)
        lane = lane_iota(shape)
        edge_b = (lane & (TB - 1)) == (TB - 1 if cb > 0 else 0)
        edge_a = (lane >> 5) == (TA - 1 if ca > 0 else 0)
        x = own
        if ca:
            face = self.a_face((0, -ca, 0), ca, key, fill)
            part = slice(CELLS - LANES, CELLS) if ca > 0 else slice(0, LANES)
            inner = lane_iota((TL, LANES))
            hit = inner >= LANES - TB if ca > 0 else inner < TB
            face = jnp.where(hit, face, x[:, part])
            x = jnp.concatenate(
                [x[:, : CELLS - LANES], face] if ca > 0 else [face, x[:, LANES:]], axis=1
            )
        if cb:
            j = self.pack.slot(2, cb, key)
            shift = -1 - j if cb > 0 else TB - j
            plane, found = self.b_plane((0, 0, -cb))
            plane = jnp.where(found, plane, fill)
            if ca:
                corner, found = self.b_plane((0, -ca, -cb))
                part = slice(CELLS - LANES, CELLS) if ca > 0 else slice(0, LANES)
                corner = jnp.where(found, corner[:, part], fill)
                corner = jnp.where(hit, corner, plane[:, part])
                plane = jnp.concatenate(
                    [plane[:, : CELLS - LANES], corner] if ca > 0 else [corner, plane[:, LANES:]],
                    axis=1,
                )
            face = lane_roll(plane, shift)
            x = jnp.where(edge_b, face, x)
        if cl:
            row = self.l_row((-cl, 0, 0), cl, key, fill)
            lane_r = lane_iota((1, CELLS))
            if ca:
                corner = self.l_row((-cl, -ca, 0), cl, key, fill)
                row = jnp.where((lane_r >> 5) == (TA - 1 if ca > 0 else 0), corner, row)
            if cb:
                corner = self.l_row((-cl, 0, -cb), cl, key, fill)
                corner = lane_roll(corner, -TB if cb > 0 else TB)
                row = jnp.where((lane_r & (TB - 1)) == (TB - 1 if cb > 0 else 0), corner, row)
            half = (TL // 2, CELLS)
            if cl > 0:
                low, edge = x[: TL // 2], x[TL // 2 :]
            else:
                edge, low = x[: TL // 2], x[TL // 2 :]
            hit = row_iota(half) == (TL // 2 - 1 if cl > 0 else 0)
            edge = jnp.where(hit, jnp.broadcast_to(row, half), edge)
            x = jnp.concatenate([low, edge] if cl > 0 else [edge, low], axis=0)
        return row_roll(lane_roll(x, TB * ca + cb), cl)


def first_kernel(pops_in, mask_in, frac_in, probe_in, post, solid, probe, ab, up, dn, pops, mask, frac, sems):
    count = pops.shape[0]
    small = [
        pltpu.make_async_copy(src, dst, sems.at[n])
        for n, (src, dst) in enumerate(((mask_in, mask), (frac_in, frac), (probe_in, probe)))
    ]
    halves = [(t, r) for t in range(count) for r in range(2)]
    large = [
        pltpu.make_async_copy(
            pops_in.at[t, :, pl.ds(8 * r, 8), :],
            pops.at[t, :, pl.ds(8 * r, 8), :],
            sems.at[len(small) + n],
        )
        for n, (t, r) in enumerate(halves)
    ]
    for copy in small[:2] + large + small[2:]:
        copy.start()
    for copy in small[:2]:
        copy.wait()
    solid[...] = mask[...].astype(jnp.float32) * frac[...]

    def collides(t):
        def run(r, c):
            if c == 0:
                large[halves.index((t, r))].wait()
            rows = slice(8 * r, 8 * r + 8)
            lanes = slice(LANES * c, LANES * (c + 1))
            f = [pops[t, i, rows, lanes] for i in range(Q)]
            out = collide(f, solid[t, rows, lanes], *flow(f))
            for i in range(Q):
                post[t, i, rows, lanes] = out[i]

        return [functools.partial(run, r, c) for r in range(2) for c in range(COLS)]

    def faces(t):
        def get(key, rows, lanes):
            if key[0] == "probe":
                return probe[t, rows, lanes]
            return post[t, key[1], rows, lanes]

        return face_jobs(PACK1, t, get, ab, up, dn)

    small[2].wait()
    staged(count, [collides, faces])


def second_kernel(
    dims, pos, post0, solid_in, probe, around, post1, adj1, dsolid, ab, up, dn, state, pulled, inv
):
    n_layers, n_cross = dims
    count = post0.shape[0]
    build_inverse(pos, inv, n_layers, n_cross * count)

    def moves(t):
        near = Neighbours(PACK1, t, around, pos, inv, n_cross, count)

        def forward(i):
            state[t, i] = near.stream(post0[t, i], vel(i), ("post", i), WEIGHTS[i])

        def backward(n, i):
            back = tuple(-v for v in vel(i))
            moved = near.stream(probe[t], back, ("probe", 0), 0.0)
            pulled[t, n] = moved if vel(i)[0] > 0 else -moved

        return [functools.partial(forward, i) for i in range(Q)] + [
            functools.partial(backward, n, i) for n, i in enumerate(AXIAL)
        ]

    def runs(t):
        def run(r, c):
            rows = slice(8 * r, 8 * r + 8)
            lanes = slice(LANES * c, LANES * (c + 1))
            f = [state[t, i, rows, lanes] for i in range(Q)]
            solid = solid_in[t, rows, lanes]
            rho, u, base = flow(f)
            out = collide(f, solid, rho, u, base)
            for i in range(Q):
                post1[t, i, rows, lanes] = out[i]
            g = [None] * Q
            for n, i in enumerate(AXIAL):
                g[i] = pulled[t, n, rows, lanes]
            back, ds = pullback(f, solid, rho, u, base, g)
            for i in range(Q):
                adj1[t, i, rows, lanes] = back[i]
            dsolid[t, rows, lanes] = ds

        return [functools.partial(run, r, c) for r in range(2) for c in range(COLS)]

    def faces(t):
        def get(key, rows, lanes):
            return (post1 if key[0] == "post" else adj1)[t, key[1], rows, lanes]

        return face_jobs(PACK2, t, get, ab, up, dn)

    staged(count, [moves, runs, faces])


def third_kernel(
    dims, pos, post1, adj1, pops, mask, solid_in, patch, dsolid, around, final_out, start_out, sums, final, start, pulled, weighted, inv, sems
):
    n_layers, n_cross = dims
    count = pops.shape[0]
    group = n_cross * count
    build_inverse(pos, inv, n_layers, group)

    base_slot = lax.axis_index("gx") * group + lax.axis_index("yz") * count
    n_high = sums.shape[0]
    high_iota = lax.broadcasted_iota(jnp.int32, (n_high, CELLS), 0)
    low_iota = lax.broadcasted_iota(jnp.int32, (LANES, CELLS), 0)
    total = [jnp.zeros((3 * n_high, LANES), jnp.float32)]

    def moves(t):
        near = Neighbours(PACK2, t, around, pos, inv, n_cross, count)

        def forward(i):
            moved = near.stream(post1[t, i], vel(i), ("post", i), WEIGHTS[i])
            final[t, i] = jnp.where(near.alive, moved, 0.0)

        def backward(i):
            back = tuple(-v for v in vel(i))
            pulled[t, i] = near.stream(adj1[t, i], back, ("adj", i), 0.0)

        order = [functools.partial(backward, i) for i in range(Q)]
        return order + [functools.partial(forward, i) for i in range(Q)]

    def runs(t):
        alive = pos[base_slot + t] >= 0

        def run(r, c):
            rows = slice(8 * r, 8 * r + 8)
            lanes = slice(LANES * c, LANES * (c + 1))
            f = [pops[t, i, rows, lanes] for i in range(Q)]
            g = [pulled[t, i, rows, lanes] for i in range(Q)]
            wall = mask[t, rows, lanes].astype(jnp.float32)
            solid = solid_in[t, rows, lanes]
            rho, u, base = flow(f)
            back, ds = pullback(f, solid, rho, u, base, g)
            for i in range(Q):
                start[t, i, rows, lanes] = jnp.where(alive, back[i], 0.0)
            part = wall * (ds + dsolid[t, rows, lanes])
            weighted[t, rows, lanes] = jnp.where(alive, part, 0.0)

        return [functools.partial(run, r, c) for r in range(2) for c in range(COLS)]

    def add(t, r):
        ids = patch[t, r : r + 1, :]
        w = weighted[t, r : r + 1, :]
        w1 = w.astype(jnp.bfloat16).astype(jnp.float32)
        w2 = (w - w1).astype(jnp.bfloat16).astype(jnp.float32)
        w3 = w - w1 - w2
        high = high_iota == (ids >> 7)
        left = jnp.concatenate(
            [jnp.where(high, part, 0.0).astype(jnp.bfloat16) for part in (w1, w2, w3)],
            axis=0,
        )
        right = jnp.where(low_iota == (ids & (LANES - 1)), 1.0, 0.0).astype(jnp.bfloat16)
        total[0] = total[0] + lax.dot_general(
            left, right, (((1,), (1,)), ((), ())), preferred_element_type=jnp.float32
        )

    def adds(t):
        return [functools.partial(add, t, r) for r in range(TL)]

    copies = []

    def send(k, t):
        if k < 2:
            src, dst = ((final, final_out), (start, start_out))[k]
            copies.append(pltpu.make_async_copy(src.at[t], dst.at[t], sems.at[len(copies)]))
            copies[-1].start()

    staged(count, [moves, runs, adds], send)
    for copy in copies:
        copy.wait()
    acc = total[0]
    sums[...] = acc[:n_high] + acc[n_high : 2 * n_high] + acc[2 * n_high :]


def call(kernel, outs, scratch, args, in_smem=(), in_hbm=(), out_hbm=()):
    vmem = pl.BlockSpec(memory_space=pltpu.VMEM)
    hbm = pl.BlockSpec(memory_space=pltpu.HBM)
    smem = pl.BlockSpec(memory_space=pltpu.SMEM)
    return pl.pallas_call(
        kernel,
        out_shape=[jax.ShapeDtypeStruct(s, jnp.float32) for s in outs],
        in_specs=[
            smem if n in in_smem else hbm if n in in_hbm else vmem for n in range(len(args))
        ],
        out_specs=[hbm if n in out_hbm else vmem for n in range(len(outs))],
        scratch_shapes=scratch,
        compiler_params=pltpu.CompilerParams(vmem_limit_bytes=40 << 20),
    )(*args)


def exchange(ab, up, dn):
    n = lax.axis_size("gx")
    m = lax.axis_size("yz")
    assert m == 4
    hop = []
    for q in range(m):
        for g in range(n):
            to = g + 1 if q % 2 == 0 else g - 1
            hop.append((g * m + q, to * m + q if 0 <= to < n else g * m + (q ^ 1)))
    is_even = lax.axis_index("yz") % 2 == 0
    one = lax.ppermute(jnp.where(is_even, up, dn), ("gx", "yz"), hop)
    two = lax.ppermute(jnp.where(is_even, dn, up), ("gx", "yz"), [(j, i) for i, j in hop])
    across = [(q, q ^ 2) for q in range(m)]
    ab_far = lax.ppermute(ab, "yz", across)
    l_near = jnp.concatenate(
        [jnp.where(is_even, one, two), jnp.where(is_even, two, one)], axis=1
    )
    l_far = lax.ppermute(l_near, "yz", across)
    both = jnp.concatenate(
        [jnp.concatenate([ab, l_near], axis=1), jnp.concatenate([ab_far, l_far], axis=1)],
        axis=0,
    )
    pairs = [[0, 1], [2, 3]]
    return lax.all_gather(both, "yz", axis=0, tiled=True, axis_index_groups=pairs)


def body(pops_start, tile_pos, wall_mask, wall_frac, patch_id, probe):
    count = pops_start.shape[0]
    n_layers = lax.axis_size("gx")
    n_cross = lax.axis_size("yz")
    parts = n_layers * n_cross
    dims = (n_layers, n_cross)
    field = pops_start.shape
    plane = wall_frac.shape
    patch_dev = 64
    n_high = patch_dev * parts // LANES
    inverse = pltpu.SMEM((3, n_cross * count + 1), jnp.int32)

    def packs(pack):
        return [
            (count, pack.ab_rows, LANES),
            (count, pack.l_rows, LANES),
            (count, pack.l_rows, LANES),
        ]

    post0, solid, probe_kept, ab, up, dn = call(
        first_kernel,
        [field, plane, plane] + packs(PACK1),
        [
            pltpu.VMEM(field, jnp.float32),
            pltpu.VMEM(plane, jnp.int32),
            pltpu.VMEM(plane, jnp.float32),
            pltpu.SemaphoreType.DMA((3 + 2 * count,)),
        ],
        tuple(
            pltpu.with_memory_space_constraint(x, pltpu.HBM)
            for x in (pops_start, wall_mask, wall_frac, probe)
        ),
        in_hbm=range(4),
    )
    around = exchange(ab, up, dn)
    post1, adj1, dsolid, ab, up, dn = call(
        functools.partial(second_kernel, dims),
        [field, field, plane] + packs(PACK2),
        [
            pltpu.VMEM(field, jnp.float32),
            pltpu.VMEM((count, len(AXIAL)) + plane[1:], jnp.float32),
            inverse,
        ],
        (tile_pos, post0, solid, probe_kept, around),
        in_smem=(0,),
    )
    around = exchange(ab, up, dn)
    pops_final, adjoint_start, sums = call(
        functools.partial(third_kernel, dims),
        [field, field, (n_high, LANES)],
        [
            pltpu.VMEM(field, jnp.float32),
            pltpu.VMEM(field, jnp.float32),
            pltpu.VMEM(field, jnp.float32),
            pltpu.VMEM(plane, jnp.float32),
            inverse,
            pltpu.SemaphoreType.DMA((2 * count,)),
        ],
        (tile_pos, post1, adj1, pops_start, wall_mask, solid, patch_id, dsolid, around),
        in_smem=(0,),
        out_hbm=(0, 1),
    )
    shares = lax.all_to_all(
        sums.reshape(parts, patch_dev), ("gx", "yz"), 0, 0, tiled=True
    )
    return (pops_final, adjoint_start, jnp.sum(shares, axis=0))


def solution(mesh):
    in_specs = (
        P(("gx", "yz"), None, None, None),
        P(),
        P(("gx", "yz"), None, None),
        P(("gx", "yz"), None, None),
        P(("gx", "yz"), None, None),
        P(("gx", "yz"), None, None),
    )
    out_specs = (
        P(("gx", "yz"), None, None, None),
        P(("gx", "yz"), None, None, None),
        P(("gx", "yz")),
    )
    return jax.shard_map(body, mesh=mesh, in_specs=in_specs, out_specs=out_specs, check_vma=False)
```

```python
import functools

import jax
import jax.numpy as jnp
import numpy as np
from jax import lax
from jax.experimental import pallas as pl
from jax.experimental.pallas import tpu as pltpu
from jax.sharding import PartitionSpec as P

TL = 16
TA = 16
TB = 32
CELLS = TA * TB
LANES = 128
COLS = CELLS // LANES
OMEGA = 1.25

VELOCITY = np.array(
    [
        [0, 0, 0],
        [1, 0, 0],
        [-1, 0, 0],
        [0, 1, 0],
        [0, -1, 0],
        [0, 0, 1],
        [0, 0, -1],
        [1, 1, 0],
        [-1, -1, 0],
        [1, -1, 0],
        [-1, 1, 0],
        [1, 0, 1],
        [-1, 0, -1],
        [1, 0, -1],
        [-1, 0, 1],
        [0, 1, 1],
        [0, -1, -1],
        [0, 1, -1],
        [0, -1, 1],
    ]
)
Q = 19
WEIGHTS = [1.0 / 3.0] + [1.0 / 18.0] * 6 + [1.0 / 36.0] * 12
PAIRS = [(2 * k + 1, 2 * k + 2) for k in range(9)]
AXIAL = [i for i in range(Q) if VELOCITY[i, 0] != 0]


def vel(i):
    return tuple(int(v) for v in VELOCITY[i])


def members_of(dim, value):
    return [i for i in range(Q) if vel(i)[dim] == value]


def face_list(stage, dim, side):
    if stage == 1:
        return [("post", i) for i in members_of(dim, side)] + [("probe", 0)]
    return [("post", i) for i in members_of(dim, side)] + [
        ("adj", i) for i in members_of(dim, -side)
    ]


class Pack:
    def __init__(self, stage):
        self.n = len(face_list(stage, 0, 1))
        self.lists = {
            (d, s): face_list(stage, d, s) for d in range(3) for s in (-1, 1)
        }
        self.fold = 2 if 2 * self.n <= TB // 2 else 1
        self.a_cols = -(-2 * self.n * TB // LANES)
        self.b_cols = COLS // self.fold
        self.a_row = 0
        self.b_row = TL * self.a_cols
        self.ab_rows = self.b_row + TL * self.b_cols
        self.l_rows = self.n * COLS
        self.up_row = self.ab_rows
        self.dn_row = self.up_row + self.l_rows
        self.rows = self.dn_row + self.l_rows

    def slot(self, dim, side, key):
        j = self.lists[(dim, side)].index(key)
        return j if dim == 0 or side < 0 else j + self.n


PACK1 = Pack(1)
PACK2 = Pack(2)


def lane_roll(x, shift):
    shift = shift % x.shape[-1]
    return x if shift == 0 else pltpu.roll(x, shift, axis=x.ndim - 1)


def row_roll(x, shift):
    shift = shift % x.shape[0]
    return x if shift == 0 else pltpu.roll(x, shift, axis=0)


def lane_iota(shape):
    return lax.broadcasted_iota(jnp.int32, shape, len(shape) - 1)


def row_iota(shape):
    return lax.broadcasted_iota(jnp.int32, shape, 0)


def combine(c, parts):
    total = None
    for v, p in zip(c, parts):
        if v == 0:
            continue
        if total is None:
            total = p if v > 0 else -p
        else:
            total = total + p if v > 0 else total - p
    return total


def flow(f):
    rho = f[0]
    momentum = [None, None, None]
    for i, j in PAIRS:
        rho = rho + (f[i] + f[j])
        diff = f[i] - f[j]
        for d, v in enumerate(vel(i)):
            if v == 0:
                continue
            if momentum[d] is None:
                momentum[d] = diff if v > 0 else -diff
            else:
                momentum[d] = momentum[d] + diff if v > 0 else momentum[d] - diff
    inv = 1.0 / rho
    u = [m * inv for m in momentum]
    square = u[0] * u[0] + u[1] * u[1] + u[2] * u[2]
    return rho, u, 1.0 - 1.5 * square


def collide(f, solid, rho, u, base):
    fluid = 1.0 - solid
    keep = (1.0 - OMEGA) * fluid
    scale = OMEGA * fluid * rho
    out = [None] * Q
    out[0] = (keep + solid) * f[0] + WEIGHTS[0] * scale * base
    for i, j in PAIRS:
        along = combine(vel(i), u)
        ws = WEIGHTS[i] * scale
        even = ws * (base + 4.5 * along * along)
        odd = ws * (3.0 * along)
        out[i] = keep * f[i] + solid * f[j] + (even + odd)
        out[j] = keep * f[j] + solid * f[i] + (even - odd)
    return out


def pullback(f, solid, rho, u, base, g):
    fluid = 1.0 - solid
    keep = (1.0 - OMEGA) * fluid
    gain = OMEGA * fluid
    lin = [None, None, None]
    total = None
    dens = None
    cross = None

    def plus(a, b):
        return b if a is None else a + b

    if g[0] is not None:
        e = WEIGHTS[0] * g[0]
        total = e
        dens = e * base
        cross = OMEGA * (g[0] * f[0])
    for i, j in PAIRS:
        if g[i] is None:
            continue
        along = combine(vel(i), u)
        w = WEIGHTS[i]
        even = w * (g[i] + g[j])
        odd = w * (g[i] - g[j])
        total = plus(total, even)
        dens = plus(dens, even * (base + 4.5 * along * along) + 3.0 * along * odd)
        push = 3.0 * odd + 9.0 * along * even
        for d, v in enumerate(vel(i)):
            if v:
                lin[d] = plus(lin[d], push if v > 0 else -push)
        cross = plus(
            cross,
            g[i] * (f[j] - (1.0 - OMEGA) * f[i]) + g[j] * (f[i] - (1.0 - OMEGA) * f[j]),
        )
    lin = [
        (-3.0 * u[d] * total if lin[d] is None else lin[d] - 3.0 * u[d] * total)
        for d in range(3)
    ]
    dsolid = cross - OMEGA * rho * dens
    shared = gain * (dens - (lin[0] * u[0] + lin[1] * u[1] + lin[2] * u[2]))
    lin = [gain * v for v in lin]
    out = [None] * Q
    out[0] = shared if g[0] is None else (keep + solid) * g[0] + shared
    for i, j in PAIRS:
        slope = combine(vel(i), lin)
        if g[i] is None:
            out[i] = shared + slope
            out[j] = shared - slope
        else:
            out[i] = keep * g[i] + solid * g[j] + (shared + slope)
            out[j] = keep * g[j] + solid * g[i] + (shared - slope)
    return out, dsolid


def side_jobs(pack, t, get, ab_ref):
    lane = lane_iota((TL, LANES))

    def a_col(col):
        acc = jnp.zeros((TL, LANES), jnp.float32)
        for side in (-1, 1):
            for key in pack.lists[(1, side)]:
                j = pack.slot(1, side, key)
                if j // 4 != col:
                    continue
                to = TB * (j % 4)
                if side < 0:
                    part = lane_roll(get(key, slice(None), slice(0, LANES)), to)
                else:
                    part = lane_roll(
                        get(key, slice(None), slice(CELLS - LANES, CELLS)),
                        to - (LANES - TB),
                    )
                acc = jnp.where((lane >> 5) == j % 4, part, acc)
        ab_ref[t, pack.a_row + TL * col : pack.a_row + TL * (col + 1), :] = acc

    def b_col(col):
        acc = jnp.zeros((TL, LANES), jnp.float32)
        for half in range(pack.fold):
            src = col + half * pack.b_cols
            for side in (-1, 1):
                for key in pack.lists[(2, side)]:
                    j = pack.slot(2, side, key) + half * (TB // 2)
                    part = get(key, slice(None), slice(LANES * src, LANES * (src + 1)))
                    part = lane_roll(part, j if side < 0 else j - (TB - 1))
                    acc = jnp.where((lane & (TB - 1)) == j, part, acc)
        ab_ref[t, pack.b_row + TL * col : pack.b_row + TL * (col + 1), :] = acc

    return [functools.partial(a_col, c) for c in range(pack.a_cols)] + [
        functools.partial(b_col, c) for c in range(pack.b_cols)
    ]


def end_jobs(pack, t, get, up_ref, dn_ref):
    def l_rows(side, ref, key):
        row = TL - 1 if side > 0 else 0
        j = pack.slot(0, side, key)
        for col in range(COLS):
            ref[t, j * COLS + col : j * COLS + col + 1, :] = get(
                key, slice(row, row + 1), slice(LANES * col, LANES * (col + 1))
            )

    return [
        functools.partial(l_rows, side, ref, key)
        for side, ref in ((1, up_ref), (-1, dn_ref))
        for key in pack.lists[(0, side)]
    ]


def first_sides(post, probe, ab):
    def sides(t):
        def get(key, rows, lanes):
            if key[0] == "probe":
                return probe[t, rows, lanes]
            return post[t, key[1], rows, lanes]

        return side_jobs(PACK1, t, get, ab)

    staged(post.shape[0], [sides])


def second_sides(post1, adj1, ab):
    def sides(t):
        def get(key, rows, lanes):
            return (post1 if key[0] == "post" else adj1)[t, key[1], rows, lanes]

        return side_jobs(PACK2, t, get, ab)

    staged(post1.shape[0], [sides])


def weave(lists):
    jobs = [
        ((n + 0.5) / len(items), k, job)
        for k, items in enumerate(lists)
        for n, job in enumerate(items)
    ]
    for _, _, job in sorted(jobs, key=lambda job: job[:2]):
        job()


def staged(count, stages, after=None):
    for step in range(count + len(stages) - 1):
        live = [(k, step - k) for k in range(len(stages)) if 0 <= step - k < count]
        weave([stages[k](t) for k, t in live])
        if after is not None:
            for k, t in live:
                after(k, t)


def build_inverse(pos_ref, inv_ref, n_layers, group):
    layer = lax.axis_index("gx")
    for off in (-1, 0, 1):
        for w in range(group + 1):
            inv_ref[off + 1, w] = -1
        target = layer + off
        valid = (target >= 0) & (target < n_layers)
        first = jnp.clip(target, 0, n_layers - 1) * group
        for s in range(group):
            p = pos_ref[first + s]
            inv_ref[off + 1, jnp.where(valid & (p >= 0), p, group)] = s


class Neighbours:
    def __init__(self, pack, t, faces_ref, pos_ref, inv_ref, n_cross, count):
        self.pack = pack
        self.ref = faces_ref
        group = n_cross * count
        own = pos_ref[lax.axis_index("gx") * group + lax.axis_index("yz") * count + t]
        p = jnp.maximum(own, 0)
        a, b = p // count, p % count
        self.alive = own >= 0
        self.where = {}
        for d in [vel(i) for i in range(1, Q)]:
            ta, tb = a + d[1], b + d[2]
            ok = (ta >= 0) & (ta < n_cross) & (tb >= 0) & (tb < count)
            s = inv_ref[d[0] + 1, jnp.where(ok, ta * count + tb, group)]
            found = ok & (s >= 0)
            s = jnp.where(found, s, 0)
            owner, slot = s // count, s % count
            half = ((owner ^ lax.axis_index("yz")) >> 1) & 1
            block = ((owner & 1) * 2 + half) * count + slot
            self.where[d] = (block, found)
        self.planes = {}

    def a_face(self, d, side, key, fill, to):
        k, found = self.where[d]
        j = self.pack.slot(1, side, key)
        row = self.pack.a_row + TL * (j // 4)
        face = self.ref[k, row : row + TL, :]
        face = lane_roll(face, to - TB * (j % 4))
        return jnp.where(found, face, fill)

    def b_plane(self, d):
        if d not in self.planes:
            k, found = self.where[d]
            row = self.pack.b_row
            half = jnp.concatenate(
                [
                    self.ref[k, row + TL * c : row + TL * (c + 1), :]
                    for c in range(self.pack.b_cols)
                ],
                axis=1,
            )
            if self.pack.fold == 2:
                half = jnp.concatenate([half, lane_roll(half, -(TB // 2))], axis=1)
            self.planes[d] = half
        return self.planes[d], self.where[d][1]

    def l_row(self, d, side, key, fill):
        k, found = self.where[d]
        first = self.pack.up_row if side > 0 else self.pack.dn_row
        first = first + self.pack.slot(0, side, key) * COLS
        row = jnp.concatenate(
            [self.ref[k, first + c : first + c + 1, :] for c in range(COLS)], axis=1
        )
        return jnp.where(found, row, fill)

    def enter(self, x, c, key, fill):
        cl, ca, cb = c
        shape = (TL, CELLS)
        if ca:
            to = 0 if ca > 0 else LANES - TB
            face = row_roll(self.a_face((0, -ca, 0), ca, key, fill, to + cb), cl)
            inner = lane_iota((TL, LANES))
            hit = inner < TB if ca > 0 else inner >= LANES - TB
            part = slice(0, LANES) if ca > 0 else slice(CELLS - LANES, CELLS)
            face = jnp.where(hit, face, x[:, part])
            x = jnp.concatenate(
                [face, x[:, LANES:]] if ca > 0 else [x[:, : CELLS - LANES], face], axis=1
            )
        if cb:
            plane, found = self.b_plane((0, 0, -cb))
            plane = jnp.where(found, plane, fill)
            if ca:
                corner, found = self.b_plane((0, -ca, -cb))
                part = slice(CELLS - LANES, CELLS) if ca > 0 else slice(0, LANES)
                inner = lane_iota((TL, LANES))
                hit = inner >= LANES - TB if ca > 0 else inner < TB
                corner = jnp.where(found, corner[:, part], fill)
                corner = jnp.where(hit, corner, plane[:, part])
                plane = jnp.concatenate(
                    [plane[:, : CELLS - LANES], corner] if ca > 0 else [corner, plane[:, LANES:]],
                    axis=1,
                )
            at = 0 if cb > 0 else TB - 1
            face = lane_roll(plane, TB * ca + at - self.pack.slot(2, cb, key))
            x = jnp.where((lane_iota(shape) & (TB - 1)) == at, row_roll(face, cl), x)
        if cl:
            row = self.l_row((-cl, 0, 0), cl, key, fill)
            lane = lane_iota((1, CELLS))
            if ca:
                corner = self.l_row((-cl, -ca, 0), cl, key, fill)
                row = jnp.where((lane >> 5) == (TA - 1 if ca > 0 else 0), corner, row)
            row = lane_roll(row, TB * ca + cb)
            if cb:
                corner = self.l_row((-cl, 0, -cb), cl, key, fill)
                corner = lane_roll(corner, -cb * (TB - 1))
                row = jnp.where((lane & (TB - 1)) == (0 if cb > 0 else TB - 1), corner, row)
            half = (TL // 2, CELLS)
            low, high = x[: TL // 2], x[TL // 2 :]
            row = jnp.broadcast_to(row, half)
            if cl > 0:
                low = jnp.where(row_iota(half) == 0, row, low)
            else:
                high = jnp.where(row_iota(half) == TL // 2 - 1, row, high)
            x = jnp.concatenate([low, high], axis=0)
        return x


def shifted(x, c):
    return row_roll(lane_roll(x, TB * c[1] + c[2]), c[0])


def against(i):
    return tuple(-v for v in vel(i))


def first_own(post, probe, after, moved, back):
    del after
    for t in range(post.shape[0]):
        for i in range(Q):
            moved[t, i] = shifted(post[t, i], vel(i))
        for n, i in enumerate(AXIAL):
            back[t, n] = shifted(probe[t], against(i))


def second_own(post1, adj1, patch, after, moved, back, onehot):
    del after
    low_iota = lax.broadcasted_iota(jnp.int32, (LANES, CELLS), 0)
    for t in range(post1.shape[0]):
        for i in range(Q):
            moved[t, i] = shifted(post1[t, i], vel(i))
            back[t, i] = shifted(adj1[t, i], against(i))
            if i < TL:
                low = patch[t, i : i + 1, :] & (LANES - 1)
                onehot[t, i] = jnp.where(low_iota == low, 1.0, 0.0).astype(jnp.bfloat16)


def first_kernel(pops_in, mask_in, frac_in, probe_in, post, solid, probe, up, dn, pops, mask, frac, sems):
    count = pops.shape[0]
    small = [
        pltpu.make_async_copy(src, dst, sems.at[n])
        for n, (src, dst) in enumerate(((mask_in, mask), (frac_in, frac), (probe_in, probe)))
    ]
    halves = [(t, r) for t in range(count) for r in range(2)]
    large = [
        pltpu.make_async_copy(
            pops_in.at[t, :, pl.ds(8 * r, 8), :],
            pops.at[t, :, pl.ds(8 * r, 8), :],
            sems.at[len(small) + n],
        )
        for n, (t, r) in enumerate(halves)
    ]
    for copy in small[:2] + large + small[2:]:
        copy.start()
    for copy in small[:2]:
        copy.wait()
    solid[...] = mask[...].astype(jnp.float32) * frac[...]

    def collides(t):
        def run(r, c):
            if c == 0:
                large[halves.index((t, r))].wait()
            rows = slice(8 * r, 8 * r + 8)
            lanes = slice(LANES * c, LANES * (c + 1))
            f = [pops[t, i, rows, lanes] for i in range(Q)]
            out = collide(f, solid[t, rows, lanes], *flow(f))
            for i in range(Q):
                post[t, i, rows, lanes] = out[i]

        return [functools.partial(run, r, c) for r in range(2) for c in range(COLS)]

    def faces(t):
        def get(key, rows, lanes):
            if key[0] == "probe":
                return probe[t, rows, lanes]
            return post[t, key[1], rows, lanes]

        return end_jobs(PACK1, t, get, up, dn)

    small[2].wait()
    staged(count, [collides, faces])


def second_kernel(
    dims, pos, moved, back, solid_in, around, post1, adj1, dsolid, up, dn, state, pulled, inv
):
    n_layers, n_cross = dims
    count = solid_in.shape[0]
    build_inverse(pos, inv, n_layers, n_cross * count)

    def moves(t):
        near = Neighbours(PACK1, t, around, pos, inv, n_cross, count)

        def forward(i):
            state[t, i] = near.enter(moved[t, i], vel(i), ("post", i), WEIGHTS[i])

        def backward(n, i):
            x = near.enter(back[t, n], against(i), ("probe", 0), 0.0)
            pulled[t, n] = x if vel(i)[0] > 0 else -x

        return [functools.partial(forward, i) for i in range(Q)] + [
            functools.partial(backward, n, i) for n, i in enumerate(AXIAL)
        ]

    def runs(t):
        def run(r, c):
            rows = slice(8 * r, 8 * r + 8)
            lanes = slice(LANES * c, LANES * (c + 1))
            f = [state[t, i, rows, lanes] for i in range(Q)]
            solid = solid_in[t, rows, lanes]
            rho, u, base = flow(f)
            out = collide(f, solid, rho, u, base)
            for i in range(Q):
                post1[t, i, rows, lanes] = out[i]
            g = [None] * Q
            for n, i in enumerate(AXIAL):
                g[i] = pulled[t, n, rows, lanes]
            df, ds = pullback(f, solid, rho, u, base, g)
            for i in range(Q):
                adj1[t, i, rows, lanes] = df[i]
            dsolid[t, rows, lanes] = ds

        return [functools.partial(run, r, c) for r in range(2) for c in range(COLS)]

    def faces(t):
        def get(key, rows, lanes):
            return (post1 if key[0] == "post" else adj1)[t, key[1], rows, lanes]

        return end_jobs(PACK2, t, get, up, dn)

    staged(count, [moves, runs, faces])


def third_kernel(
    dims, pos, moved, back, onehot, pops, mask, solid_in, patch, dsolid, around, final_out, start_out, sums, final, start, pulled, weighted, inv, sems
):
    n_layers, n_cross = dims
    count = pops.shape[0]
    group = n_cross * count
    build_inverse(pos, inv, n_layers, group)

    base_slot = lax.axis_index("gx") * group + lax.axis_index("yz") * count
    n_high = sums.shape[0]
    high_iota = lax.broadcasted_iota(jnp.int32, (n_high, CELLS), 0)
    total = [jnp.zeros((3 * n_high, LANES), jnp.float32)]

    def moves(t):
        near = Neighbours(PACK2, t, around, pos, inv, n_cross, count)

        def forward(i):
            x = near.enter(moved[t, i], vel(i), ("post", i), WEIGHTS[i])
            final[t, i] = jnp.where(near.alive, x, 0.0)

        def backward(i):
            pulled[t, i] = near.enter(back[t, i], against(i), ("adj", i), 0.0)

        order = [functools.partial(backward, i) for i in range(Q)]
        return order + [functools.partial(forward, i) for i in range(Q)]

    def runs(t):
        alive = pos[base_slot + t] >= 0

        def run(r, c):
            rows = slice(8 * r, 8 * r + 8)
            lanes = slice(LANES * c, LANES * (c + 1))
            f = [pops[t, i, rows, lanes] for i in range(Q)]
            g = [pulled[t, i, rows, lanes] for i in range(Q)]
            wall = mask[t, rows, lanes].astype(jnp.float32)
            solid = solid_in[t, rows, lanes]
            rho, u, base = flow(f)
            df, ds = pullback(f, solid, rho, u, base, g)
            for i in range(Q):
                start[t, i, rows, lanes] = jnp.where(alive, df[i], 0.0)
            part = wall * (ds + dsolid[t, rows, lanes])
            weighted[t, rows, lanes] = jnp.where(alive, part, 0.0)

        return [functools.partial(run, r, c) for r in range(2) for c in range(COLS)]

    def add(t, r):
        ids = patch[t, r : r + 1, :]
        w = weighted[t, r : r + 1, :]
        w1 = w.astype(jnp.bfloat16).astype(jnp.float32)
        w2 = (w - w1).astype(jnp.bfloat16).astype(jnp.float32)
        w3 = w - w1 - w2
        high = high_iota == (ids >> 7)
        left = jnp.concatenate(
            [jnp.where(high, part, 0.0).astype(jnp.bfloat16) for part in (w1, w2, w3)],
            axis=0,
        )
        total[0] = total[0] + lax.dot_general(
            left, onehot[t, r], (((1,), (1,)), ((), ())), preferred_element_type=jnp.float32
        )

    def adds(t):
        return [functools.partial(add, t, r) for r in range(TL)]

    copies = []

    def send(k, t):
        if k < 2:
            src, dst = ((final, final_out), (start, start_out))[k]
            copies.append(pltpu.make_async_copy(src.at[t], dst.at[t], sems.at[len(copies)]))
            copies[-1].start()

    staged(count, [moves, runs, adds], send)
    for copy in copies:
        copy.wait()
    acc = total[0]
    sums[...] = acc[:n_high] + acc[n_high : 2 * n_high] + acc[2 * n_high :]


def call(kernel, outs, scratch, args, in_smem=(), in_hbm=(), in_any=(), out_hbm=(), types={}):
    vmem = pl.BlockSpec(memory_space=pltpu.VMEM)
    hbm = pl.BlockSpec(memory_space=pltpu.HBM)
    free = pl.BlockSpec(memory_space=pl.ANY)
    smem = pl.BlockSpec(memory_space=pltpu.SMEM)
    return pl.pallas_call(
        kernel,
        out_shape=[
            jax.ShapeDtypeStruct(s, types.get(n, jnp.float32)) for n, s in enumerate(outs)
        ],
        in_specs=[
            smem if n in in_smem else hbm if n in in_hbm else free if n in in_any else vmem
            for n in range(len(args))
        ],
        out_specs=[hbm if n in out_hbm else vmem for n in range(len(outs))],
        scratch_shapes=scratch,
        compiler_params=pltpu.CompilerParams(vmem_limit_bytes=40 << 20),
    )(*args)


def exchange(ab, up, dn):
    n = lax.axis_size("gx")
    m = lax.axis_size("yz")
    assert m == 4
    hop = []
    for q in range(m):
        for g in range(n):
            to = g + 1 if q % 2 == 0 else g - 1
            hop.append((g * m + q, to * m + q if 0 <= to < n else g * m + (q ^ 1)))
    is_even = lax.axis_index("yz") % 2 == 0
    one = lax.ppermute(jnp.where(is_even, up, dn), ("gx", "yz"), hop)
    two = lax.ppermute(jnp.where(is_even, dn, up), ("gx", "yz"), [(j, i) for i, j in hop])
    across = [(q, q ^ 2) for q in range(m)]
    ab_far = lax.ppermute(ab, "yz", across)
    one_far = lax.ppermute(one, "yz", across)
    two_far = lax.ppermute(two, "yz", across)
    l_near = jnp.concatenate(
        [jnp.where(is_even, one, two), jnp.where(is_even, two, one)], axis=1
    )
    l_far = jnp.concatenate(
        [jnp.where(is_even, one_far, two_far), jnp.where(is_even, two_far, one_far)], axis=1
    )
    both = jnp.concatenate(
        [jnp.concatenate([ab, l_near], axis=1), jnp.concatenate([ab_far, l_far], axis=1)],
        axis=0,
    )
    pairs = [[0, 1], [2, 3]]
    return two, lax.all_gather(both, "yz", axis=0, tiled=True, axis_index_groups=pairs)


def body(pops_start, tile_pos, wall_mask, wall_frac, patch_id, probe):
    count = pops_start.shape[0]
    n_layers = lax.axis_size("gx")
    n_cross = lax.axis_size("yz")
    parts = n_layers * n_cross
    dims = (n_layers, n_cross)
    field = pops_start.shape
    plane = wall_frac.shape
    patch_dev = 64
    n_high = patch_dev * parts // LANES
    inverse = pltpu.SMEM((3, n_cross * count + 1), jnp.int32)

    def ends(pack):
        return [(count, pack.l_rows, LANES)] * 2

    def sides(pack):
        return [(count, pack.ab_rows, LANES)]

    post0, solid, probe_kept, up, dn = call(
        first_kernel,
        [field, plane, plane] + ends(PACK1),
        [
            pltpu.VMEM(field, jnp.float32),
            pltpu.VMEM(plane, jnp.int32),
            pltpu.VMEM(plane, jnp.float32),
            pltpu.SemaphoreType.DMA((3 + 2 * count,)),
        ],
        tuple(
            pltpu.with_memory_space_constraint(x, pltpu.HBM)
            for x in (pops_start, wall_mask, wall_frac, probe)
        ),
        in_hbm=range(4),
    )
    (ab,) = call(first_sides, sides(PACK1), [], (post0, probe_kept))
    token, around = exchange(ab, up, dn)
    axial = (count, len(AXIAL)) + plane[1:]
    moved, back = call(first_own, [field, axial], [], (post0, probe_kept, token), in_any=(2,))
    post1, adj1, dsolid, up, dn = call(
        functools.partial(second_kernel, dims),
        [field, field, plane] + ends(PACK2),
        [
            pltpu.VMEM(field, jnp.float32),
            pltpu.VMEM((count, len(AXIAL)) + plane[1:], jnp.float32),
            inverse,
        ],
        (tile_pos, moved, back, solid, around),
        in_smem=(0,),
    )
    (ab,) = call(second_sides, sides(PACK2), [], (post1, adj1))
    token, around = exchange(ab, up, dn)
    moved, back, onehot = call(
        second_own,
        [field, field, (count, TL, LANES, CELLS)],
        [],
        (post1, adj1, patch_id, token),
        in_any=(3,),
        types={2: jnp.bfloat16},
    )
    pops_final, adjoint_start, sums = call(
        functools.partial(third_kernel, dims),
        [field, field, (n_high, LANES)],
        [
            pltpu.VMEM(field, jnp.float32),
            pltpu.VMEM(field, jnp.float32),
            pltpu.VMEM(field, jnp.float32),
            pltpu.VMEM(plane, jnp.float32),
            inverse,
            pltpu.SemaphoreType.DMA((2 * count,)),
        ],
        (tile_pos, moved, back, onehot, pops_start, wall_mask, solid, patch_id, dsolid, around),
        in_smem=(0,),
        out_hbm=(0, 1),
    )
    shares = lax.all_to_all(
        sums.reshape(parts, patch_dev), ("gx", "yz"), 0, 0, tiled=True
    )
    return (pops_final, adjoint_start, jnp.sum(shares, axis=0))


def solution(mesh):
    in_specs = (
        P(("gx", "yz"), None, None, None),
        P(),
        P(("gx", "yz"), None, None),
        P(("gx", "yz"), None, None),
        P(("gx", "yz"), None, None),
        P(("gx", "yz"), None, None),
    )
    out_specs = (
        P(("gx", "yz"), None, None, None),
        P(("gx", "yz"), None, None, None),
        P(("gx", "yz")),
    )
    return jax.shard_map(body, mesh=mesh, in_specs=in_specs, out_specs=out_specs, check_vma=False)
```

```python
import functools

import jax
import jax.numpy as jnp
import numpy as np
from jax import lax
from jax.experimental import pallas as pl
from jax.experimental.pallas import tpu as pltpu
from jax.sharding import PartitionSpec as P

TL = 16
TA = 16
TB = 32
CELLS = TA * TB
LANES = 128
COLS = CELLS // LANES
OMEGA = 1.25

VELOCITY = np.array(
    [
        [0, 0, 0],
        [1, 0, 0],
        [-1, 0, 0],
        [0, 1, 0],
        [0, -1, 0],
        [0, 0, 1],
        [0, 0, -1],
        [1, 1, 0],
        [-1, -1, 0],
        [1, -1, 0],
        [-1, 1, 0],
        [1, 0, 1],
        [-1, 0, -1],
        [1, 0, -1],
        [-1, 0, 1],
        [0, 1, 1],
        [0, -1, -1],
        [0, 1, -1],
        [0, -1, 1],
    ]
)
Q = 19
WEIGHTS = [1.0 / 3.0] + [1.0 / 18.0] * 6 + [1.0 / 36.0] * 12
PAIRS = [(2 * k + 1, 2 * k + 2) for k in range(9)]
AXIAL = [i for i in range(Q) if VELOCITY[i, 0] != 0]


def vel(i):
    return tuple(int(v) for v in VELOCITY[i])


def members_of(dim, value):
    return [i for i in range(Q) if vel(i)[dim] == value]


def face_list(stage, dim, side):
    if stage == 1:
        return [("post", i) for i in members_of(dim, side)] + [("probe", 0)]
    return [("post", i) for i in members_of(dim, side)] + [
        ("adj", i) for i in members_of(dim, -side)
    ]


class Pack:
    def __init__(self, stage):
        self.n = len(face_list(stage, 0, 1))
        self.lists = {
            (d, s): face_list(stage, d, s) for d in range(3) for s in (-1, 1)
        }
        self.fold = 2 if 2 * self.n <= TB // 2 else 1
        self.a_cols = -(-2 * self.n * TB // LANES)
        self.b_cols = COLS // self.fold
        self.a_row = 0
        self.b_row = TL * self.a_cols
        self.ab_rows = self.b_row + TL * self.b_cols
        self.l_rows = self.n * COLS
        self.up_row = self.ab_rows
        self.dn_row = self.up_row + self.l_rows
        self.rows = self.dn_row + self.l_rows

    def slot(self, dim, side, key):
        j = self.lists[(dim, side)].index(key)
        return j if dim == 0 or side < 0 else j + self.n


PACK1 = Pack(1)
PACK2 = Pack(2)


def lane_roll(x, shift):
    shift = shift % x.shape[-1]
    return x if shift == 0 else pltpu.roll(x, shift, axis=x.ndim - 1)


def row_roll(x, shift):
    shift = shift % x.shape[0]
    return x if shift == 0 else pltpu.roll(x, shift, axis=0)


def lane_iota(shape):
    return lax.broadcasted_iota(jnp.int32, shape, len(shape) - 1)


def row_iota(shape):
    return lax.broadcasted_iota(jnp.int32, shape, 0)


def combine(c, parts):
    total = None
    for v, p in zip(c, parts):
        if v == 0:
            continue
        if total is None:
            total = p if v > 0 else -p
        else:
            total = total + p if v > 0 else total - p
    return total


def flow(f):
    rho = f[0]
    momentum = [None, None, None]
    for i, j in PAIRS:
        rho = rho + (f[i] + f[j])
        diff = f[i] - f[j]
        for d, v in enumerate(vel(i)):
            if v == 0:
                continue
            if momentum[d] is None:
                momentum[d] = diff if v > 0 else -diff
            else:
                momentum[d] = momentum[d] + diff if v > 0 else momentum[d] - diff
    inv = 1.0 / rho
    u = [m * inv for m in momentum]
    square = u[0] * u[0] + u[1] * u[1] + u[2] * u[2]
    return rho, u, 1.0 - 1.5 * square


def collide(f, solid, rho, u, base):
    fluid = 1.0 - solid
    keep = (1.0 - OMEGA) * fluid
    scale = OMEGA * fluid * rho
    out = [None] * Q
    out[0] = (keep + solid) * f[0] + WEIGHTS[0] * scale * base
    for i, j in PAIRS:
        along = combine(vel(i), u)
        ws = WEIGHTS[i] * scale
        even = ws * (base + 4.5 * along * along)
        odd = ws * (3.0 * along)
        out[i] = keep * f[i] + solid * f[j] + (even + odd)
        out[j] = keep * f[j] + solid * f[i] + (even - odd)
    return out


def pullback(f, solid, rho, u, base, g):
    fluid = 1.0 - solid
    keep = (1.0 - OMEGA) * fluid
    gain = OMEGA * fluid
    lin = [None, None, None]
    total = None
    dens = None
    cross = None

    def plus(a, b):
        return b if a is None else a + b

    if g[0] is not None:
        e = WEIGHTS[0] * g[0]
        total = e
        dens = e * base
        cross = OMEGA * (g[0] * f[0])
    for i, j in PAIRS:
        if g[i] is None:
            continue
        along = combine(vel(i), u)
        w = WEIGHTS[i]
        even = w * (g[i] + g[j])
        odd = w * (g[i] - g[j])
        total = plus(total, even)
        dens = plus(dens, even * (base + 4.5 * along * along) + 3.0 * along * odd)
        push = 3.0 * odd + 9.0 * along * even
        for d, v in enumerate(vel(i)):
            if v:
                lin[d] = plus(lin[d], push if v > 0 else -push)
        cross = plus(
            cross,
            g[i] * (f[j] - (1.0 - OMEGA) * f[i]) + g[j] * (f[i] - (1.0 - OMEGA) * f[j]),
        )
    lin = [
        (-3.0 * u[d] * total if lin[d] is None else lin[d] - 3.0 * u[d] * total)
        for d in range(3)
    ]
    dsolid = cross - OMEGA * rho * dens
    shared = gain * (dens - (lin[0] * u[0] + lin[1] * u[1] + lin[2] * u[2]))
    lin = [gain * v for v in lin]
    out = [None] * Q
    out[0] = shared if g[0] is None else (keep + solid) * g[0] + shared
    for i, j in PAIRS:
        slope = combine(vel(i), lin)
        if g[i] is None:
            out[i] = shared + slope
            out[j] = shared - slope
        else:
            out[i] = keep * g[i] + solid * g[j] + (shared + slope)
            out[j] = keep * g[j] + solid * g[i] + (shared - slope)
    return out, dsolid


def side_jobs(pack, t, get, ab_ref):
    lane = lane_iota((TL, LANES))

    def a_col(col):
        acc = jnp.zeros((TL, LANES), jnp.float32)
        for side in (-1, 1):
            for key in pack.lists[(1, side)]:
                j = pack.slot(1, side, key)
                if j // 4 != col:
                    continue
                to = TB * (j % 4)
                if side < 0:
                    part = lane_roll(get(key, slice(None), slice(0, LANES)), to)
                else:
                    part = lane_roll(
                        get(key, slice(None), slice(CELLS - LANES, CELLS)),
                        to - (LANES - TB),
                    )
                acc = jnp.where((lane >> 5) == j % 4, part, acc)
        ab_ref[t, pack.a_row + TL * col : pack.a_row + TL * (col + 1), :] = acc

    def b_col(col):
        acc = jnp.zeros((TL, LANES), jnp.float32)
        for half in range(pack.fold):
            src = col + half * pack.b_cols
            for side in (-1, 1):
                for key in pack.lists[(2, side)]:
                    j = pack.slot(2, side, key) + half * (TB // 2)
                    part = get(key, slice(None), slice(LANES * src, LANES * (src + 1)))
                    part = lane_roll(part, j if side < 0 else j - (TB - 1))
                    acc = jnp.where((lane & (TB - 1)) == j, part, acc)
        ab_ref[t, pack.b_row + TL * col : pack.b_row + TL * (col + 1), :] = acc

    return [functools.partial(a_col, c) for c in range(pack.a_cols)] + [
        functools.partial(b_col, c) for c in range(pack.b_cols)
    ]


def end_jobs(pack, t, get, up_ref, dn_ref):
    def l_rows(side, ref, key):
        row = TL - 1 if side > 0 else 0
        j = pack.slot(0, side, key)
        for col in range(COLS):
            ref[t, j * COLS + col : j * COLS + col + 1, :] = get(
                key, slice(row, row + 1), slice(LANES * col, LANES * (col + 1))
            )

    return [
        functools.partial(l_rows, side, ref, key)
        for side, ref in ((1, up_ref), (-1, dn_ref))
        for key in pack.lists[(0, side)]
    ]


def first_sides(post, probe, ab):
    def sides(t):
        def get(key, rows, lanes):
            if key[0] == "probe":
                return probe[t, rows, lanes]
            return post[t, key[1], rows, lanes]

        return side_jobs(PACK1, t, get, ab)

    staged(post.shape[0], [sides])


def second_sides(post1, adj1, ab):
    def sides(t):
        def get(key, rows, lanes):
            return (post1 if key[0] == "post" else adj1)[t, key[1], rows, lanes]

        return side_jobs(PACK2, t, get, ab)

    staged(post1.shape[0], [sides])


def weave(lists):
    jobs = [
        ((n + 0.5) / len(items), k, job)
        for k, items in enumerate(lists)
        for n, job in enumerate(items)
    ]
    for _, _, job in sorted(jobs, key=lambda job: job[:2]):
        job()


def staged(count, stages, after=None):
    for step in range(count + len(stages) - 1):
        live = [(k, step - k) for k in range(len(stages)) if 0 <= step - k < count]
        weave([stages[k](t) for k, t in live])
        if after is not None:
            for k, t in live:
                after(k, t)


def build_inverse(pos_ref, inv_ref, n_layers, group):
    layer = lax.axis_index("gx")
    for off in (-1, 0, 1):
        for w in range(group + 1):
            inv_ref[off + 1, w] = -1
        target = layer + off
        valid = (target >= 0) & (target < n_layers)
        first = jnp.clip(target, 0, n_layers - 1) * group
        for s in range(group):
            p = pos_ref[first + s]
            inv_ref[off + 1, jnp.where(valid & (p >= 0), p, group)] = s


class Neighbours:
    def __init__(self, pack, t, faces_ref, pos_ref, inv_ref, n_cross, count):
        self.pack = pack
        self.ref = faces_ref
        group = n_cross * count
        own = pos_ref[lax.axis_index("gx") * group + lax.axis_index("yz") * count + t]
        p = jnp.maximum(own, 0)
        a, b = p // count, p % count
        self.alive = own >= 0
        self.where = {}
        for d in [vel(i) for i in range(1, Q)]:
            ta, tb = a + d[1], b + d[2]
            ok = (ta >= 0) & (ta < n_cross) & (tb >= 0) & (tb < count)
            s = inv_ref[d[0] + 1, jnp.where(ok, ta * count + tb, group)]
            found = ok & (s >= 0)
            s = jnp.where(found, s, 0)
            owner, slot = s // count, s % count
            half = ((owner ^ lax.axis_index("yz")) >> 1) & 1
            side = owner & 1
            if pack is PACK1:
                side = side ^ (lax.axis_index("yz") & 1)
            block = (side * 2 + half) * count + slot
            self.where[d] = (block, found)
        self.planes = {}

    def a_face(self, d, side, key, fill, to):
        k, found = self.where[d]
        j = self.pack.slot(1, side, key)
        row = self.pack.a_row + TL * (j // 4)
        face = self.ref[k, row : row + TL, :]
        face = lane_roll(face, to - TB * (j % 4))
        return jnp.where(found, face, fill)

    def b_plane(self, d):
        if d not in self.planes:
            k, found = self.where[d]
            row = self.pack.b_row
            half = jnp.concatenate(
                [
                    self.ref[k, row + TL * c : row + TL * (c + 1), :]
                    for c in range(self.pack.b_cols)
                ],
                axis=1,
            )
            if self.pack.fold == 2:
                half = jnp.concatenate([half, lane_roll(half, -(TB // 2))], axis=1)
            self.planes[d] = half
        return self.planes[d], self.where[d][1]

    def l_row(self, d, side, key, fill):
        k, found = self.where[d]
        first = self.pack.up_row if side > 0 else self.pack.dn_row
        first = first + self.pack.slot(0, side, key) * COLS
        row = jnp.concatenate(
            [self.ref[k, first + c : first + c + 1, :] for c in range(COLS)], axis=1
        )
        return jnp.where(found, row, fill)

    def enter(self, x, c, key, fill):
        cl, ca, cb = c
        shape = (TL, CELLS)
        if ca:
            to = 0 if ca > 0 else LANES - TB
            face = row_roll(self.a_face((0, -ca, 0), ca, key, fill, to + cb), cl)
            inner = lane_iota((TL, LANES))
            hit = inner < TB if ca > 0 else inner >= LANES - TB
            part = slice(0, LANES) if ca > 0 else slice(CELLS - LANES, CELLS)
            face = jnp.where(hit, face, x[:, part])
            x = jnp.concatenate(
                [face, x[:, LANES:]] if ca > 0 else [x[:, : CELLS - LANES], face], axis=1
            )
        if cb:
            plane, found = self.b_plane((0, 0, -cb))
            plane = jnp.where(found, plane, fill)
            if ca:
                corner, found = self.b_plane((0, -ca, -cb))
                part = slice(CELLS - LANES, CELLS) if ca > 0 else slice(0, LANES)
                inner = lane_iota((TL, LANES))
                hit = inner >= LANES - TB if ca > 0 else inner < TB
                corner = jnp.where(found, corner[:, part], fill)
                corner = jnp.where(hit, corner, plane[:, part])
                plane = jnp.concatenate(
                    [plane[:, : CELLS - LANES], corner] if ca > 0 else [corner, plane[:, LANES:]],
                    axis=1,
                )
            at = 0 if cb > 0 else TB - 1
            face = lane_roll(plane, TB * ca + at - self.pack.slot(2, cb, key))
            x = jnp.where((lane_iota(shape) & (TB - 1)) == at, row_roll(face, cl), x)
        if cl:
            row = self.l_row((-cl, 0, 0), cl, key, fill)
            lane = lane_iota((1, CELLS))
            if ca:
                corner = self.l_row((-cl, -ca, 0), cl, key, fill)
                row = jnp.where((lane >> 5) == (TA - 1 if ca > 0 else 0), corner, row)
            row = lane_roll(row, TB * ca + cb)
            if cb:
                corner = self.l_row((-cl, 0, -cb), cl, key, fill)
                corner = lane_roll(corner, -cb * (TB - 1))
                row = jnp.where((lane & (TB - 1)) == (0 if cb > 0 else TB - 1), corner, row)
            half = (TL // 2, CELLS)
            low, high = x[: TL // 2], x[TL // 2 :]
            row = jnp.broadcast_to(row, half)
            if cl > 0:
                low = jnp.where(row_iota(half) == 0, row, low)
            else:
                high = jnp.where(row_iota(half) == TL // 2 - 1, row, high)
            x = jnp.concatenate([low, high], axis=0)
        return x


def shifted(x, c):
    return row_roll(lane_roll(x, TB * c[1] + c[2]), c[0])


def against(i):
    return tuple(-v for v in vel(i))


def first_own(post, probe, after, moved, back):
    del after
    for t in range(post.shape[0]):
        for i in range(Q):
            moved[t, i] = shifted(post[t, i], vel(i))
        for n, i in enumerate(AXIAL):
            back[t, n] = shifted(probe[t], against(i))


def second_own(post1, adj1, patch, after, moved, back, onehot):
    del after
    low_iota = lax.broadcasted_iota(jnp.int32, (LANES, CELLS), 0)
    for t in range(post1.shape[0]):
        for i in range(Q):
            moved[t, i] = shifted(post1[t, i], vel(i))
            back[t, i] = shifted(adj1[t, i], against(i))
            if i < TL:
                low = patch[t, i : i + 1, :] & (LANES - 1)
                onehot[t, i] = jnp.where(low_iota == low, 1.0, 0.0).astype(jnp.bfloat16)


def first_kernel(pops_in, mask_in, frac_in, probe_in, post, solid, probe, up, dn, pops, mask, frac, sems):
    count = pops.shape[0]
    small = [
        pltpu.make_async_copy(src, dst, sems.at[n])
        for n, (src, dst) in enumerate(((mask_in, mask), (frac_in, frac), (probe_in, probe)))
    ]
    halves = [(t, r) for t in range(count) for r in range(2)]
    large = [
        pltpu.make_async_copy(
            pops_in.at[t, :, pl.ds(8 * r, 8), :],
            pops.at[t, :, pl.ds(8 * r, 8), :],
            sems.at[len(small) + n],
        )
        for n, (t, r) in enumerate(halves)
    ]
    for copy in small[:2] + large + small[2:]:
        copy.start()
    for copy in small[:2]:
        copy.wait()
    solid[...] = mask[...].astype(jnp.float32) * frac[...]

    def collides(t):
        def run(r, c):
            if c == 0:
                large[halves.index((t, r))].wait()
            rows = slice(8 * r, 8 * r + 8)
            lanes = slice(LANES * c, LANES * (c + 1))
            f = [pops[t, i, rows, lanes] for i in range(Q)]
            out = collide(f, solid[t, rows, lanes], *flow(f))
            for i in range(Q):
                post[t, i, rows, lanes] = out[i]

        return [functools.partial(run, r, c) for r in range(2) for c in range(COLS)]

    def faces(t):
        def get(key, rows, lanes):
            if key[0] == "probe":
                return probe[t, rows, lanes]
            return post[t, key[1], rows, lanes]

        return end_jobs(PACK1, t, get, up, dn)

    small[2].wait()
    staged(count, [collides, faces])


def second_kernel(
    dims, pos, moved, back, solid_in, around, post1, adj1, dsolid, up, dn, state, pulled, inv
):
    n_layers, n_cross = dims
    count = solid_in.shape[0]
    build_inverse(pos, inv, n_layers, n_cross * count)

    def moves(t):
        near = Neighbours(PACK1, t, around, pos, inv, n_cross, count)

        def forward(i):
            state[t, i] = near.enter(moved[t, i], vel(i), ("post", i), WEIGHTS[i])

        def backward(n, i):
            x = near.enter(back[t, n], against(i), ("probe", 0), 0.0)
            pulled[t, n] = x if vel(i)[0] > 0 else -x

        jobs = [(vel(i), functools.partial(forward, i)) for i in range(Q)]
        jobs += [(against(i), functools.partial(backward, n, i)) for n, i in enumerate(AXIAL)]
        return [job for _, job in sorted(jobs, key=lambda item: (item[0][2], item[0][1]))]

    def runs(t):
        def run(r, c):
            rows = slice(8 * r, 8 * r + 8)
            lanes = slice(LANES * c, LANES * (c + 1))
            f = [state[t, i, rows, lanes] for i in range(Q)]
            solid = solid_in[t, rows, lanes]
            rho, u, base = flow(f)
            out = collide(f, solid, rho, u, base)
            for i in range(Q):
                post1[t, i, rows, lanes] = out[i]
            g = [None] * Q
            for n, i in enumerate(AXIAL):
                g[i] = pulled[t, n, rows, lanes]
            df, ds = pullback(f, solid, rho, u, base, g)
            for i in range(Q):
                adj1[t, i, rows, lanes] = df[i]
            dsolid[t, rows, lanes] = ds

        return [functools.partial(run, r, c) for r in range(2) for c in range(COLS)]

    def faces(t):
        def get(key, rows, lanes):
            return (post1 if key[0] == "post" else adj1)[t, key[1], rows, lanes]

        return end_jobs(PACK2, t, get, up, dn)

    staged(count, [moves, runs, faces])


def third_kernel(
    dims, pos, moved, back, onehot, pops, mask, solid_in, patch, dsolid, around, final_out, start_out, sums, final, start, pulled, weighted, inv, sems
):
    n_layers, n_cross = dims
    count = pops.shape[0]
    group = n_cross * count
    build_inverse(pos, inv, n_layers, group)

    base_slot = lax.axis_index("gx") * group + lax.axis_index("yz") * count
    n_high = sums.shape[0]
    high_iota = lax.broadcasted_iota(jnp.int32, (n_high, CELLS), 0)
    total = [jnp.zeros((3 * n_high, LANES), jnp.float32)]

    def moves(t):
        near = Neighbours(PACK2, t, around, pos, inv, n_cross, count)

        def forward(i):
            x = near.enter(moved[t, i], vel(i), ("post", i), WEIGHTS[i])
            final[t, i] = jnp.where(near.alive, x, 0.0)

        def backward(i):
            pulled[t, i] = near.enter(back[t, i], against(i), ("adj", i), 0.0)

        order = [functools.partial(backward, i) for i in range(Q)]
        return order + [functools.partial(forward, i) for i in range(Q)]

    def runs(t):
        alive = pos[base_slot + t] >= 0

        def run(r, c):
            rows = slice(8 * r, 8 * r + 8)
            lanes = slice(LANES * c, LANES * (c + 1))
            f = [pops[t, i, rows, lanes] for i in range(Q)]
            g = [pulled[t, i, rows, lanes] for i in range(Q)]
            wall = mask[t, rows, lanes].astype(jnp.float32)
            solid = solid_in[t, rows, lanes]
            rho, u, base = flow(f)
            df, ds = pullback(f, solid, rho, u, base, g)
            for i in range(Q):
                start[t, i, rows, lanes] = jnp.where(alive, df[i], 0.0)
            part = wall * (ds + dsolid[t, rows, lanes])
            weighted[t, rows, lanes] = jnp.where(alive, part, 0.0)

        return [functools.partial(run, r, c) for r in range(2) for c in range(COLS)]

    def add(t, r):
        ids = patch[t, r : r + 1, :]
        w = weighted[t, r : r + 1, :]
        w1 = w.astype(jnp.bfloat16).astype(jnp.float32)
        w2 = (w - w1).astype(jnp.bfloat16).astype(jnp.float32)
        w3 = w - w1 - w2
        high = high_iota == (ids >> 7)
        left = jnp.concatenate(
            [jnp.where(high, part, 0.0).astype(jnp.bfloat16) for part in (w1, w2, w3)],
            axis=0,
        )
        total[0] = total[0] + lax.dot_general(
            left, onehot[t, r], (((1,), (1,)), ((), ())), preferred_element_type=jnp.float32
        )

    def adds(t):
        return [functools.partial(add, t, r) for r in range(TL)]

    copies = []

    def send(k, t):
        if k < 2:
            src, dst = ((final, final_out), (start, start_out))[k]
            copies.append(pltpu.make_async_copy(src.at[t], dst.at[t], sems.at[len(copies)]))
            copies[-1].start()

    staged(count, [moves, runs, adds], send)
    for copy in copies:
        copy.wait()
    acc = total[0]
    sums[...] = acc[:n_high] + acc[n_high : 2 * n_high] + acc[2 * n_high :]


def call(kernel, outs, scratch, args, in_smem=(), in_hbm=(), in_any=(), out_hbm=(), types={}):
    vmem = pl.BlockSpec(memory_space=pltpu.VMEM)
    hbm = pl.BlockSpec(memory_space=pltpu.HBM)
    free = pl.BlockSpec(memory_space=pl.ANY)
    smem = pl.BlockSpec(memory_space=pltpu.SMEM)
    return pl.pallas_call(
        kernel,
        out_shape=[
            jax.ShapeDtypeStruct(s, types.get(n, jnp.float32)) for n, s in enumerate(outs)
        ],
        in_specs=[
            smem if n in in_smem else hbm if n in in_hbm else free if n in in_any else vmem
            for n in range(len(args))
        ],
        out_specs=[hbm if n in out_hbm else vmem for n in range(len(outs))],
        scratch_shapes=scratch,
        compiler_params=pltpu.CompilerParams(vmem_limit_bytes=40 << 20),
    )(*args)


def exchange(ab, up, dn, first):
    n = lax.axis_size("gx")
    m = lax.axis_size("yz")
    assert m == 4
    hop = []
    for q in range(m):
        for g in range(n):
            to = g + 1 if q < 2 else g - 1
            hop.append((g * m + q, to * m + q if 0 <= to < n else g * m + (q ^ 2)))
    is_low = lax.axis_index("yz") < 2
    one = lax.ppermute(jnp.where(is_low, up, dn), ("gx", "yz"), hop)
    two = lax.ppermute(jnp.where(is_low, dn, up), ("gx", "yz"), [(j, i) for i, j in hop])
    across = [(q, q ^ 2) for q in range(m)]
    ab_far = lax.ppermute(ab, "yz", across)
    one_far = lax.ppermute(one, "yz", across)
    two_far = lax.ppermute(two, "yz", across)
    l_near = jnp.concatenate(
        [jnp.where(is_low, one, two), jnp.where(is_low, two, one)], axis=1
    )
    l_far = jnp.concatenate(
        [jnp.where(is_low, two_far, one_far), jnp.where(is_low, one_far, two_far)], axis=1
    )
    both = jnp.concatenate(
        [jnp.concatenate([ab, l_near], axis=1), jnp.concatenate([ab_far, l_far], axis=1)],
        axis=0,
    )
    if first:
        other = lax.ppermute(both, "yz", [(q, q ^ 1) for q in range(m)])
        return two, jnp.concatenate([both, other], axis=0)
    pairs = [[0, 1], [2, 3]]
    return two, lax.all_gather(both, "yz", axis=0, tiled=True, axis_index_groups=pairs)


def body(pops_start, tile_pos, wall_mask, wall_frac, patch_id, probe):
    count = pops_start.shape[0]
    n_layers = lax.axis_size("gx")
    n_cross = lax.axis_size("yz")
    parts = n_layers * n_cross
    dims = (n_layers, n_cross)
    field = pops_start.shape
    plane = wall_frac.shape
    patch_dev = 64
    n_high = patch_dev * parts // LANES
    inverse = pltpu.SMEM((3, n_cross * count + 1), jnp.int32)

    def ends(pack):
        return [(count, pack.l_rows, LANES)] * 2

    def sides(pack):
        return [(count, pack.ab_rows, LANES)]

    post0, solid, probe_kept, up, dn = call(
        first_kernel,
        [field, plane, plane] + ends(PACK1),
        [
            pltpu.VMEM(field, jnp.float32),
            pltpu.VMEM(plane, jnp.int32),
            pltpu.VMEM(plane, jnp.float32),
            pltpu.SemaphoreType.DMA((3 + 2 * count,)),
        ],
        tuple(
            pltpu.with_memory_space_constraint(x, pltpu.HBM)
            for x in (pops_start, wall_mask, wall_frac, probe)
        ),
        in_hbm=range(4),
    )
    (ab,) = call(first_sides, sides(PACK1), [], (post0, probe_kept))
    token, around = exchange(ab, up, dn, True)
    axial = (count, len(AXIAL)) + plane[1:]
    moved, back = call(first_own, [field, axial], [], (post0, probe_kept, token), in_any=(2,))
    post1, adj1, dsolid, up, dn = call(
        functools.partial(second_kernel, dims),
        [field, field, plane] + ends(PACK2),
        [
            pltpu.VMEM(field, jnp.float32),
            pltpu.VMEM((count, len(AXIAL)) + plane[1:], jnp.float32),
            inverse,
        ],
        (tile_pos, moved, back, solid, around),
        in_smem=(0,),
    )
    (ab,) = call(second_sides, sides(PACK2), [], (post1, adj1))
    token, around = exchange(ab, up, dn, False)
    moved, back, onehot = call(
        second_own,
        [field, field, (count, TL, LANES, CELLS)],
        [],
        (post1, adj1, patch_id, token),
        in_any=(3,),
        types={2: jnp.bfloat16},
    )
    pops_final, adjoint_start, sums = call(
        functools.partial(third_kernel, dims),
        [field, field, (n_high, LANES)],
        [
            pltpu.VMEM(field, jnp.float32),
            pltpu.VMEM(field, jnp.float32),
            pltpu.VMEM(field, jnp.float32),
            pltpu.VMEM(plane, jnp.float32),
            inverse,
            pltpu.SemaphoreType.DMA((2 * count,)),
        ],
        (tile_pos, moved, back, onehot, pops_start, wall_mask, solid, patch_id, dsolid, around),
        in_smem=(0,),
        out_hbm=(0, 1),
    )
    shares = lax.all_to_all(
        sums.reshape(parts, patch_dev), ("gx", "yz"), 0, 0, tiled=True
    )
    return (pops_final, adjoint_start, jnp.sum(shares, axis=0))


def solution(mesh):
    in_specs = (
        P(("gx", "yz"), None, None, None),
        P(),
        P(("gx", "yz"), None, None),
        P(("gx", "yz"), None, None),
        P(("gx", "yz"), None, None),
        P(("gx", "yz"), None, None),
    )
    out_specs = (
        P(("gx", "yz"), None, None, None),
        P(("gx", "yz"), None, None, None),
        P(("gx", "yz")),
    )
    return jax.shard_map(body, mesh=mesh, in_specs=in_specs, out_specs=out_specs, check_vma=False)
```

```python
import functools

import jax
import jax.numpy as jnp
import numpy as np
from jax import lax
from jax.experimental import pallas as pl
from jax.experimental.pallas import tpu as pltpu
from jax.sharding import PartitionSpec as P

TL = 16
TA = 16
TB = 32
CELLS = TA * TB
LANES = 128
COLS = CELLS // LANES
OMEGA = 1.25

VELOCITY = np.array(
    [
        [0, 0, 0],
        [1, 0, 0],
        [-1, 0, 0],
        [0, 1, 0],
        [0, -1, 0],
        [0, 0, 1],
        [0, 0, -1],
        [1, 1, 0],
        [-1, -1, 0],
        [1, -1, 0],
        [-1, 1, 0],
        [1, 0, 1],
        [-1, 0, -1],
        [1, 0, -1],
        [-1, 0, 1],
        [0, 1, 1],
        [0, -1, -1],
        [0, 1, -1],
        [0, -1, 1],
    ]
)
Q = 19
WEIGHTS = [1.0 / 3.0] + [1.0 / 18.0] * 6 + [1.0 / 36.0] * 12
PAIRS = [(2 * k + 1, 2 * k + 2) for k in range(9)]
AXIAL = [i for i in range(Q) if VELOCITY[i, 0] != 0]


def vel(i):
    return tuple(int(v) for v in VELOCITY[i])


def members_of(dim, value):
    return [i for i in range(Q) if vel(i)[dim] == value]


def face_list(stage, dim, side):
    if stage == 1:
        return [("post", i) for i in members_of(dim, side)] + [("probe", 0)]
    return [("post", i) for i in members_of(dim, side)] + [
        ("adj", i) for i in members_of(dim, -side)
    ]


class Pack:
    def __init__(self, stage):
        self.n = len(face_list(stage, 0, 1))
        self.lists = {
            (d, s): face_list(stage, d, s) for d in range(3) for s in (-1, 1)
        }
        self.fold = 2 if 2 * self.n <= TB // 2 else 1
        self.a_cols = -(-2 * self.n * TB // LANES)
        self.b_cols = COLS // self.fold
        self.a_row = 0
        self.b_row = TL * self.a_cols
        self.ab_rows = self.b_row + TL * self.b_cols
        self.l_rows = self.n * COLS
        self.up_row = self.ab_rows
        self.dn_row = self.up_row + self.l_rows
        self.rows = self.dn_row + self.l_rows

    def slot(self, dim, side, key):
        j = self.lists[(dim, side)].index(key)
        return j if dim == 0 or side < 0 else j + self.n


PACK1 = Pack(1)
PACK2 = Pack(2)


def lane_roll(x, shift):
    shift = shift % x.shape[-1]
    return x if shift == 0 else pltpu.roll(x, shift, axis=x.ndim - 1)


def row_roll(x, shift):
    shift = shift % x.shape[0]
    return x if shift == 0 else pltpu.roll(x, shift, axis=0)


def lane_iota(shape):
    return lax.broadcasted_iota(jnp.int32, shape, len(shape) - 1)


def row_iota(shape):
    return lax.broadcasted_iota(jnp.int32, shape, 0)


def combine(c, parts):
    total = None
    for v, p in zip(c, parts):
        if v == 0:
            continue
        if total is None:
            total = p if v > 0 else -p
        else:
            total = total + p if v > 0 else total - p
    return total


def flow(f):
    rho = f[0]
    momentum = [None, None, None]
    for i, j in PAIRS:
        rho = rho + (f[i] + f[j])
        diff = f[i] - f[j]
        for d, v in enumerate(vel(i)):
            if v == 0:
                continue
            if momentum[d] is None:
                momentum[d] = diff if v > 0 else -diff
            else:
                momentum[d] = momentum[d] + diff if v > 0 else momentum[d] - diff
    inv = 1.0 / rho
    u = [m * inv for m in momentum]
    square = u[0] * u[0] + u[1] * u[1] + u[2] * u[2]
    return rho, u, 1.0 - 1.5 * square


def collide(f, solid, rho, u, base):
    fluid = 1.0 - solid
    keep = (1.0 - OMEGA) * fluid
    scale = OMEGA * fluid * rho
    out = [None] * Q
    out[0] = (keep + solid) * f[0] + WEIGHTS[0] * scale * base
    for i, j in PAIRS:
        along = combine(vel(i), u)
        ws = WEIGHTS[i] * scale
        even = ws * (base + 4.5 * along * along)
        odd = ws * (3.0 * along)
        out[i] = keep * f[i] + solid * f[j] + (even + odd)
        out[j] = keep * f[j] + solid * f[i] + (even - odd)
    return out


def pullback(f, solid, rho, u, base, g):
    fluid = 1.0 - solid
    keep = (1.0 - OMEGA) * fluid
    gain = OMEGA * fluid
    lin = [None, None, None]
    total = None
    dens = None
    cross = None

    def plus(a, b):
        return b if a is None else a + b

    if g[0] is not None:
        e = WEIGHTS[0] * g[0]
        total = e
        dens = e * base
        cross = OMEGA * (g[0] * f[0])
    for i, j in PAIRS:
        if g[i] is None:
            continue
        along = combine(vel(i), u)
        w = WEIGHTS[i]
        even = w * (g[i] + g[j])
        odd = w * (g[i] - g[j])
        total = plus(total, even)
        dens = plus(dens, even * (base + 4.5 * along * along) + 3.0 * along * odd)
        push = 3.0 * odd + 9.0 * along * even
        for d, v in enumerate(vel(i)):
            if v:
                lin[d] = plus(lin[d], push if v > 0 else -push)
        cross = plus(
            cross,
            g[i] * (f[j] - (1.0 - OMEGA) * f[i]) + g[j] * (f[i] - (1.0 - OMEGA) * f[j]),
        )
    lin = [
        (-3.0 * u[d] * total if lin[d] is None else lin[d] - 3.0 * u[d] * total)
        for d in range(3)
    ]
    dsolid = cross - OMEGA * rho * dens
    shared = gain * (dens - (lin[0] * u[0] + lin[1] * u[1] + lin[2] * u[2]))
    lin = [gain * v for v in lin]
    out = [None] * Q
    out[0] = shared if g[0] is None else (keep + solid) * g[0] + shared
    for i, j in PAIRS:
        slope = combine(vel(i), lin)
        if g[i] is None:
            out[i] = shared + slope
            out[j] = shared - slope
        else:
            out[i] = keep * g[i] + solid * g[j] + (shared + slope)
            out[j] = keep * g[j] + solid * g[i] + (shared - slope)
    return out, dsolid


def side_jobs(pack, t, get, ab_ref):
    lane = lane_iota((TL, LANES))

    def a_col(col):
        acc = jnp.zeros((TL, LANES), jnp.float32)
        for side in (-1, 1):
            for key in pack.lists[(1, side)]:
                j = pack.slot(1, side, key)
                if j // 4 != col:
                    continue
                to = TB * (j % 4)
                if side < 0:
                    part = lane_roll(get(key, slice(None), slice(0, LANES)), to)
                else:
                    part = lane_roll(
                        get(key, slice(None), slice(CELLS - LANES, CELLS)),
                        to - (LANES - TB),
                    )
                acc = jnp.where((lane >> 5) == j % 4, part, acc)
        ab_ref[t, pack.a_row + TL * col : pack.a_row + TL * (col + 1), :] = acc

    def b_col(col):
        acc = jnp.zeros((TL, LANES), jnp.float32)
        for half in range(pack.fold):
            src = col + half * pack.b_cols
            for side in (-1, 1):
                for key in pack.lists[(2, side)]:
                    j = pack.slot(2, side, key) + half * (TB // 2)
                    part = get(key, slice(None), slice(LANES * src, LANES * (src + 1)))
                    part = lane_roll(part, j if side < 0 else j - (TB - 1))
                    acc = jnp.where((lane & (TB - 1)) == j, part, acc)
        ab_ref[t, pack.b_row + TL * col : pack.b_row + TL * (col + 1), :] = acc

    return [functools.partial(a_col, c) for c in range(pack.a_cols)] + [
        functools.partial(b_col, c) for c in range(pack.b_cols)
    ]


def end_jobs(pack, t, get, up_ref, dn_ref):
    def l_rows(side, ref, key):
        row = TL - 1 if side > 0 else 0
        j = pack.slot(0, side, key)
        for col in range(COLS):
            ref[t, j * COLS + col : j * COLS + col + 1, :] = get(
                key, slice(row, row + 1), slice(LANES * col, LANES * (col + 1))
            )

    return [
        functools.partial(l_rows, side, ref, key)
        for side, ref in ((1, up_ref), (-1, dn_ref))
        for key in pack.lists[(0, side)]
    ]


def first_sides(post, probe, ab):
    def sides(t):
        def get(key, rows, lanes):
            if key[0] == "probe":
                return probe[t, rows, lanes]
            return post[t, key[1], rows, lanes]

        return side_jobs(PACK1, t, get, ab)

    staged(post.shape[0], [sides])


def second_sides(post1, adj1, ab):
    def sides(t):
        def get(key, rows, lanes):
            return (post1 if key[0] == "post" else adj1)[t, key[1], rows, lanes]

        return side_jobs(PACK2, t, get, ab)

    staged(post1.shape[0], [sides])


def weave(lists):
    jobs = [
        ((n + 0.5) / len(items), k, job)
        for k, items in enumerate(lists)
        for n, job in enumerate(items)
    ]
    for _, _, job in sorted(jobs, key=lambda job: job[:2]):
        job()


def staged(count, stages, after=None):
    for step in range(count + len(stages) - 1):
        live = [(k, step - k) for k in range(len(stages)) if 0 <= step - k < count]
        weave([stages[k](t) for k, t in live])
        if after is not None:
            for k, t in live:
                after(k, t)


def build_inverse(pos_ref, inv_ref, n_layers, group):
    layer = lax.axis_index("gx")
    for off in (-1, 0, 1):
        for w in range(group + 1):
            inv_ref[off + 1, w] = -1
        target = layer + off
        valid = (target >= 0) & (target < n_layers)
        first = jnp.clip(target, 0, n_layers - 1) * group
        for s in range(group):
            p = pos_ref[first + s]
            inv_ref[off + 1, jnp.where(valid & (p >= 0), p, group)] = s


class Neighbours:
    def __init__(self, pack, t, faces_ref, pos_ref, inv_ref, n_cross, count):
        self.pack = pack
        self.ref = faces_ref
        group = n_cross * count
        own = pos_ref[lax.axis_index("gx") * group + lax.axis_index("yz") * count + t]
        p = jnp.maximum(own, 0)
        a, b = p // count, p % count
        self.alive = own >= 0
        self.where = {}
        for d in [vel(i) for i in range(1, Q)]:
            ta, tb = a + d[1], b + d[2]
            ok = (ta >= 0) & (ta < n_cross) & (tb >= 0) & (tb < count)
            s = inv_ref[d[0] + 1, jnp.where(ok, ta * count + tb, group)]
            found = ok & (s >= 0)
            s = jnp.where(found, s, 0)
            owner, slot = s // count, s % count
            half = ((owner ^ lax.axis_index("yz")) >> 1) & 1
            side = owner & 1
            if pack is PACK1:
                side = side ^ (lax.axis_index("yz") & 1)
            block = (side * 2 + half) * count + slot
            self.where[d] = (block, found)
        self.planes = {}

    def a_face(self, d, side, key, fill, to):
        k, found = self.where[d]
        j = self.pack.slot(1, side, key)
        row = self.pack.a_row + TL * (j // 4)
        face = self.ref[k, row : row + TL, :]
        face = lane_roll(face, to - TB * (j % 4))
        return jnp.where(found, face, fill)

    def b_plane(self, d):
        if d not in self.planes:
            k, found = self.where[d]
            row = self.pack.b_row
            half = jnp.concatenate(
                [
                    self.ref[k, row + TL * c : row + TL * (c + 1), :]
                    for c in range(self.pack.b_cols)
                ],
                axis=1,
            )
            if self.pack.fold == 2:
                half = jnp.concatenate([half, lane_roll(half, -(TB // 2))], axis=1)
            self.planes[d] = half
        return self.planes[d], self.where[d][1]

    def l_row(self, d, side, key, fill):
        k, found = self.where[d]
        first = self.pack.up_row if side > 0 else self.pack.dn_row
        first = first + self.pack.slot(0, side, key) * COLS
        row = jnp.concatenate(
            [self.ref[k, first + c : first + c + 1, :] for c in range(COLS)], axis=1
        )
        return jnp.where(found, row, fill)

    def enter(self, x, c, key, fill):
        cl, ca, cb = c
        shape = (TL, CELLS)
        if ca:
            to = 0 if ca > 0 else LANES - TB
            face = row_roll(self.a_face((0, -ca, 0), ca, key, fill, to + cb), cl)
            inner = lane_iota((TL, LANES))
            hit = inner < TB if ca > 0 else inner >= LANES - TB
            part = slice(0, LANES) if ca > 0 else slice(CELLS - LANES, CELLS)
            face = jnp.where(hit, face, x[:, part])
            x = jnp.concatenate(
                [face, x[:, LANES:]] if ca > 0 else [x[:, : CELLS - LANES], face], axis=1
            )
        if cb:
            plane, found = self.b_plane((0, 0, -cb))
            plane = jnp.where(found, plane, fill)
            if ca:
                corner, found = self.b_plane((0, -ca, -cb))
                part = slice(CELLS - LANES, CELLS) if ca > 0 else slice(0, LANES)
                inner = lane_iota((TL, LANES))
                hit = inner >= LANES - TB if ca > 0 else inner < TB
                corner = jnp.where(found, corner[:, part], fill)
                corner = jnp.where(hit, corner, plane[:, part])
                plane = jnp.concatenate(
                    [plane[:, : CELLS - LANES], corner] if ca > 0 else [corner, plane[:, LANES:]],
                    axis=1,
                )
            at = 0 if cb > 0 else TB - 1
            face = lane_roll(plane, TB * ca + at - self.pack.slot(2, cb, key))
            x = jnp.where((lane_iota(shape) & (TB - 1)) == at, row_roll(face, cl), x)
        if cl:
            row = self.l_row((-cl, 0, 0), cl, key, fill)
            lane = lane_iota((1, CELLS))
            if ca:
                corner = self.l_row((-cl, -ca, 0), cl, key, fill)
                row = jnp.where((lane >> 5) == (TA - 1 if ca > 0 else 0), corner, row)
            row = lane_roll(row, TB * ca + cb)
            if cb:
                corner = self.l_row((-cl, 0, -cb), cl, key, fill)
                corner = lane_roll(corner, -cb * (TB - 1))
                row = jnp.where((lane & (TB - 1)) == (0 if cb > 0 else TB - 1), corner, row)
            half = (TL // 2, CELLS)
            low, high = x[: TL // 2], x[TL // 2 :]
            row = jnp.broadcast_to(row, half)
            if cl > 0:
                low = jnp.where(row_iota(half) == 0, row, low)
            else:
                high = jnp.where(row_iota(half) == TL // 2 - 1, row, high)
            x = jnp.concatenate([low, high], axis=0)
        return x


def shifted(x, c):
    return row_roll(lane_roll(x, TB * c[1] + c[2]), c[0])


def against(i):
    return tuple(-v for v in vel(i))


def first_own(post, probe, after, moved, back):
    del after
    for t in range(post.shape[0]):
        for i in range(Q):
            moved[t, i] = shifted(post[t, i], vel(i))
        for n, i in enumerate(AXIAL):
            back[t, n] = shifted(probe[t], against(i))


def second_own(post1, adj1, patch, after, moved, back, onehot):
    del after
    low_iota = lax.broadcasted_iota(jnp.int32, (LANES, CELLS), 0)
    for t in range(post1.shape[0]):
        for i in range(Q):
            moved[t, i] = shifted(post1[t, i], vel(i))
            back[t, i] = shifted(adj1[t, i], against(i))
            if i < TL:
                low = patch[t, i : i + 1, :] & (LANES - 1)
                onehot[t, i] = jnp.where(low_iota == low, 1.0, 0.0).astype(jnp.bfloat16)


def first_kernel(pops_in, mask_in, frac_in, probe_in, post, solid, probe, up, dn, pops, mask, frac, sems):
    count = pops.shape[0]
    small = [
        pltpu.make_async_copy(src, dst, sems.at[n])
        for n, (src, dst) in enumerate(((mask_in, mask), (frac_in, frac), (probe_in, probe)))
    ]
    halves = [(t, r) for t in range(count) for r in range(2)]
    large = [
        pltpu.make_async_copy(
            pops_in.at[t, :, pl.ds(8 * r, 8), :],
            pops.at[t, :, pl.ds(8 * r, 8), :],
            sems.at[len(small) + n],
        )
        for n, (t, r) in enumerate(halves)
    ]
    for copy in small[:2] + large + small[2:]:
        copy.start()
    for copy in small[:2]:
        copy.wait()
    solid[...] = mask[...].astype(jnp.float32) * frac[...]

    def collides(t):
        def run(r, c):
            if c == 0:
                large[halves.index((t, r))].wait()
            rows = slice(8 * r, 8 * r + 8)
            lanes = slice(LANES * c, LANES * (c + 1))
            f = [pops[t, i, rows, lanes] for i in range(Q)]
            out = collide(f, solid[t, rows, lanes], *flow(f))
            for i in range(Q):
                post[t, i, rows, lanes] = out[i]

        return [functools.partial(run, r, c) for r in range(2) for c in range(COLS)]

    def faces(t):
        def get(key, rows, lanes):
            if key[0] == "probe":
                return probe[t, rows, lanes]
            return post[t, key[1], rows, lanes]

        return end_jobs(PACK1, t, get, up, dn)

    small[2].wait()
    staged(count, [collides, faces])


def second_kernel(
    dims, pos, moved, back, solid_in, around, post1, adj1, dsolid, up, dn, state, pulled, inv
):
    n_layers, n_cross = dims
    count = solid_in.shape[0]
    build_inverse(pos, inv, n_layers, n_cross * count)

    def moves(t):
        near = Neighbours(PACK1, t, around, pos, inv, n_cross, count)

        def forward(i):
            state[t, i] = near.enter(moved[t, i], vel(i), ("post", i), WEIGHTS[i])

        def backward(n, i):
            x = near.enter(back[t, n], against(i), ("probe", 0), 0.0)
            pulled[t, n] = x if vel(i)[0] > 0 else -x

        jobs = [(vel(i), functools.partial(forward, i)) for i in range(Q)]
        jobs += [(against(i), functools.partial(backward, n, i)) for n, i in enumerate(AXIAL)]
        return [job for _, job in sorted(jobs, key=lambda item: (item[0][2], item[0][1]))]

    def runs(t):
        def run(r, c):
            rows = slice(8 * r, 8 * r + 8)
            lanes = slice(LANES * c, LANES * (c + 1))
            f = [state[t, i, rows, lanes] for i in range(Q)]
            solid = solid_in[t, rows, lanes]
            rho, u, base = flow(f)
            out = collide(f, solid, rho, u, base)
            for i in range(Q):
                post1[t, i, rows, lanes] = out[i]
            g = [None] * Q
            for n, i in enumerate(AXIAL):
                g[i] = pulled[t, n, rows, lanes]
            df, ds = pullback(f, solid, rho, u, base, g)
            for i in range(Q):
                adj1[t, i, rows, lanes] = df[i]
            dsolid[t, rows, lanes] = ds

        return [functools.partial(run, r, c) for r in range(2) for c in range(COLS)]

    def faces(t):
        def get(key, rows, lanes):
            return (post1 if key[0] == "post" else adj1)[t, key[1], rows, lanes]

        return end_jobs(PACK2, t, get, up, dn)

    staged(count, [moves, runs, faces])


def third_kernel(
    dims, pos, moved, back, onehot, pops, mask, solid_in, patch, dsolid, around, final_out, start_out, sums, final, start, pulled, weighted, inv, sems
):
    n_layers, n_cross = dims
    count = pops.shape[0]
    group = n_cross * count
    build_inverse(pos, inv, n_layers, group)

    base_slot = lax.axis_index("gx") * group + lax.axis_index("yz") * count
    n_high = sums.shape[0]
    high_iota = lax.broadcasted_iota(jnp.int32, (n_high, CELLS), 0)
    total = [jnp.zeros((3 * n_high, LANES), jnp.float32)]

    def moves(t):
        near = Neighbours(PACK2, t, around, pos, inv, n_cross, count)

        def forward(i):
            x = near.enter(moved[t, i], vel(i), ("post", i), WEIGHTS[i])
            final[t, i] = jnp.where(near.alive, x, 0.0)

        def backward(i):
            pulled[t, i] = near.enter(back[t, i], against(i), ("adj", i), 0.0)

        order = [functools.partial(backward, i) for i in range(Q)]
        return order + [functools.partial(forward, i) for i in range(Q)]

    def runs(t):
        alive = pos[base_slot + t] >= 0

        def run(r, c):
            rows = slice(8 * r, 8 * r + 8)
            lanes = slice(LANES * c, LANES * (c + 1))
            f = [pops[t, i, rows, lanes] for i in range(Q)]
            g = [pulled[t, i, rows, lanes] for i in range(Q)]
            wall = mask[t, rows, lanes].astype(jnp.float32)
            solid = solid_in[t, rows, lanes]
            rho, u, base = flow(f)
            df, ds = pullback(f, solid, rho, u, base, g)
            for i in range(Q):
                start[t, i, rows, lanes] = jnp.where(alive, df[i], 0.0)
            part = wall * (ds + dsolid[t, rows, lanes])
            weighted[t, rows, lanes] = jnp.where(alive, part, 0.0)

        return [functools.partial(run, r, c) for r in range(2) for c in range(COLS)]

    def add(t, r):
        ids = patch[t, r : r + 1, :]
        w = weighted[t, r : r + 1, :]
        w1 = w.astype(jnp.bfloat16).astype(jnp.float32)
        w2 = (w - w1).astype(jnp.bfloat16).astype(jnp.float32)
        w3 = w - w1 - w2
        high = high_iota == (ids >> 7)
        left = jnp.concatenate(
            [jnp.where(high, part, 0.0).astype(jnp.bfloat16) for part in (w1, w2, w3)],
            axis=0,
        )
        total[0] = total[0] + lax.dot_general(
            left, onehot[t, r], (((1,), (1,)), ((), ())), preferred_element_type=jnp.float32
        )

    def adds(t):
        return [functools.partial(add, t, r) for r in range(TL)]

    copies = []

    def send(k, t):
        if k < 2:
            src, dst = ((final, final_out), (start, start_out))[k]
            copies.append(pltpu.make_async_copy(src.at[t], dst.at[t], sems.at[len(copies)]))
            copies[-1].start()

    staged(count, [moves, runs, adds], send)
    for copy in copies:
        copy.wait()
    acc = total[0]
    sums[...] = acc[:n_high] + acc[n_high : 2 * n_high] + acc[2 * n_high :]


def call(kernel, outs, scratch, args, in_smem=(), in_hbm=(), in_any=(), out_hbm=(), types={}):
    vmem = pl.BlockSpec(memory_space=pltpu.VMEM)
    hbm = pl.BlockSpec(memory_space=pltpu.HBM)
    free = pl.BlockSpec(memory_space=pl.ANY)
    smem = pl.BlockSpec(memory_space=pltpu.SMEM)
    return pl.pallas_call(
        kernel,
        out_shape=[
            jax.ShapeDtypeStruct(s, types.get(n, jnp.float32)) for n, s in enumerate(outs)
        ],
        in_specs=[
            smem if n in in_smem else hbm if n in in_hbm else free if n in in_any else vmem
            for n in range(len(args))
        ],
        out_specs=[hbm if n in out_hbm else vmem for n in range(len(outs))],
        scratch_shapes=scratch,
        compiler_params=pltpu.CompilerParams(vmem_limit_bytes=40 << 20),
    )(*args)


def exchange(ab, up, dn, first):
    n = lax.axis_size("gx")
    m = lax.axis_size("yz")
    assert m == 4
    hop = []
    for q in range(m):
        for g in range(n):
            to = g + 1 if q >= 2 else g - 1
            hop.append((g * m + q, to * m + q if 0 <= to < n else g * m + (q ^ 2)))
    rising = lax.axis_index("yz") >= 2
    one = lax.ppermute(jnp.where(rising, up, dn), ("gx", "yz"), hop)
    two = lax.ppermute(jnp.where(rising, dn, up), ("gx", "yz"), [(j, i) for i, j in hop])
    across = [(q, q ^ 2) for q in range(m)]
    ab_far = lax.ppermute(ab, "yz", across)
    one_far = lax.ppermute(one, "yz", across)
    two_far = lax.ppermute(two, "yz", across)
    l_near = jnp.concatenate(
        [jnp.where(rising, one, two), jnp.where(rising, two, one)], axis=1
    )
    l_far = jnp.concatenate(
        [jnp.where(rising, two_far, one_far), jnp.where(rising, one_far, two_far)], axis=1
    )
    both = jnp.concatenate(
        [jnp.concatenate([ab, l_near], axis=1), jnp.concatenate([ab_far, l_far], axis=1)],
        axis=0,
    )
    if first:
        other = lax.ppermute(both, "yz", [(q, q ^ 1) for q in range(m)])
        return two, jnp.concatenate([both, other], axis=0)
    pairs = [[0, 1], [2, 3]]
    return two, lax.all_gather(both, "yz", axis=0, tiled=True, axis_index_groups=pairs)


def body(pops_start, tile_pos, wall_mask, wall_frac, patch_id, probe):
    count = pops_start.shape[0]
    n_layers = lax.axis_size("gx")
    n_cross = lax.axis_size("yz")
    parts = n_layers * n_cross
    dims = (n_layers, n_cross)
    field = pops_start.shape
    plane = wall_frac.shape
    patch_dev = 64
    n_high = patch_dev * parts // LANES
    inverse = pltpu.SMEM((3, n_cross * count + 1), jnp.int32)

    def ends(pack):
        return [(count, pack.l_rows, LANES)] * 2

    def sides(pack):
        return [(count, pack.ab_rows, LANES)]

    post0, solid, probe_kept, up, dn = call(
        first_kernel,
        [field, plane, plane] + ends(PACK1),
        [
            pltpu.VMEM(field, jnp.float32),
            pltpu.VMEM(plane, jnp.int32),
            pltpu.VMEM(plane, jnp.float32),
            pltpu.SemaphoreType.DMA((3 + 2 * count,)),
        ],
        tuple(
            pltpu.with_memory_space_constraint(x, pltpu.HBM)
            for x in (pops_start, wall_mask, wall_frac, probe)
        ),
        in_hbm=range(4),
    )
    (ab,) = call(first_sides, sides(PACK1), [], (post0, probe_kept))
    token, around = exchange(ab, up, dn, True)
    axial = (count, len(AXIAL)) + plane[1:]
    moved, back = call(first_own, [field, axial], [], (post0, probe_kept, token), in_any=(2,))
    post1, adj1, dsolid, up, dn = call(
        functools.partial(second_kernel, dims),
        [field, field, plane] + ends(PACK2),
        [
            pltpu.VMEM(field, jnp.float32),
            pltpu.VMEM((count, len(AXIAL)) + plane[1:], jnp.float32),
            inverse,
        ],
        (tile_pos, moved, back, solid, around),
        in_smem=(0,),
    )
    (ab,) = call(second_sides, sides(PACK2), [], (post1, adj1))
    token, around = exchange(ab, up, dn, False)
    moved, back, onehot = call(
        second_own,
        [field, field, (count, TL, LANES, CELLS)],
        [],
        (post1, adj1, patch_id, token),
        in_any=(3,),
        types={2: jnp.bfloat16},
    )
    pops_final, adjoint_start, sums = call(
        functools.partial(third_kernel, dims),
        [field, field, (n_high, LANES)],
        [
            pltpu.VMEM(field, jnp.float32),
            pltpu.VMEM(field, jnp.float32),
            pltpu.VMEM(field, jnp.float32),
            pltpu.VMEM(plane, jnp.float32),
            inverse,
            pltpu.SemaphoreType.DMA((2 * count,)),
        ],
        (tile_pos, moved, back, onehot, pops_start, wall_mask, solid, patch_id, dsolid, around),
        in_smem=(0,),
        out_hbm=(0, 1),
    )
    shares = lax.all_to_all(
        sums.reshape(parts, patch_dev), ("gx", "yz"), 0, 0, tiled=True
    )
    return (pops_final, adjoint_start, jnp.sum(shares, axis=0))


def solution(mesh):
    in_specs = (
        P(("gx", "yz"), None, None, None),
        P(),
        P(("gx", "yz"), None, None),
        P(("gx", "yz"), None, None),
        P(("gx", "yz"), None, None),
        P(("gx", "yz"), None, None),
    )
    out_specs = (
        P(("gx", "yz"), None, None, None),
        P(("gx", "yz"), None, None, None),
        P(("gx", "yz")),
    )
    return jax.shard_map(body, mesh=mesh, in_specs=in_specs, out_specs=out_specs, check_vma=False)
```

```python
import functools

import jax
import jax.numpy as jnp
import numpy as np
from jax import lax
from jax.experimental import pallas as pl
from jax.experimental.pallas import tpu as pltpu
from jax.sharding import PartitionSpec as P

TL = 16
TA = 16
TB = 32
CELLS = TA * TB
LANES = 128
COLS = CELLS // LANES
OMEGA = 1.25

VELOCITY = np.array(
    [
        [0, 0, 0],
        [1, 0, 0],
        [-1, 0, 0],
        [0, 1, 0],
        [0, -1, 0],
        [0, 0, 1],
        [0, 0, -1],
        [1, 1, 0],
        [-1, -1, 0],
        [1, -1, 0],
        [-1, 1, 0],
        [1, 0, 1],
        [-1, 0, -1],
        [1, 0, -1],
        [-1, 0, 1],
        [0, 1, 1],
        [0, -1, -1],
        [0, 1, -1],
        [0, -1, 1],
    ]
)
Q = 19
WEIGHTS = [1.0 / 3.0] + [1.0 / 18.0] * 6 + [1.0 / 36.0] * 12
PAIRS = [(2 * k + 1, 2 * k + 2) for k in range(9)]
AXIAL = [i for i in range(Q) if VELOCITY[i, 0] != 0]


def vel(i):
    return tuple(int(v) for v in VELOCITY[i])


def members_of(dim, value):
    return [i for i in range(Q) if vel(i)[dim] == value]


def face_list(stage, dim, side):
    if stage == 1:
        return [("post", i) for i in members_of(dim, side)] + [("probe", 0)]
    return [("post", i) for i in members_of(dim, side)] + [
        ("adj", i) for i in members_of(dim, -side)
    ]


class Pack:
    def __init__(self, stage):
        self.n = len(face_list(stage, 0, 1))
        self.lists = {
            (d, s): face_list(stage, d, s) for d in range(3) for s in (-1, 1)
        }
        self.fold = 2 if 2 * self.n <= TB // 2 else 1
        self.a_cols = -(-2 * self.n * TB // LANES)
        self.b_cols = COLS // self.fold
        self.a_row = 0
        self.b_row = TL * self.a_cols
        self.ab_rows = self.b_row + TL * self.b_cols
        self.l_rows = self.n * COLS
        self.up_row = self.ab_rows
        self.dn_row = self.up_row + self.l_rows
        self.rows = self.dn_row + self.l_rows

    def slot(self, dim, side, key):
        j = self.lists[(dim, side)].index(key)
        return j if dim == 0 or side < 0 else j + self.n


PACK1 = Pack(1)
PACK2 = Pack(2)


def lane_roll(x, shift):
    shift = shift % x.shape[-1]
    return x if shift == 0 else pltpu.roll(x, shift, axis=x.ndim - 1)


def row_roll(x, shift):
    shift = shift % x.shape[0]
    return x if shift == 0 else pltpu.roll(x, shift, axis=0)


def lane_iota(shape):
    return lax.broadcasted_iota(jnp.int32, shape, len(shape) - 1)


def row_iota(shape):
    return lax.broadcasted_iota(jnp.int32, shape, 0)


def combine(c, parts):
    total = None
    for v, p in zip(c, parts):
        if v == 0:
            continue
        if total is None:
            total = p if v > 0 else -p
        else:
            total = total + p if v > 0 else total - p
    return total


def flow(f):
    rho = f[0]
    momentum = [None, None, None]
    for i, j in PAIRS:
        rho = rho + (f[i] + f[j])
        diff = f[i] - f[j]
        for d, v in enumerate(vel(i)):
            if v == 0:
                continue
            if momentum[d] is None:
                momentum[d] = diff if v > 0 else -diff
            else:
                momentum[d] = momentum[d] + diff if v > 0 else momentum[d] - diff
    inv = 1.0 / rho
    u = [m * inv for m in momentum]
    square = u[0] * u[0] + u[1] * u[1] + u[2] * u[2]
    return rho, u, 1.0 - 1.5 * square


def collide(f, solid, rho, u, base):
    fluid = 1.0 - solid
    keep = (1.0 - OMEGA) * fluid
    scale = OMEGA * fluid * rho
    out = [None] * Q
    out[0] = (keep + solid) * f[0] + WEIGHTS[0] * scale * base
    for i, j in PAIRS:
        along = combine(vel(i), u)
        ws = WEIGHTS[i] * scale
        even = ws * (base + 4.5 * along * along)
        odd = ws * (3.0 * along)
        out[i] = keep * f[i] + solid * f[j] + (even + odd)
        out[j] = keep * f[j] + solid * f[i] + (even - odd)
    return out


def pullback(f, solid, rho, u, base, g):
    fluid = 1.0 - solid
    keep = (1.0 - OMEGA) * fluid
    gain = OMEGA * fluid
    lin = [None, None, None]
    total = None
    dens = None
    cross = None

    def plus(a, b):
        return b if a is None else a + b

    if g[0] is not None:
        e = WEIGHTS[0] * g[0]
        total = e
        dens = e * base
        cross = OMEGA * (g[0] * f[0])
    for i, j in PAIRS:
        if g[i] is None:
            continue
        along = combine(vel(i), u)
        w = WEIGHTS[i]
        even = w * (g[i] + g[j])
        odd = w * (g[i] - g[j])
        total = plus(total, even)
        dens = plus(dens, even * (base + 4.5 * along * along) + 3.0 * along * odd)
        push = 3.0 * odd + 9.0 * along * even
        for d, v in enumerate(vel(i)):
            if v:
                lin[d] = plus(lin[d], push if v > 0 else -push)
        cross = plus(
            cross,
            g[i] * (f[j] - (1.0 - OMEGA) * f[i]) + g[j] * (f[i] - (1.0 - OMEGA) * f[j]),
        )
    lin = [
        (-3.0 * u[d] * total if lin[d] is None else lin[d] - 3.0 * u[d] * total)
        for d in range(3)
    ]
    dsolid = cross - OMEGA * rho * dens
    shared = gain * (dens - (lin[0] * u[0] + lin[1] * u[1] + lin[2] * u[2]))
    lin = [gain * v for v in lin]
    out = [None] * Q
    out[0] = shared if g[0] is None else (keep + solid) * g[0] + shared
    for i, j in PAIRS:
        slope = combine(vel(i), lin)
        if g[i] is None:
            out[i] = shared + slope
            out[j] = shared - slope
        else:
            out[i] = keep * g[i] + solid * g[j] + (shared + slope)
            out[j] = keep * g[j] + solid * g[i] + (shared - slope)
    return out, dsolid


def side_jobs(pack, t, get, ab_ref):
    lane = lane_iota((TL, LANES))

    def a_col(col):
        acc = jnp.zeros((TL, LANES), jnp.float32)
        for side in (-1, 1):
            for key in pack.lists[(1, side)]:
                j = pack.slot(1, side, key)
                if j // 4 != col:
                    continue
                to = TB * (j % 4)
                if side < 0:
                    part = lane_roll(get(key, slice(None), slice(0, LANES)), to)
                else:
                    part = lane_roll(
                        get(key, slice(None), slice(CELLS - LANES, CELLS)),
                        to - (LANES - TB),
                    )
                acc = jnp.where((lane >> 5) == j % 4, part, acc)
        ab_ref[t, pack.a_row + TL * col : pack.a_row + TL * (col + 1), :] = acc

    def b_col(col):
        acc = jnp.zeros((TL, LANES), jnp.float32)
        for half in range(pack.fold):
            src = col + half * pack.b_cols
            for side in (-1, 1):
                for key in pack.lists[(2, side)]:
                    j = pack.slot(2, side, key) + half * (TB // 2)
                    part = get(key, slice(None), slice(LANES * src, LANES * (src + 1)))
                    part = lane_roll(part, j if side < 0 else j - (TB - 1))
                    acc = jnp.where((lane & (TB - 1)) == j, part, acc)
        ab_ref[t, pack.b_row + TL * col : pack.b_row + TL * (col + 1), :] = acc

    return [functools.partial(a_col, c) for c in range(pack.a_cols)] + [
        functools.partial(b_col, c) for c in range(pack.b_cols)
    ]


def end_jobs(pack, t, get, up_ref, dn_ref):
    def l_rows(side, ref, key):
        row = TL - 1 if side > 0 else 0
        j = pack.slot(0, side, key)
        for col in range(COLS):
            ref[t, j * COLS + col : j * COLS + col + 1, :] = get(
                key, slice(row, row + 1), slice(LANES * col, LANES * (col + 1))
            )

    return [
        functools.partial(l_rows, side, ref, key)
        for side, ref in ((1, up_ref), (-1, dn_ref))
        for key in pack.lists[(0, side)]
    ]


def first_sides(post, probe, ab):
    def sides(t):
        def get(key, rows, lanes):
            if key[0] == "probe":
                return probe[t, rows, lanes]
            return post[t, key[1], rows, lanes]

        return side_jobs(PACK1, t, get, ab)

    staged(post.shape[0], [sides])


def second_sides(post1, adj1, ab):
    def sides(t):
        def get(key, rows, lanes):
            return (post1 if key[0] == "post" else adj1)[t, key[1], rows, lanes]

        return side_jobs(PACK2, t, get, ab)

    staged(post1.shape[0], [sides])


def weave(lists):
    jobs = [
        ((n + 0.5) / len(items), k, job)
        for k, items in enumerate(lists)
        for n, job in enumerate(items)
    ]
    for _, _, job in sorted(jobs, key=lambda job: job[:2]):
        job()


def staged(count, stages, after=None):
    for step in range(count + len(stages) - 1):
        live = [(k, step - k) for k in range(len(stages)) if 0 <= step - k < count]
        weave([stages[k](t) for k, t in live])
        if after is not None:
            for k, t in live:
                after(k, t)


def build_inverse(pos_ref, inv_ref, n_layers, group):
    layer = lax.axis_index("gx")
    for off in (-1, 0, 1):
        for w in range(group + 1):
            inv_ref[off + 1, w] = -1
        target = layer + off
        valid = (target >= 0) & (target < n_layers)
        first = jnp.clip(target, 0, n_layers - 1) * group
        for s in range(group):
            p = pos_ref[first + s]
            inv_ref[off + 1, jnp.where(valid & (p >= 0), p, group)] = s


class Neighbours:
    def __init__(self, pack, t, faces_ref, pos_ref, inv_ref, n_cross, count):
        self.pack = pack
        self.ref = faces_ref
        group = n_cross * count
        own = pos_ref[lax.axis_index("gx") * group + lax.axis_index("yz") * count + t]
        p = jnp.maximum(own, 0)
        a, b = p // count, p % count
        self.alive = own >= 0
        self.where = {}
        for d in [vel(i) for i in range(1, Q)]:
            ta, tb = a + d[1], b + d[2]
            ok = (ta >= 0) & (ta < n_cross) & (tb >= 0) & (tb < count)
            s = inv_ref[d[0] + 1, jnp.where(ok, ta * count + tb, group)]
            found = ok & (s >= 0)
            s = jnp.where(found, s, 0)
            owner, slot = s // count, s % count
            half = ((owner ^ lax.axis_index("yz")) >> 1) & 1
            side = owner & 1
            if pack is PACK1:
                side = side ^ (lax.axis_index("yz") & 1)
            block = (side * 2 + half) * count + slot
            self.where[d] = (block, found)
        self.planes = {}

    def a_face(self, d, side, key, fill, to):
        k, found = self.where[d]
        j = self.pack.slot(1, side, key)
        row = self.pack.a_row + TL * (j // 4)
        face = self.ref[k, row : row + TL, :]
        face = lane_roll(face, to - TB * (j % 4))
        return jnp.where(found, face, fill)

    def b_plane(self, d):
        if d not in self.planes:
            k, found = self.where[d]
            row = self.pack.b_row
            half = jnp.concatenate(
                [
                    self.ref[k, row + TL * c : row + TL * (c + 1), :]
                    for c in range(self.pack.b_cols)
                ],
                axis=1,
            )
            if self.pack.fold == 2:
                half = jnp.concatenate([half, lane_roll(half, -(TB // 2))], axis=1)
            self.planes[d] = half
        return self.planes[d], self.where[d][1]

    def l_row(self, d, side, key, fill):
        k, found = self.where[d]
        first = self.pack.up_row if side > 0 else self.pack.dn_row
        first = first + self.pack.slot(0, side, key) * COLS
        row = jnp.concatenate(
            [self.ref[k, first + c : first + c + 1, :] for c in range(COLS)], axis=1
        )
        return jnp.where(found, row, fill)

    def enter(self, x, c, key, fill):
        cl, ca, cb = c
        shape = (TL, CELLS)
        if ca:
            to = 0 if ca > 0 else LANES - TB
            face = row_roll(self.a_face((0, -ca, 0), ca, key, fill, to + cb), cl)
            inner = lane_iota((TL, LANES))
            hit = inner < TB if ca > 0 else inner >= LANES - TB
            part = slice(0, LANES) if ca > 0 else slice(CELLS - LANES, CELLS)
            face = jnp.where(hit, face, x[:, part])
            x = jnp.concatenate(
                [face, x[:, LANES:]] if ca > 0 else [x[:, : CELLS - LANES], face], axis=1
            )
        if cb:
            plane, found = self.b_plane((0, 0, -cb))
            plane = jnp.where(found, plane, fill)
            if ca:
                corner, found = self.b_plane((0, -ca, -cb))
                part = slice(CELLS - LANES, CELLS) if ca > 0 else slice(0, LANES)
                inner = lane_iota((TL, LANES))
                hit = inner >= LANES - TB if ca > 0 else inner < TB
                corner = jnp.where(found, corner[:, part], fill)
                corner = jnp.where(hit, corner, plane[:, part])
                plane = jnp.concatenate(
                    [plane[:, : CELLS - LANES], corner] if ca > 0 else [corner, plane[:, LANES:]],
                    axis=1,
                )
            at = 0 if cb > 0 else TB - 1
            face = lane_roll(plane, TB * ca + at - self.pack.slot(2, cb, key))
            x = jnp.where((lane_iota(shape) & (TB - 1)) == at, row_roll(face, cl), x)
        if cl:
            row = self.l_row((-cl, 0, 0), cl, key, fill)
            lane = lane_iota((1, CELLS))
            if ca:
                corner = self.l_row((-cl, -ca, 0), cl, key, fill)
                row = jnp.where((lane >> 5) == (TA - 1 if ca > 0 else 0), corner, row)
            row = lane_roll(row, TB * ca + cb)
            if cb:
                corner = self.l_row((-cl, 0, -cb), cl, key, fill)
                corner = lane_roll(corner, -cb * (TB - 1))
                row = jnp.where((lane & (TB - 1)) == (0 if cb > 0 else TB - 1), corner, row)
            half = (TL // 2, CELLS)
            low, high = x[: TL // 2], x[TL // 2 :]
            row = jnp.broadcast_to(row, half)
            if cl > 0:
                low = jnp.where(row_iota(half) == 0, row, low)
            else:
                high = jnp.where(row_iota(half) == TL // 2 - 1, row, high)
            x = jnp.concatenate([low, high], axis=0)
        return x


def shifted(x, c):
    return row_roll(lane_roll(x, TB * c[1] + c[2]), c[0])


def against(i):
    return tuple(-v for v in vel(i))


def first_own(post, probe, after, moved, back):
    del after
    for t in range(post.shape[0]):
        for i in range(Q):
            moved[t, i] = shifted(post[t, i], vel(i))
        for n, i in enumerate(AXIAL):
            back[t, n] = shifted(probe[t], against(i))


def second_own(post1, adj1, patch, after, moved, back, onehot):
    del after
    low_iota = lax.broadcasted_iota(jnp.int32, (LANES, CELLS), 0)
    for t in range(post1.shape[0]):
        for i in range(Q):
            moved[t, i] = shifted(post1[t, i], vel(i))
            back[t, i] = shifted(adj1[t, i], against(i))
            if i < TL:
                low = patch[t, i : i + 1, :] & (LANES - 1)
                onehot[t, i] = jnp.where(low_iota == low, 1.0, 0.0).astype(jnp.bfloat16)


def first_kernel(pops_in, mask_in, frac_in, probe_in, post, solid, probe, up, dn, pops, mask, frac, sems):
    count = pops.shape[0]
    small = [
        pltpu.make_async_copy(src, dst, sems.at[n])
        for n, (src, dst) in enumerate(((mask_in, mask), (frac_in, frac), (probe_in, probe)))
    ]
    large = [
        pltpu.make_async_copy(pops_in.at[t], pops.at[t], sems.at[len(small) + t])
        for t in range(count)
    ]
    for copy in small[:2] + large + small[2:]:
        copy.start()
    for copy in small[:2]:
        copy.wait()
    solid[...] = mask[...].astype(jnp.float32) * frac[...]

    def collides(t):
        def run(r, c):
            if r == 0 and c == 0:
                large[t].wait()
            rows = slice(8 * r, 8 * r + 8)
            lanes = slice(LANES * c, LANES * (c + 1))
            f = [pops[t, i, rows, lanes] for i in range(Q)]
            out = collide(f, solid[t, rows, lanes], *flow(f))
            for i in range(Q):
                post[t, i, rows, lanes] = out[i]

        return [functools.partial(run, r, c) for r in range(2) for c in range(COLS)]

    def faces(t):
        def get(key, rows, lanes):
            if key[0] == "probe":
                return probe[t, rows, lanes]
            return post[t, key[1], rows, lanes]

        return end_jobs(PACK1, t, get, up, dn)

    small[2].wait()
    staged(count, [collides, faces])


def second_kernel(
    dims, pos, moved, back, solid_in, around, post1, adj1, dsolid, up, dn, state, pulled, inv
):
    n_layers, n_cross = dims
    count = solid_in.shape[0]
    build_inverse(pos, inv, n_layers, n_cross * count)

    def moves(t):
        near = Neighbours(PACK1, t, around, pos, inv, n_cross, count)

        def forward(i):
            state[t, i] = near.enter(moved[t, i], vel(i), ("post", i), WEIGHTS[i])

        def backward(n, i):
            x = near.enter(back[t, n], against(i), ("probe", 0), 0.0)
            pulled[t, n] = x if vel(i)[0] > 0 else -x

        jobs = [(vel(i), functools.partial(forward, i)) for i in range(Q)]
        jobs += [(against(i), functools.partial(backward, n, i)) for n, i in enumerate(AXIAL)]
        return [job for _, job in sorted(jobs, key=lambda item: (item[0][2], item[0][1]))]

    def runs(t):
        def run(r, c):
            rows = slice(8 * r, 8 * r + 8)
            lanes = slice(LANES * c, LANES * (c + 1))
            f = [state[t, i, rows, lanes] for i in range(Q)]
            solid = solid_in[t, rows, lanes]
            rho, u, base = flow(f)
            out = collide(f, solid, rho, u, base)
            for i in range(Q):
                post1[t, i, rows, lanes] = out[i]
            g = [None] * Q
            for n, i in enumerate(AXIAL):
                g[i] = pulled[t, n, rows, lanes]
            df, ds = pullback(f, solid, rho, u, base, g)
            for i in range(Q):
                adj1[t, i, rows, lanes] = df[i]
            dsolid[t, rows, lanes] = ds

        return [functools.partial(run, r, c) for r in range(2) for c in range(COLS)]

    def faces(t):
        def get(key, rows, lanes):
            return (post1 if key[0] == "post" else adj1)[t, key[1], rows, lanes]

        return end_jobs(PACK2, t, get, up, dn)

    staged(count, [moves, runs, faces])


def third_kernel(
    dims, pos, moved, back, onehot, pops, mask, solid_in, patch, dsolid, around, final_out, start_out, sums, final, start, pulled, weighted, inv, sems
):
    n_layers, n_cross = dims
    count = pops.shape[0]
    group = n_cross * count
    build_inverse(pos, inv, n_layers, group)

    base_slot = lax.axis_index("gx") * group + lax.axis_index("yz") * count
    n_high = sums.shape[0]
    high_iota = lax.broadcasted_iota(jnp.int32, (n_high, CELLS), 0)
    total = [jnp.zeros((3 * n_high, LANES), jnp.float32)]

    def moves(t):
        near = Neighbours(PACK2, t, around, pos, inv, n_cross, count)

        def forward(i):
            x = near.enter(moved[t, i], vel(i), ("post", i), WEIGHTS[i])
            final[t, i] = jnp.where(near.alive, x, 0.0)

        def backward(i):
            pulled[t, i] = near.enter(back[t, i], against(i), ("adj", i), 0.0)

        order = [functools.partial(backward, i) for i in range(Q)]
        return order + [functools.partial(forward, i) for i in range(Q)]

    def runs(t):
        alive = pos[base_slot + t] >= 0

        def run(r, c):
            rows = slice(8 * r, 8 * r + 8)
            lanes = slice(LANES * c, LANES * (c + 1))
            f = [pops[t, i, rows, lanes] for i in range(Q)]
            g = [pulled[t, i, rows, lanes] for i in range(Q)]
            wall = mask[t, rows, lanes].astype(jnp.float32)
            solid = solid_in[t, rows, lanes]
            rho, u, base = flow(f)
            df, ds = pullback(f, solid, rho, u, base, g)
            for i in range(Q):
                start[t, i, rows, lanes] = jnp.where(alive, df[i], 0.0)
            part = wall * (ds + dsolid[t, rows, lanes])
            weighted[t, rows, lanes] = jnp.where(alive, part, 0.0)

        return [functools.partial(run, r, c) for r in range(2) for c in range(COLS)]

    def add(t, r):
        ids = patch[t, r : r + 1, :]
        w = weighted[t, r : r + 1, :]
        w1 = w.astype(jnp.bfloat16).astype(jnp.float32)
        w2 = (w - w1).astype(jnp.bfloat16).astype(jnp.float32)
        w3 = w - w1 - w2
        high = high_iota == (ids >> 7)
        left = jnp.concatenate(
            [jnp.where(high, part, 0.0).astype(jnp.bfloat16) for part in (w1, w2, w3)],
            axis=0,
        )
        total[0] = total[0] + lax.dot_general(
            left, onehot[t, r], (((1,), (1,)), ((), ())), preferred_element_type=jnp.float32
        )

    def adds(t):
        return [functools.partial(add, t, r) for r in range(TL)]

    copies = []

    def send(k, t):
        if k < 2:
            src, dst = ((final, final_out), (start, start_out))[k]
            copies.append(pltpu.make_async_copy(src.at[t], dst.at[t], sems.at[len(copies)]))
            copies[-1].start()

    staged(count, [moves, runs, adds], send)
    for copy in copies:
        copy.wait()
    acc = total[0]
    sums[...] = acc[:n_high] + acc[n_high : 2 * n_high] + acc[2 * n_high :]


def call(kernel, outs, scratch, args, in_smem=(), in_hbm=(), in_any=(), out_hbm=(), types={}):
    vmem = pl.BlockSpec(memory_space=pltpu.VMEM)
    hbm = pl.BlockSpec(memory_space=pltpu.HBM)
    free = pl.BlockSpec(memory_space=pl.ANY)
    smem = pl.BlockSpec(memory_space=pltpu.SMEM)
    return pl.pallas_call(
        kernel,
        out_shape=[
            jax.ShapeDtypeStruct(s, types.get(n, jnp.float32)) for n, s in enumerate(outs)
        ],
        in_specs=[
            smem if n in in_smem else hbm if n in in_hbm else free if n in in_any else vmem
            for n in range(len(args))
        ],
        out_specs=[hbm if n in out_hbm else vmem for n in range(len(outs))],
        scratch_shapes=scratch,
        compiler_params=pltpu.CompilerParams(vmem_limit_bytes=40 << 20),
    )(*args)


def exchange(ab, up, dn, first):
    n = lax.axis_size("gx")
    m = lax.axis_size("yz")
    assert m == 4
    hop = []
    for q in range(m):
        for g in range(n):
            to = g + 1 if q >= 2 else g - 1
            hop.append((g * m + q, to * m + q if 0 <= to < n else g * m + (q ^ 2)))
    rising = lax.axis_index("yz") >= 2
    one = lax.ppermute(jnp.where(rising, up, dn), ("gx", "yz"), hop)
    two = lax.ppermute(jnp.where(rising, dn, up), ("gx", "yz"), [(j, i) for i, j in hop])
    across = [(q, q ^ 2) for q in range(m)]
    ab_far = lax.ppermute(ab, "yz", across)
    one_far = lax.ppermute(one, "yz", across)
    two_far = lax.ppermute(two, "yz", across)
    l_near = jnp.concatenate(
        [jnp.where(rising, one, two), jnp.where(rising, two, one)], axis=1
    )
    l_far = jnp.concatenate(
        [jnp.where(rising, two_far, one_far), jnp.where(rising, one_far, two_far)], axis=1
    )
    both = jnp.concatenate(
        [jnp.concatenate([ab, l_near], axis=1), jnp.concatenate([ab_far, l_far], axis=1)],
        axis=0,
    )
    if first:
        other = lax.ppermute(both, "yz", [(q, q ^ 1) for q in range(m)])
        return two, jnp.concatenate([both, other], axis=0)
    pairs = [[0, 1], [2, 3]]
    return two, lax.all_gather(both, "yz", axis=0, tiled=True, axis_index_groups=pairs)


def body(pops_start, tile_pos, wall_mask, wall_frac, patch_id, probe):
    count = pops_start.shape[0]
    n_layers = lax.axis_size("gx")
    n_cross = lax.axis_size("yz")
    parts = n_layers * n_cross
    dims = (n_layers, n_cross)
    field = pops_start.shape
    plane = wall_frac.shape
    patch_dev = 64
    n_high = patch_dev * parts // LANES
    inverse = pltpu.SMEM((3, n_cross * count + 1), jnp.int32)

    def ends(pack):
        return [(count, pack.l_rows, LANES)] * 2

    def sides(pack):
        return [(count, pack.ab_rows, LANES)]

    post0, solid, probe_kept, up, dn = call(
        first_kernel,
        [field, plane, plane] + ends(PACK1),
        [
            pltpu.VMEM(field, jnp.float32),
            pltpu.VMEM(plane, jnp.int32),
            pltpu.VMEM(plane, jnp.float32),
            pltpu.SemaphoreType.DMA((3 + count,)),
        ],
        tuple(
            pltpu.with_memory_space_constraint(x, pltpu.HBM)
            for x in (pops_start, wall_mask, wall_frac, probe)
        ),
        in_hbm=range(4),
    )
    (ab,) = call(first_sides, sides(PACK1), [], (post0, probe_kept))
    token, around = exchange(ab, up, dn, True)
    axial = (count, len(AXIAL)) + plane[1:]
    moved, back = call(first_own, [field, axial], [], (post0, probe_kept, token), in_any=(2,))
    post1, adj1, dsolid, up, dn = call(
        functools.partial(second_kernel, dims),
        [field, field, plane] + ends(PACK2),
        [
            pltpu.VMEM(field, jnp.float32),
            pltpu.VMEM((count, len(AXIAL)) + plane[1:], jnp.float32),
            inverse,
        ],
        (tile_pos, moved, back, solid, around),
        in_smem=(0,),
    )
    (ab,) = call(second_sides, sides(PACK2), [], (post1, adj1))
    token, around = exchange(ab, up, dn, False)
    moved, back, onehot = call(
        second_own,
        [field, field, (count, TL, LANES, CELLS)],
        [],
        (post1, adj1, patch_id, token),
        in_any=(3,),
        types={2: jnp.bfloat16},
    )
    pops_final, adjoint_start, sums = call(
        functools.partial(third_kernel, dims),
        [field, field, (n_high, LANES)],
        [
            pltpu.VMEM(field, jnp.float32),
            pltpu.VMEM(field, jnp.float32),
            pltpu.VMEM(field, jnp.float32),
            pltpu.VMEM(plane, jnp.float32),
            inverse,
            pltpu.SemaphoreType.DMA((2 * count,)),
        ],
        (tile_pos, moved, back, onehot, pops_start, wall_mask, solid, patch_id, dsolid, around),
        in_smem=(0,),
        out_hbm=(0, 1),
    )
    shares = lax.all_to_all(
        sums.reshape(parts, patch_dev), ("gx", "yz"), 0, 0, tiled=True
    )
    return (pops_final, adjoint_start, jnp.sum(shares, axis=0))


def solution(mesh):
    in_specs = (
        P(("gx", "yz"), None, None, None),
        P(),
        P(("gx", "yz"), None, None),
        P(("gx", "yz"), None, None),
        P(("gx", "yz"), None, None),
        P(("gx", "yz"), None, None),
    )
    out_specs = (
        P(("gx", "yz"), None, None, None),
        P(("gx", "yz"), None, None, None),
        P(("gx", "yz")),
    )
    return jax.shard_map(body, mesh=mesh, in_specs=in_specs, out_specs=out_specs, check_vma=False)
```
